32 devices in a mesh: seq: 4 (over y, core), fsdp: 8 (over z, x).
Axes of the slice: x: 2, y: 2, z: 4, core: 2. Of those that a mesh axis runs over, the one named last changes fastest.
Arguments:
- activations: bfloat16 [24, 1024, 768], P('fsdp', 'seq'), may hold values from -6 to 6
- cotangent: bfloat16 [24, 1024, 768], P('fsdp', 'seq'), may hold values from -6 to 6
- lengths: int32 [24], P('fsdp'), may hold values from 512 to 1024, as said below
- w_qkv: bfloat16 [768, 2304], P('fsdp'), may hold values from -0.21875 to 0.21875
- w_out: bfloat16 [768, 768], P('fsdp'), may hold values from -0.375 to 0.375
- w_fc1: bfloat16 [768, 3072], P('fsdp'), may hold values from -0.21875 to 0.21875
- w_fc2: bfloat16 [3072, 768], P('fsdp'), may hold values from -0.1875 to 0.1875
- d_gains: bfloat16 [768, 3], P('fsdp'), may hold values from 0.5 to 1.5
- d_biases: bfloat16 [768, 7], P('fsdp'), may hold values from -3 to 3
- ff_gain: bfloat16 [3072], P('fsdp'), may hold values from 0.5 to 1.5
- ff_biases: bfloat16 [3072, 2], P('fsdp'), may hold values from -3 to 3
Outputs:
- block_out: bfloat16 [24, 1024, 768], P('fsdp', 'seq')
- input_grad: float32 [24, 1024, 768], P('fsdp', 'seq')
- w_qkv_grad: float32 [768, 2304], P('fsdp')
- w_out_grad: float32 [768, 768], P('fsdp')
- w_fc1_grad: float32 [768, 3072], P('fsdp')
- w_fc2_grad: float32 [3072, 768], P('fsdp')
- d_gains_grad: float32 [768, 3], P('fsdp')
- d_biases_grad: float32 [768, 7], P('fsdp')
- ff_gain_grad: float32 [3072], P('fsdp')
- ff_biases_grad: float32 [3072, 2], P('fsdp')
The draws below stay inside these ranges and needn't reach their ends.
Inputs may be any that keep to these rules, and one draw needn't show every extreme that they name: `lengths`: slots of a sequence from its length on are padding. One sequence has exactly 1024 live tokens and one exactly 512.
All inputs are finite; a program needn't handle non-finite values.
Results may differ from the reference program's by a relative error of at most 0.0085.
Values may be sent and summed in bfloat16 or wider, within the bound.
No kernel may reach another device: no remote copies, remote signals or barrier semaphores. Data moves between devices by JAX's collectives and lax.ppermute only.
A program may use at most 192 MiB of HBM per device.

```python
import jax
import jax.numpy as jnp
from jax import lax

D = 768
H = 12
HD = 64
FF = 3072
L = 1024
SEQS = 24


def draw_lengths(key, part):
    first_key, second_key = jax.random.split(jax.random.fold_in(key, 11))
    drawn = jax.random.randint(first_key, (SEQS,), L // 2, L + 1)
    order = jax.random.permutation(second_key, SEQS)
    drawn = drawn.at[order[0]].set(L)
    drawn = drawn.at[order[1]].set(L // 2)
    return drawn.astype(jnp.int32)


def raised(entries, own_key, source, target, blocks, factor):
    def block_of(axis_at):
        return (jnp.arange(entries.shape[axis_at]) // (entries.shape[axis_at] // blocks)).reshape((-1,) + (1,) * (entries.ndim - 1 - axis_at))

    first = jax.random.permutation(own_key, blocks)[block_of(target)]
    second = (block_of(target) + blocks // 2) % blocks
    return jnp.where((block_of(source) == first) | (block_of(source) == second), factor * entries, entries)


def steps_of(key, dims, shards, smallest, largest):
    factor_of, own = 1.0, jax.random.fold_in(key, 6)
    for position, blocks in shards:
        heights = jnp.exp(jax.random.uniform(jax.random.fold_in(own, position), (blocks,), jnp.float32, smallest / len(shards), largest / len(shards)))
        factor_of = factor_of * jnp.repeat(heights, dims[position] // blocks).reshape([-1 if axis == position else 1 for axis in range(len(dims))])
    return factor_of


def centred(own_key, shape, scale, reach, shards=(), kind=jnp.bfloat16):
    entries = scale * jax.random.normal(own_key, shape, jnp.float32)
    if shards:
        entries = entries * steps_of(own_key, shape, shards, -0.22, 0.18)
    return jnp.clip(entries, -reach, reach).astype(kind)


def bell_draw_with(rng, dims, scale, most, cuts, heavy, kind=jnp.bfloat16):
    values = scale * jax.random.normal(rng, dims, jnp.float32)
    if cuts:
        values = values * steps_of(rng, dims, cuts, -0.22, 0.18)
    return jnp.clip(raised(values, jax.random.fold_in(rng, 3), *heavy), -most, most).astype(kind)


def setup_inputs(seed: int = 0) -> dict:
    key_of = jax.random.split(jax.random.key(seed), 12)
    return {
        "activations": centred(key_of[0], (SEQS, L, D), 1.0, 6.0, ((0, 8), (1, 4))),
        "cotangent": bell_draw_with(key_of[1], (SEQS, L, D), 1.0, 6.0, ((0, 8), (1, 4)), (0, 2, 8, 2.0)),
        "lengths": draw_lengths(jax.random.fold_in(key_of[11], 71), 0),
        "w_qkv": centred(key_of[3], (D, 3 * D), D ** -0.5, 0.21875, ((0, 8),)),
        "w_out": centred(key_of[4], (D, D), (D // 3) ** -0.5, 0.375, ((0, 8),)),
        "w_fc1": centred(key_of[5], (D, FF), D ** -0.5, 0.21875, ((0, 8),)),
        "w_fc2": centred(key_of[6], (FF, D), (FF // 3) ** -0.5, 0.1875, ((0, 8),)),
        "d_gains": jnp.clip(1.0 + 0.1 * jax.random.normal(key_of[7], (D, 3), jnp.float32), 0.5, 1.5).astype(jnp.bfloat16),
        "d_biases": centred(key_of[8], (D, 7), 0.5, 3.0, ((0, 8),)),
        "ff_gain": jnp.clip(1.0 + 0.1 * jax.random.normal(key_of[9], (FF,), jnp.float32), 0.5, 1.5).astype(jnp.bfloat16),
        "ff_biases": centred(key_of[10], (FF, 2), 0.5, 3.0, ((0, 8),)),
    }


@jax.custom_vjp
def low(v):
    return lax.optimization_barrier(v.astype(jnp.bfloat16)).astype(jnp.float32)

@jax.custom_vjp
def low_back(v):
    return v

def low_keep(v):
    return (low(v), None)

def low_pass(kept, grad):
    return (grad,)

def back_keep(v):
    return (v, None)

def back_low(kept, grad):
    return (low(grad),)
low.defvjp(low_keep, low_pass)
low_back.defvjp(back_keep, back_low)
eps = 1e-05
highest = lax.Precision.HIGHEST

def layer_norm(values, norm_gain, norm_shift):
    center = values - lax.optimization_barrier(jnp.mean(values, axis=-1, keepdims=True))
    spread = lax.optimization_barrier(jnp.mean(center * center, axis=-1, keepdims=True))
    return center * lax.rsqrt(spread + eps) * norm_gain + norm_shift

def attend_head(query, key_rows, value_rows, key_live):
    scores = jnp.einsum('pqd,pkd->pqk', query, key_rows, precision=highest) * 0.125
    scores = low_back(jnp.where(key_live[:, None, :], scores, -1e+30))
    row_top = lax.optimization_barrier(jnp.max(scores, axis=-1, keepdims=True))
    exp_scores = jnp.exp(scores - row_top)
    attn_probs = exp_scores / lax.optimization_barrier(jnp.sum(exp_scores, axis=-1, keepdims=True))
    mixed_out = jnp.einsum('pqk,pkd->pqd', low(attn_probs), value_rows, precision=highest)
    return low(low_back(mixed_out))

def block_forward(x_rows, key_live, params):
    w_qkv, w_out, w_fc1, w_fc2, d_gains, d_biases, ff_gain, ff_biases = params
    seq_here, seq_len, model_width = x_rows.shape
    normed_in = low(layer_norm(x_rows, d_gains[:, 0], d_biases[:, 0]))
    qkv_bias = jnp.concatenate([d_biases[:, 1], jnp.zeros_like(d_biases[:, 1]), d_biases[:, 2]])
    qkv_rows = low(low_back(jnp.dot(normed_in, w_qkv, precision=highest) + qkv_bias))
    qkv_rows = qkv_rows.reshape(seq_here, seq_len, 3, H, HD)
    head_major = jnp.moveaxis(qkv_rows, 3, 0)

    def per_head(head_rows):
        return attend_head(head_rows[:, :, 0], head_rows[:, :, 1], head_rows[:, :, 2], key_live)
    mixed_heads = lax.map(jax.checkpoint(per_head), head_major)
    attn_mixed = jnp.moveaxis(mixed_heads, 0, 2).reshape(seq_here, seq_len, model_width)
    attn_normed = low(layer_norm(attn_mixed, d_gains[:, 1], d_biases[:, 3]))
    resid_one = x_rows + low_back(jnp.dot(attn_normed, w_out, precision=highest)) + d_biases[:, 4]
    ffn_normed = low(layer_norm(resid_one, d_gains[:, 2], d_biases[:, 5]))
    pre_act = low_back(jnp.dot(ffn_normed, w_fc1, precision=highest) + ff_biases[:, 0])
    hidden = low(layer_norm(jax.nn.gelu(pre_act, approximate=False), ff_gain, ff_biases[:, 1]))
    feed_out = low_back(jnp.dot(hidden, w_fc2, precision=highest))
    live = key_live.astype(x_rows.dtype)[..., None]
    return live * (resid_one + feed_out + d_biases[:, 6])

def reference(activations, cotangent, lengths, w_qkv, w_out, w_fc1, w_fc2, d_gains, d_biases, ff_gain, ff_biases):
    seq_total = activations.shape[0]
    per_step = max(1, min(seq_total, 4096 // L))
    while seq_total % per_step != 0:
        per_step = per_step - 1
    step_count = seq_total // per_step
    params = (w_qkv.astype(jnp.float32), w_out.astype(jnp.float32), w_fc1.astype(jnp.float32), w_fc2.astype(jnp.float32), d_gains.astype(jnp.float32), d_biases.astype(jnp.float32), ff_gain.astype(jnp.float32), ff_biases.astype(jnp.float32))
    key_live = jnp.arange(L, dtype=jnp.int32)[None, :] < lengths[:, None]
    inputs = (activations.astype(jnp.float32).reshape(step_count, per_step, L, D), cotangent.astype(jnp.float32).reshape(step_count, per_step, L, D), key_live.reshape(step_count, per_step, L))

    def one_step(grad_sums, step_in):
        x_part, cot_part, live_part = step_in

        def forward_fn(x_in, param_in):
            return block_forward(x_in, live_part, param_in)
        out_part, pull_back = jax.vjp(forward_fn, x_part, params)
        grad_x, grad_params = pull_back(cot_part)
        grad_sums = jax.tree.map(lambda total_old, added: total_old + added, grad_sums, grad_params)
        return (grad_sums, (out_part, grad_x))
    zero_sums = jax.tree.map(jnp.zeros_like, params)
    grad_sums, (out_all, grad_all) = lax.scan(one_step, zero_sums, inputs)
    block_out = out_all.reshape(seq_total, L, D).astype(jnp.bfloat16)
    input_grad = grad_all.reshape(seq_total, L, D).astype(jnp.float32)
    return (block_out, input_grad, grad_sums[0], grad_sums[1], grad_sums[2], grad_sums[3], grad_sums[4], grad_sums[5], grad_sums[6], grad_sums[7])
```

```python
import functools

import jax
import jax.numpy as jnp
from jax import lax
from jax.experimental import pallas as pl
from jax.experimental.pallas import tpu as pltpu
from jax.sharding import PartitionSpec as P

H = 12
HD = 64
eps = 1e-05
F32 = jnp.float32
BF16 = jnp.bfloat16
NT = (((1,), (1,)), ((), ()))


def mm(left, right):
    return jnp.dot(left, right, preferred_element_type=F32)


def mm_nt(left, right):
    return lax.dot_general(left, right, NT, preferred_element_type=F32)


def mm_tn(left, right):
    return lax.dot_general(left, right, (((0,), (0,)), ((), ())), preferred_element_type=F32)


def centred(values):
    center = values - jnp.mean(values, axis=-1, keepdims=True)
    spread = jnp.mean(center * center, axis=-1, keepdims=True)
    scale = lax.rsqrt(spread + eps)
    return center * scale, scale


def norm_back(grad, unit, scale):
    return scale * (
        grad
        - jnp.mean(grad, axis=-1, keepdims=True)
        - unit * jnp.mean(grad * unit, axis=-1, keepdims=True)
    )


def key_mask(block, live_rows):
    rows = lax.broadcasted_iota(jnp.int32, block.shape, 0)
    return jnp.where(rows < live_rows, block, -1e30)


def attend_kernel(parts, heads, rows, info, *refs):
    xs = refs[:parts]
    w, gain, shift, bias = refs[parts : parts + 4]
    nrm, q, k, v, kt = refs[parts + 4 : parts + 9]
    outs = refs[parts + 9 : 2 * parts + 9]
    lse, vt, ot = refs[2 * parts + 9 :]
    me, live = info[0], info[1]
    span = heads * HD
    for j in range(parts):
        g = me ^ j
        at = pl.ds(pl.multiple_of(g * rows, rows), rows)
        unit, _ = centred(xs[j][...].astype(F32))
        normed = (unit * gain[...] + shift[...]).astype(BF16)
        nrm[j] = normed
        qkv = mm(normed, w[...]) + bias[...]
        for h in range(heads):
            cols = slice(h * HD, (h + 1) * HD)
            kk = qkv[:, span + h * HD : span + (h + 1) * HD]
            vv = qkv[:, 2 * span + h * HD : 2 * span + (h + 1) * HD]
            q[h, at, :] = (qkv[:, cols].astype(BF16).astype(F32) * 0.125).astype(BF16)
            k[h, at, :] = kk.astype(BF16)
            v[h, at, :] = vv.astype(BF16)
            kt[h, g] = kk.T.astype(BF16)
            vt[h, g] = vv.T.astype(BF16)

    def variant(count):
        def step(t, carry):
            h, j = t // parts, t % parts
            g = me ^ j

            @pl.when(g < count)
            def _():
                qb = q[h, pl.ds(pl.multiple_of(g * rows, rows), rows), :]
                scores = [
                    mm_nt(k[h, c * rows : (c + 1) * rows, :], qb) for c in range(count)
                ]
                scores[-1] = key_mask(scores[-1], live - (count - 1) * rows)
                top = functools.reduce(
                    jnp.maximum, [jnp.max(s, axis=0, keepdims=True) for s in scores]
                )
                total, mixed = 0.0, 0.0
                for c in range(count):
                    e = jnp.exp(scores[c] - top)
                    total = total + jnp.sum(e, axis=0, keepdims=True)
                    mixed = mixed + mm(vt[h, c], e.astype(BF16))
                ot[t] = mixed / total
                lse[t] = jnp.broadcast_to(top + jnp.log(total), (8, rows))

            @pl.when(g >= count)
            def _():
                ot[t] = jnp.zeros((HD, rows), F32)
                lse[t] = jnp.zeros((8, rows), F32)

            return carry

        lax.fori_loop(0, heads * parts, step, 0)

    blocks = (live + rows - 1) // rows
    for count in range(1, parts + 1):
        pl.when(blocks == count)(functools.partial(variant, count))
    for j in range(parts):
        stacked = jnp.concatenate([ot[h * parts + j] for h in range(heads)], axis=0)
        outs[j][...] = stacked.T.astype(BF16)


def attend_forward(place, live, xs, w, gain, shift, bias):
    parts, (rows, width) = len(xs), xs[0].shape
    span = w.shape[1] // 3
    heads, full = span // HD, parts * rows
    shape = jax.ShapeDtypeStruct
    vmem = pl.BlockSpec(memory_space=pltpu.VMEM)
    outs = pl.pallas_call(
        functools.partial(attend_kernel, parts, heads, rows),
        in_specs=[pl.BlockSpec(memory_space=pltpu.SMEM)] + [vmem] * (parts + 4),
        out_specs=[vmem] * (parts + 6),
        out_shape=[
            shape((parts, rows, width), BF16),
            shape((heads, full, HD), BF16),
            shape((heads, full, HD), BF16),
            shape((heads, full, HD), BF16),
            shape((heads, parts, HD, rows), BF16),
        ]
        + [shape((rows, span), BF16)] * parts
        + [shape((heads * parts, 8, rows), F32)],
        scratch_shapes=[
            pltpu.VMEM((heads, parts, HD, rows), BF16),
            pltpu.VMEM((heads * parts, HD, rows), F32),
        ],
        cost_estimate=pl.CostEstimate(
            flops=2 * full * width * 3 * span + 4 * full * full * span,
            bytes_accessed=2 * (2 * full * width + width * 3 * span + 6 * full * span),
            transcendentals=heads * full * full,
        ),
        compiler_params=pltpu.CompilerParams(vmem_limit_bytes=48 << 20),
        name="attend_forward",
    )(jnp.stack([place, live]), *xs, w, gain, shift, bias)
    return outs[0], outs[1:5], outs[5 : 5 + parts], outs[5 + parts]


def attend_back_kernel(parts, heads, rows, info, *refs):
    xs, grads = refs[:parts], refs[parts : 2 * parts]
    w, q, k, v, kt, lse = refs[2 * parts : 2 * parts + 6]
    dqkv = refs[2 * parts + 6]
    dns = refs[2 * parts + 7 : 3 * parts + 7]
    sums, cols = refs[3 * parts + 7 : 3 * parts + 9]
    do, dk, dv, dqt = refs[3 * parts + 9 :]
    me, live = info[0], info[1]
    for j in range(parts):
        block = grads[j][...].astype(F32)
        for h in range(heads):
            do[h * parts + j] = block[:, h * HD : (h + 1) * HD].astype(BF16)
    dk[...] = jnp.zeros_like(dk)
    dv[...] = jnp.zeros_like(dv)

    def variant(count):
        def step(t, carry):
            h, j = t // parts, t % parts
            g = me ^ j

            @pl.when(g < count)
            def _():
                qb = q[h, pl.ds(pl.multiple_of(g * rows, rows), rows), :]
                dob = do[t]
                shift = lse[t][0:1, :]
                probs, dps, inner = [], [], 0.0
                for c in range(count):
                    span = slice(c * rows, (c + 1) * rows)
                    s = mm_nt(k[h, span, :], qb)
                    if c == count - 1:
                        s = key_mask(s, live - c * rows)
                    p = jnp.exp(s - shift)
                    dp = mm_nt(v[h, span, :], dob)
                    inner = inner + jnp.sum(p * dp, axis=0, keepdims=True)
                    dv[h, c] += mm(p.astype(BF16), dob)
                    probs.append(p)
                    dps.append(dp)
                dq = 0.0
                for c in range(count):
                    ds = (probs[c] * (dps[c] - inner)).astype(BF16)
                    dk[h, c] += mm(ds, qb)
                    dq = dq + mm(kt[h, c], ds)
                dqt[t] = dq * 0.125

            @pl.when(g >= count)
            def _():
                dqt[t] = jnp.zeros((HD, rows), F32)

            return carry

        lax.fori_loop(0, heads * parts, step, 0)

    blocks = (live + rows - 1) // rows
    for count in range(1, parts + 1):
        pl.when(blocks == count)(functools.partial(variant, count))
    shift_sum, gain_sum, col_sum = 0.0, 0.0, 0.0
    for j in range(parts):
        g = me ^ j
        dq = jnp.concatenate([dqt[h * parts + j] for h in range(heads)], axis=0).T
        pieces = [dq] + [dk[h, g] for h in range(heads)] + [dv[h, g] for h in range(heads)]
        block = jnp.concatenate(pieces, axis=1).astype(BF16)
        dqkv[j] = block
        col_sum = col_sum + jnp.sum(block.astype(F32), axis=0, keepdims=True)
        dn = mm_nt(block, w[...])
        unit, _ = centred(xs[j][...].astype(F32))
        shift_sum = shift_sum + jnp.sum(dn, axis=0, keepdims=True)
        gain_sum = gain_sum + jnp.sum(dn * unit, axis=0, keepdims=True)
        dns[j][...] = dn.astype(BF16)
    sums[0:1, :] = gain_sum
    sums[1:2, :] = shift_sum
    cols[0:1, :] = col_sum


def attend_backward(place, live, xs, grads, w, saved, lse):
    parts, (rows, width) = len(xs), xs[0].shape
    span = w.shape[1] // 3
    heads, full = span // HD, parts * rows
    shape = jax.ShapeDtypeStruct
    vmem = pl.BlockSpec(memory_space=pltpu.VMEM)
    outs = pl.pallas_call(
        functools.partial(attend_back_kernel, parts, heads, rows),
        in_specs=[pl.BlockSpec(memory_space=pltpu.SMEM)] + [vmem] * (2 * parts + 6),
        out_specs=[vmem] * (parts + 3),
        out_shape=[shape((parts, rows, 3 * span), BF16)]
        + [shape((rows, width), BF16)] * parts
        + [shape((2, width), F32), shape((1, 3 * span), F32)],
        scratch_shapes=[
            pltpu.VMEM((heads * parts, rows, HD), BF16),
            pltpu.VMEM((heads, parts, rows, HD), F32),
            pltpu.VMEM((heads, parts, rows, HD), F32),
            pltpu.VMEM((heads * parts, HD, rows), F32),
        ],
        cost_estimate=pl.CostEstimate(
            flops=2 * full * width * 3 * span + 10 * full * full * span,
            bytes_accessed=2 * (3 * full * width + width * 3 * span + 9 * full * span),
            transcendentals=heads * full * full,
        ),
        compiler_params=pltpu.CompilerParams(vmem_limit_bytes=48 << 20),
        name="attend_backward",
    )(jnp.stack([place, live]), *xs, *grads, w, *saved, lse)
    return outs[0], outs[1 : 1 + parts], outs[1 + parts], outs[2 + parts]


def swap(values, axis, mask):
    count = lax.axis_size(axis)
    return lax.ppermute(values, axis, [(i, i ^ mask) for i in range(count)])


def pick(values, index, axis):
    return lax.dynamic_index_in_dim(values, index, axis, keepdims=False)


def spread_blocks(block, axis):
    count, me = lax.axis_size(axis), lax.axis_index(axis)
    held = {0: block}
    bit = count // 2
    while bit:
        held |= {mask | bit: swap(part, axis, bit) for mask, part in held.items()}
        bit //= 2
    rows = block.shape[0]
    whole = jnp.zeros((count * rows,) + block.shape[1:], block.dtype)
    for mask, part in held.items():
        start = ((me ^ mask) * rows,) + (0,) * (block.ndim - 1)
        whole = lax.dynamic_update_slice(whole, part, start)
    return whole


def sum_blocks(blocks, axis):
    count, me = lax.axis_size(axis), lax.axis_index(axis)
    bit = 1
    while bit < count:
        pairs = blocks.reshape((blocks.shape[0] // 2, 2) + blocks.shape[1:])
        mine = (me // bit) % 2
        sent = swap(pick(pairs, 1 - mine, 1).astype(BF16), axis, bit)
        blocks = pick(pairs, mine, 1).astype(F32) + sent.astype(F32)
        bit *= 2
    return blocks[0]


def shards(
    activations,
    cotangent,
    lengths,
    w_qkv,
    w_out,
    w_fc1,
    w_fc2,
    d_gains,
    d_biases,
    ff_gain,
    ff_biases,
):
    seqs, rows, width = activations.shape
    parts, owners = lax.axis_size("seq"), lax.axis_size("fsdp")
    s, owner = lax.axis_index("seq"), lax.axis_index("fsdp")
    core = s % 2
    span = width // parts
    n = seqs * rows
    own_rows = w_qkv.shape[0]
    own_ff = w_fc2.shape[0]
    half_ff = own_ff // 2
    ff_half = half_ff * owners
    quarter = own_ff // own_rows

    own_w = pick(w_qkv.reshape(own_rows, 3, parts, span), s, 2).reshape(own_rows, 3 * span)
    ff_small = jnp.concatenate([ff_gain[:, None], ff_biases], axis=1).T.reshape(
        3 * quarter, own_rows
    )
    small = jnp.concatenate([d_gains.T, d_biases.T, ff_small], axis=0)
    kinds = small.shape[0]
    small_rows = 32
    small = jnp.pad(small, ((0, small_rows - kinds), (0, 3 * span - own_rows)))
    first = spread_blocks(jnp.concatenate([own_w, small], axis=0), "fsdp")
    first = first.reshape(owners, own_rows + small_rows, 3 * span)
    my_qkv = first[:, :own_rows].reshape(width, 3 * span)
    small = first[:, own_rows : own_rows + kinds, :own_rows].astype(F32)
    d_small = small[:, :10].transpose(1, 0, 2).reshape(10, width)
    gains, biases = d_small[:3], d_small[3:]
    ff_small = small[:, 10:].reshape(owners, 3, 2, half_ff)
    ff_small = jnp.concatenate(
        [pick(ff_small, core, 2), pick(ff_small, 1 - core, 2)], axis=0
    )
    ff_small = ff_small.reshape(2, owners, 3, half_ff).transpose(2, 0, 1, 3).reshape(3, 2 * ff_half)
    feed_gain, feed_bias, feed_shift = ff_small[0], ff_small[1], ff_small[2]

    out_half = pick(w_out.reshape(own_rows, 2, width // 2), core, 1)
    fc1_half = pick(w_fc1.reshape(own_rows, owners, 2, half_ff), core, 2).reshape(own_rows, ff_half)
    fc2_half = pick(w_fc2.reshape(2, half_ff, width), core, 0)
    early = lax.all_gather(
        jnp.concatenate([out_half, fc1_half], axis=1), "fsdp", axis=0, tiled=True
    )
    late = lax.all_gather(fc2_half, "fsdp", axis=0, tiled=True)
    early_other, late_other = swap(early, "seq", 1), swap(late, "seq", 1)
    half = width // 2
    mine, theirs = early[:, :half], early_other[:, :half]
    full_out = jnp.where(
        core == 0,
        jnp.concatenate([mine, theirs], axis=1),
        jnp.concatenate([theirs, mine], axis=1),
    )
    full_fc1 = jnp.concatenate([early[:, half:], early_other[:, half:]], axis=1)
    full_fc2 = jnp.concatenate([late, late_other], axis=0)

    qkv_bias = pick(
        jnp.stack([biases[1], jnp.zeros_like(biases[1]), biases[2]]).reshape(3, parts, span), s, 1
    ).reshape(1, 3 * span)
    x_parts, mixed_parts, kept = [], [], []
    for i in range(seqs):
        mine = activations[i]
        across = swap(mine, "seq", 2)
        x_parts.append([mine, swap(mine, "seq", 1), across, swap(across, "seq", 1)])
    for i in range(seqs):
        normed, saved, outs, lse = attend_forward(
            s, lengths[i], x_parts[i], my_qkv, gains[0:1], biases[0:1], qkv_bias
        )
        kept.append((normed, saved, lse))
        mixed_parts.append([outs[0]] + [swap(outs[j], "seq", j) for j in range(1, parts)])

    order = s ^ jnp.arange(parts)

    def by_parts(values):
        return jnp.take(values.reshape((parts, span) + values.shape[1:]), order, axis=0).reshape(
            values.shape
        )

    mixed_gain, mixed_shift = by_parts(gains[1]), by_parts(biases[3])
    part_out = by_parts(full_out)
    positions = s * rows + jnp.arange(rows, dtype=jnp.int32)
    row_live = (positions[None, :] < lengths[:, None]).astype(F32).reshape(n, 1)
    x_rows = activations.reshape(n, width).astype(F32)
    attn_mixed = jnp.concatenate([jnp.concatenate(p, axis=1) for p in mixed_parts], axis=0)
    mixed_unit, mixed_scale = centred(attn_mixed.astype(F32))
    attn_normed = (mixed_unit * mixed_gain + mixed_shift).astype(BF16)
    resid_one = x_rows + mm(attn_normed, part_out) + biases[4]
    ffn_unit, ffn_scale = centred(resid_one)
    ffn_normed = (ffn_unit * gains[2] + biases[5]).astype(BF16)
    pre_act = mm(ffn_normed, full_fc1) + feed_bias
    act, act_pull = jax.vjp(lambda v: jax.nn.gelu(v, approximate=False), pre_act)
    act_unit, act_scale = centred(act)
    hidden = (act_unit * feed_gain + feed_shift).astype(BF16)
    block_out = (row_live * (resid_one + mm(hidden, full_fc2) + biases[6])).astype(BF16)

    out_grad_low = jnp.where(row_live > 0, cotangent.reshape(n, width), 0)
    out_grad = out_grad_low.astype(F32)
    grad_fc2 = mm_tn(hidden, out_grad_low)
    hidden_grad = mm_nt(out_grad_low, full_fc2)
    grad_feed_gain = jnp.sum(hidden_grad * act_unit, axis=0)
    grad_feed_shift = jnp.sum(hidden_grad, axis=0)
    (pre_grad,) = act_pull(norm_back(hidden_grad * feed_gain, act_unit, act_scale))
    pre_grad = pre_grad.astype(BF16)
    grad_feed_bias = jnp.sum(pre_grad.astype(F32), axis=0)
    grad_fc1 = mm_tn(ffn_normed, pre_grad)
    ffn_grad = mm_nt(pre_grad, full_fc1)
    resid_grad = out_grad + norm_back(ffn_grad * gains[2], ffn_unit, ffn_scale)
    branch_grad = resid_grad.astype(BF16)
    grad_out = mm_tn(attn_normed, branch_grad)
    normed_grad = mm_nt(branch_grad, part_out)
    mixed_grad = norm_back(normed_grad * mixed_gain, mixed_unit, mixed_scale).astype(BF16)

    grad_own, summed, head_sums, unit_sums = 0.0, [], 0.0, 0.0
    for i in range(seqs):
        block = mixed_grad[i * rows : (i + 1) * rows]
        pieces = [block[:, j * span : (j + 1) * span] for j in range(parts)]
        pieces = [pieces[0]] + [swap(pieces[j], "seq", j) for j in range(1, parts)]
        normed, saved, lse = kept[i]
        dqkv, dns, sums, cols = attend_backward(
            s, lengths[i], x_parts[i], pieces, my_qkv, saved, lse
        )
        grad_own = grad_own + mm_tn(
            normed.reshape(parts * rows, width), dqkv.reshape(parts * rows, 3 * span)
        )
        unit_sums, head_sums = unit_sums + sums, head_sums + cols
        near = [swap(dns[j], "seq", 1).astype(F32) for j in (1, 3)]
        far = (dns[2].astype(F32) + near[1]).astype(BF16)
        summed.append(dns[0].astype(F32) + near[0] + swap(far, "seq", 2).astype(F32))
    first_grad = jnp.concatenate(summed, axis=0)
    first_unit, first_scale = centred(x_rows)
    input_grad = resid_grad + norm_back(first_grad * gains[0], first_unit, first_scale)

    def head_columns(values):
        blank = jnp.zeros((parts, span), F32)
        return lax.dynamic_update_slice(blank, values[None], (s, 0)).reshape(width)

    inner_grad = normed_grad * mixed_unit
    small_grads = jnp.stack(
        [
            unit_sums[0],
            by_parts(jnp.sum(inner_grad, axis=0)),
            jnp.sum(ffn_grad * ffn_unit, axis=0),
            unit_sums[1],
            head_columns(head_sums[0, :span]),
            head_columns(head_sums[0, 2 * span :]),
            by_parts(jnp.sum(normed_grad, axis=0)),
            jnp.sum(resid_grad, axis=0),
            jnp.sum(ffn_grad, axis=0),
            jnp.sum(out_grad, axis=0),
        ]
    )
    feed_grads = jnp.stack([grad_feed_gain, grad_feed_bias, grad_feed_shift]).reshape(
        3, 2, owners, half_ff
    )
    feed_grads = jnp.where(core == 0, feed_grads, feed_grads[:, ::-1])
    small_blocks = jnp.concatenate(
        [
            small_grads.reshape(10, owners, own_rows).transpose(1, 0, 2),
            feed_grads.transpose(2, 0, 1, 3).reshape(owners, 3 * quarter, own_rows),
        ],
        axis=1,
    )
    small_blocks = jnp.pad(
        small_blocks, ((0, 0), (0, small_rows - kinds), (0, 3 * span - own_rows))
    )
    first_blocks = jnp.concatenate(
        [grad_own.reshape(owners, own_rows, 3 * span), small_blocks], axis=1
    )
    first_sum = sum_blocks(first_blocks, "fsdp")
    group = [first_sum] + [swap(first_sum, "seq", j) for j in range(1, parts)]
    stacked = jnp.stack([g[:own_rows] for g in group])
    w_qkv_grad = jnp.take(stacked, order, axis=0).reshape(parts, own_rows, 3, span)
    w_qkv_grad = w_qkv_grad.transpose(1, 2, 0, 3).reshape(own_rows, 3 * width)
    small_sum = sum(g[own_rows : own_rows + kinds, :own_rows] for g in group)
    feed_sum = small_sum[10:].reshape(3, own_ff)

    def halves(values, axis):
        size = values.shape[axis] // 2
        keep = lax.slice_in_dim(values, 0, size, axis=axis)
        give = lax.slice_in_dim(values, size, 2 * size, axis=axis)
        return (keep + swap(give.astype(BF16), "seq", 1).astype(F32)).astype(BF16)

    grad_out = by_parts(grad_out).reshape(width, 2, half)
    out_own = pick(grad_out, core, 1) + swap(pick(grad_out, 1 - core, 1).astype(BF16), "seq", 1)
    fc2_own = lax.psum_scatter(halves(grad_fc2, 0), "fsdp", scatter_dimension=0, tiled=True)
    rest = lax.psum_scatter(
        jnp.concatenate([out_own.astype(BF16), halves(grad_fc1, 1)], axis=1),
        "fsdp",
        scatter_dimension=0,
        tiled=True,
    )
    fc2_own = fc2_own.astype(F32) + swap(fc2_own, "seq", 2).astype(F32)
    rest = rest.astype(F32) + swap(rest, "seq", 2).astype(F32)
    fc2_other, rest_other = swap(fc2_own, "seq", 1), swap(rest, "seq", 1)

    def in_order(own, other, axis):
        pair = jnp.stack([own, other], axis=axis)
        return jnp.where(core == 0, pair, jnp.flip(pair, axis=axis))

    w_fc2_grad = in_order(fc2_own, fc2_other, 0).reshape(own_ff, width)
    w_out_grad = in_order(rest[:, :half], rest_other[:, :half], 1).reshape(own_rows, width)
    w_fc1_grad = in_order(
        rest[:, half:].reshape(own_rows, owners, half_ff),
        rest_other[:, half:].reshape(own_rows, owners, half_ff),
        2,
    ).reshape(own_rows, 2 * ff_half)
    return (
        block_out.reshape(seqs, rows, width),
        input_grad.reshape(seqs, rows, width),
        w_qkv_grad,
        w_out_grad,
        w_fc1_grad,
        w_fc2_grad,
        small_sum[:3].T,
        small_sum[3:10].T,
        feed_sum[0],
        feed_sum[1:].T,
    )


def solution(mesh):
    return jax.shard_map(
        shards,
        mesh=mesh,
        in_specs=(
            P("fsdp", "seq", None),
            P("fsdp", "seq", None),
            P("fsdp"),
            P("fsdp", None),
            P("fsdp", None),
            P("fsdp", None),
            P("fsdp", None),
            P("fsdp", None),
            P("fsdp", None),
            P("fsdp"),
            P("fsdp", None),
        ),
        out_specs=(
            P("fsdp", "seq", None),
            P("fsdp", "seq", None),
            P("fsdp", None),
            P("fsdp", None),
            P("fsdp", None),
            P("fsdp", None),
            P("fsdp", None),
            P("fsdp", None),
            P("fsdp"),
            P("fsdp", None),
        ),
        check_vma=False,
    )
```

```python
import functools

import jax
import jax.numpy as jnp
from jax import lax
from jax.experimental import pallas as pl
from jax.experimental.pallas import tpu as pltpu
from jax.sharding import PartitionSpec as P

H = 12
HD = 64
eps = 1e-05
F32 = jnp.float32
BF16 = jnp.bfloat16
NT = (((1,), (1,)), ((), ()))


def mm(left, right):
    return jnp.dot(left, right, preferred_element_type=F32)


def mm_nt(left, right):
    return lax.dot_general(left, right, NT, preferred_element_type=F32)


def mm_tn(left, right):
    return lax.dot_general(left, right, (((0,), (0,)), ((), ())), preferred_element_type=F32)


def centred(values):
    center = values - jnp.mean(values, axis=-1, keepdims=True)
    spread = jnp.mean(center * center, axis=-1, keepdims=True)
    scale = lax.rsqrt(spread + eps)
    return center * scale, scale


def norm_back(grad, unit, scale):
    return scale * (
        grad
        - jnp.mean(grad, axis=-1, keepdims=True)
        - unit * jnp.mean(grad * unit, axis=-1, keepdims=True)
    )


def key_mask(block, live_rows):
    rows = lax.broadcasted_iota(jnp.int32, block.shape, 0)
    return jnp.where(rows < live_rows, block, -1e30)


def attend_kernel(parts, heads, rows, info, *refs):
    xs = refs[:parts]
    w, gain, shift, bias = refs[parts : parts + 4]
    nrm, q, k, v, kt = refs[parts + 4 : parts + 9]
    outs = refs[parts + 9 : 2 * parts + 9]
    lse, vt, ot = refs[2 * parts + 9 :]
    me, live = info[0], info[1]
    span = heads * HD
    for j in range(parts):
        g = me ^ j
        at = pl.ds(pl.multiple_of(g * rows, rows), rows)
        unit, _ = centred(xs[j][...].astype(F32))
        normed = (unit * gain[...] + shift[...]).astype(BF16)
        nrm[j] = normed
        qkv = mm(normed, w[...]) + bias[...]
        for h in range(heads):
            cols = slice(h * HD, (h + 1) * HD)
            kk = qkv[:, span + h * HD : span + (h + 1) * HD]
            vv = qkv[:, 2 * span + h * HD : 2 * span + (h + 1) * HD]
            q[h, at, :] = (qkv[:, cols].astype(BF16).astype(F32) * 0.125).astype(BF16)
            k[h, at, :] = kk.astype(BF16)
            v[h, at, :] = vv.astype(BF16)
            kt[h, g] = kk.T.astype(BF16)
            vt[h, g] = vv.T.astype(BF16)

    def variant(count):
        def step(t, carry):
            h, j = t // parts, t % parts
            g = me ^ j

            @pl.when(g < count)
            def _():
                qb = q[h, pl.ds(pl.multiple_of(g * rows, rows), rows), :]
                scores = [
                    mm_nt(k[h, c * rows : (c + 1) * rows, :], qb) for c in range(count)
                ]
                scores[-1] = key_mask(scores[-1], live - (count - 1) * rows)
                top = functools.reduce(
                    jnp.maximum, [jnp.max(s, axis=0, keepdims=True) for s in scores]
                )
                total, mixed = 0.0, 0.0
                for c in range(count):
                    e = jnp.exp(scores[c] - top)
                    total = total + jnp.sum(e, axis=0, keepdims=True)
                    mixed = mixed + mm(vt[h, c], e.astype(BF16))
                ot[t] = mixed / total
                lse[t] = jnp.broadcast_to(top + jnp.log(total), (8, rows))

            @pl.when(g >= count)
            def _():
                ot[t] = jnp.zeros((HD, rows), F32)
                lse[t] = jnp.zeros((8, rows), F32)

            return carry

        lax.fori_loop(0, heads * parts, step, 0)

    blocks = (live + rows - 1) // rows
    for count in range(1, parts + 1):
        pl.when(blocks == count)(functools.partial(variant, count))
    for j in range(parts):
        stacked = jnp.concatenate([ot[h * parts + j] for h in range(heads)], axis=0)
        outs[j][...] = stacked.T.astype(BF16)


def attend_forward(place, live, xs, w, gain, shift, bias):
    parts, (rows, width) = len(xs), xs[0].shape
    span = w.shape[1] // 3
    heads, full = span // HD, parts * rows
    shape = jax.ShapeDtypeStruct
    vmem = pl.BlockSpec(memory_space=pltpu.VMEM)
    outs = pl.pallas_call(
        functools.partial(attend_kernel, parts, heads, rows),
        in_specs=[pl.BlockSpec(memory_space=pltpu.SMEM)] + [vmem] * (parts + 4),
        out_specs=[vmem] * (parts + 6),
        out_shape=[
            shape((parts, rows, width), BF16),
            shape((heads, full, HD), BF16),
            shape((heads, full, HD), BF16),
            shape((heads, full, HD), BF16),
            shape((heads, parts, HD, rows), BF16),
        ]
        + [shape((rows, span), BF16)] * parts
        + [shape((heads * parts, 8, rows), F32)],
        scratch_shapes=[
            pltpu.VMEM((heads, parts, HD, rows), BF16),
            pltpu.VMEM((heads * parts, HD, rows), F32),
        ],
        cost_estimate=pl.CostEstimate(
            flops=2 * full * width * 3 * span + 4 * full * full * span,
            bytes_accessed=2 * (2 * full * width + width * 3 * span + 6 * full * span),
            transcendentals=heads * full * full,
        ),
        compiler_params=pltpu.CompilerParams(vmem_limit_bytes=48 << 20),
        name="attend_forward",
    )(jnp.stack([place, live]), *xs, w, gain, shift, bias)
    return outs[0], outs[1:5], outs[5 : 5 + parts], outs[5 + parts]


def attend_back_kernel(parts, heads, rows, info, *refs):
    xs, grads = refs[:parts], refs[parts : 2 * parts]
    w, q, k, v, kt, lse = refs[2 * parts : 2 * parts + 6]
    dqkv = refs[2 * parts + 6]
    dns = refs[2 * parts + 7 : 3 * parts + 7]
    sums, cols = refs[3 * parts + 7 : 3 * parts + 9]
    do, dk, dv, dqt = refs[3 * parts + 9 :]
    me, live = info[0], info[1]
    for j in range(parts):
        block = grads[j][...].astype(F32)
        for h in range(heads):
            do[h * parts + j] = block[:, h * HD : (h + 1) * HD].astype(BF16)
    dk[...] = jnp.zeros_like(dk)
    dv[...] = jnp.zeros_like(dv)

    def variant(count):
        def step(t, carry):
            h, j = t // parts, t % parts
            g = me ^ j

            @pl.when(g < count)
            def _():
                qb = q[h, pl.ds(pl.multiple_of(g * rows, rows), rows), :]
                dob = do[t]
                shift = lse[t][0:1, :]
                probs, dps, inner = [], [], 0.0
                for c in range(count):
                    span = slice(c * rows, (c + 1) * rows)
                    s = mm_nt(k[h, span, :], qb)
                    if c == count - 1:
                        s = key_mask(s, live - c * rows)
                    p = jnp.exp(s - shift)
                    dp = mm_nt(v[h, span, :], dob)
                    inner = inner + jnp.sum(p * dp, axis=0, keepdims=True)
                    dv[h, c] += mm(p.astype(BF16), dob)
                    probs.append(p)
                    dps.append(dp)
                dq = 0.0
                for c in range(count):
                    ds = (probs[c] * (dps[c] - inner)).astype(BF16)
                    dk[h, c] += mm(ds, qb)
                    dq = dq + mm(kt[h, c], ds)
                dqt[t] = dq * 0.125

            @pl.when(g >= count)
            def _():
                dqt[t] = jnp.zeros((HD, rows), F32)

            return carry

        lax.fori_loop(0, heads * parts, step, 0)

    blocks = (live + rows - 1) // rows
    for count in range(1, parts + 1):
        pl.when(blocks == count)(functools.partial(variant, count))
    shift_sum, gain_sum, col_sum = 0.0, 0.0, 0.0
    for j in range(parts):
        g = me ^ j
        dq = jnp.concatenate([dqt[h * parts + j] for h in range(heads)], axis=0).T
        pieces = [dq] + [dk[h, g] for h in range(heads)] + [dv[h, g] for h in range(heads)]
        block = jnp.concatenate(pieces, axis=1).astype(BF16)
        dqkv[j] = block
        col_sum = col_sum + jnp.sum(block.astype(F32), axis=0, keepdims=True)
        dn = mm_nt(block, w[...])
        unit, _ = centred(xs[j][...].astype(F32))
        shift_sum = shift_sum + jnp.sum(dn, axis=0, keepdims=True)
        gain_sum = gain_sum + jnp.sum(dn * unit, axis=0, keepdims=True)
        dns[j][...] = dn.astype(BF16)
    sums[0:1, :] = gain_sum
    sums[1:2, :] = shift_sum
    cols[0:1, :] = col_sum


def attend_backward(place, live, xs, grads, w, saved, lse):
    parts, (rows, width) = len(xs), xs[0].shape
    span = w.shape[1] // 3
    heads, full = span // HD, parts * rows
    shape = jax.ShapeDtypeStruct
    vmem = pl.BlockSpec(memory_space=pltpu.VMEM)
    outs = pl.pallas_call(
        functools.partial(attend_back_kernel, parts, heads, rows),
        in_specs=[pl.BlockSpec(memory_space=pltpu.SMEM)] + [vmem] * (2 * parts + 6),
        out_specs=[vmem] * (parts + 3),
        out_shape=[shape((parts, rows, 3 * span), BF16)]
        + [shape((rows, width), BF16)] * parts
        + [shape((2, width), F32), shape((1, 3 * span), F32)],
        scratch_shapes=[
            pltpu.VMEM((heads * parts, rows, HD), BF16),
            pltpu.VMEM((heads, parts, rows, HD), F32),
            pltpu.VMEM((heads, parts, rows, HD), F32),
            pltpu.VMEM((heads * parts, HD, rows), F32),
        ],
        cost_estimate=pl.CostEstimate(
            flops=2 * full * width * 3 * span + 10 * full * full * span,
            bytes_accessed=2 * (3 * full * width + width * 3 * span + 9 * full * span),
            transcendentals=heads * full * full,
        ),
        compiler_params=pltpu.CompilerParams(vmem_limit_bytes=48 << 20),
        name="attend_backward",
    )(jnp.stack([place, live]), *xs, *grads, w, *saved, lse)
    return outs[0], outs[1 : 1 + parts], outs[1 + parts], outs[2 + parts]


def live_only(values, first, live):
    rows = first + lax.broadcasted_iota(jnp.int32, values.shape, 0)
    return jnp.where(rows < live, values, jnp.zeros_like(values))


def folded(values):
    return functools.reduce(
        jnp.add, [values[r : r + 8] for r in range(0, values.shape[0], 8)]
    )


def token_kernel(plan, seqs, parts, info, *refs):
    refs = list(refs)
    take = lambda count: [refs.pop(0) for _ in range(count)]
    sources = take(max(p[0] for p in plan) + 1)
    pieces = take(seqs * parts)
    x, cot, dvec, mgain, mshift, fvec = take(6)
    block_out, resid_grad, fnorm, branch, og, anorm = take(6)
    hid, pg = take(2), take(4)
    mds = take(seqs * parts)
    dsum, msum, fsum = take(3)
    wo, w1, w2, ob, munit, mscale, res, runit, rscale = take(9)
    pre, cdf, act, hg, fscale, ngs, dacc, macc, facc, sems = take(10)
    step = pl.program_id(0)
    me, core = info[seqs], info[seqs + 1]
    live = info[step] - me * x.shape[0]
    rows, width = x.shape
    span, units = width // parts, pre.shape[1]
    half, tile, wide = units // 2, 16, 384
    targets = {"out": wo, "fc1": w1, "fc2": w2}

    @pl.when(step == 0)
    def _():
        copies = []
        for index, (src, k, start, count, name, at, flip, col) in enumerate(plan):
            source = sources[src] if k is None else sources[src].at[k]
            target = targets[name]
            if flip is not None:
                at = pl.multiple_of(at + count * (core if flip == 0 else 1 - core), count)
            target = target.at[pl.ds(at, count), pl.ds(col, width if k is not None else target.shape[1])]
            copies.append(
                pltpu.make_async_copy(source.at[pl.ds(start, count)], target, sems.at[index])
            )
        for copy in copies:
            copy.start()
        dacc[...] = jnp.zeros_like(dacc)
        macc[...] = jnp.zeros_like(macc)
        facc[...] = jnp.zeros_like(facc)
        for copy in copies:
            copy.wait()

    for i in range(seqs):

        @pl.when(step == i)
        def _(i=i):
            for j in range(parts):
                ob[j] = pieces[i * parts + j][...]

    def tiles(size):
        def decorate(body):
            def run(t, carry):
                body(pl.ds(pl.multiple_of(t * size, size), size), t * size)
                return carry

            lax.fori_loop(0, rows // size, run, 0)

        return decorate

    @tiles(32)
    def _(at, first):
        blocks = [ob[j, at, :].astype(F32) for j in range(parts)]
        mean = sum(jnp.sum(b, axis=1, keepdims=True) for b in blocks) / width
        blocks = [b - mean for b in blocks]
        var = sum(jnp.sum(b * b, axis=1, keepdims=True) for b in blocks) / width
        scale = lax.rsqrt(var + eps)
        mscale[at, :] = jnp.broadcast_to(scale, (32, 128))
        for j in range(parts):
            g = me ^ j
            unit = blocks[j] * scale
            munit[j, at, :] = unit
            anorm[g, at, :] = (unit * mgain[g] + mshift[g]).astype(BF16)

    mixed = sum(mm(anorm[g], wo[g * span : (g + 1) * span, :]) for g in range(parts))
    res[...] = x[...].astype(F32) + mixed + dvec[2:3, :]

    @tiles(32)
    def _(at, first):
        unit, scale = centred(res[at, :])
        runit[at, :] = unit
        rscale[at, :] = jnp.broadcast_to(scale, (32, 128))
        fnorm[at, :] = (unit * dvec[0:1, :] + dvec[1:2, :]).astype(BF16)

    for c in range(units // width):
        cols = slice(c * width, (c + 1) * width)
        pre[:, cols] = mm(fnorm[...], w1[:, cols])
    chunks = [slice(c, c + wide) for c in range(0, units, wide)]

    @tiles(tile)
    def _(at, first):
        total, square = 0.0, 0.0
        for c in chunks:
            v = pre[at, c] + fvec[1:2, c]
            below = 0.5 * (1.0 + lax.erf(v * 0.7071067811865476))
            a = v * below
            pre[at, c] = v
            cdf[at, c] = below
            act[at, c] = a
            total = total + a
        mean = jnp.sum(total, axis=1, keepdims=True) / units
        for c in chunks:
            d = act[at, c] - mean
            act[at, c] = d
            square = square + d * d
        scale = lax.rsqrt(jnp.sum(square, axis=1, keepdims=True) / units + eps)
        fscale[at, :] = jnp.broadcast_to(scale, (tile, 128))
        for c in chunks:
            unit = act[at, c] * scale
            act[at, c] = unit
            value = (unit * fvec[0:1, c] + fvec[2:3, c]).astype(BF16)
            hid[c.start // half][at, c.start % half : c.start % half + wide] = value

    out = res[...] + mm(hid[0][...], w2[:half, :]) + mm(hid[1][...], w2[half:, :]) + dvec[3:4, :]
    block_out[...] = live_only(out, 0, live).astype(BF16)
    kept = live_only(cot[...].astype(F32), 0, live)
    og[...] = kept.astype(BF16)
    dacc[24:32, :] += folded(kept)
    for c in range(units // width):
        cols = slice(c * width, (c + 1) * width)
        hg[:, cols] = mm_nt(og[...], w2[cols, :])

    @tiles(tile)
    def _(at, first):
        one, two = 0.0, 0.0
        for c in chunks:
            unit, grad = act[at, c], hg[at, c]
            both = grad * unit
            facc[0:8, c] += folded(both)
            facc[16:24, c] += folded(grad)
            gain = fvec[0:1, c]
            hg[at, c] = grad * gain
            one = one + grad * gain
            two = two + both * gain
        one = jnp.sum(one, axis=1, keepdims=True) / units
        two = jnp.sum(two, axis=1, keepdims=True) / units
        scale = fscale[at, 0:1]
        for c in chunks:
            v = pre[at, c]
            slope = cdf[at, c] + v * (jnp.exp(-0.5 * v * v) * 0.3989422804014327)
            grad = scale * (hg[at, c] - one - act[at, c] * two) * slope
            low = grad.astype(BF16)
            pg[c.start // width][at, c.start % width : c.start % width + wide] = low
            facc[8:16, c] += folded(low.astype(F32))

    fg = hg.at[:, 0:width]
    fg[...] = sum(
        mm_nt(pg[c][...], w1[:, c * width : (c + 1) * width]) for c in range(units // width)
    )

    @tiles(32)
    def _(at, first):
        grad, unit = fg[at, :], runit[at, :]
        dacc[0:8, :] += folded(grad * unit)
        dacc[8:16, :] += folded(grad)
        total = og[at, :].astype(F32) + norm_back(grad * dvec[0:1, :], unit, rscale[at, 0:1])
        resid_grad[at, :] = total
        branch[at, :] = total.astype(BF16)
        dacc[16:24, :] += folded(total)

    for g in range(parts):
        ngs[g] = mm_nt(branch[...], wo[g * span : (g + 1) * span, :])

    @tiles(32)
    def _(at, first):
        one, two, scaled = 0.0, 0.0, []
        for j in range(parts):
            g = me ^ j
            grad, unit = ngs[g, at, :], munit[j, at, :]
            macc[g, 0:8, :] += folded(grad * unit)
            macc[g, 8:16, :] += folded(grad)
            m = grad * mgain[g]
            one = one + jnp.sum(m, axis=1, keepdims=True)
            two = two + jnp.sum(m * unit, axis=1, keepdims=True)
            scaled.append(m)
        one, two, scale = one / width, two / width, mscale[at, 0:1]
        for j in range(parts):
            value = scale * (scaled[j] - one - munit[j, at, :] * two)
            ob[j, at, :] = value.astype(BF16)

    for i in range(seqs):

        @pl.when(step == i)
        def _(i=i):
            for j in range(parts):
                mds[i * parts + j][...] = ob[j]

    @pl.when(step == seqs - 1)
    def _():
        for r in range(4):
            dsum[r : r + 1, :] = jnp.sum(dacc[8 * r : 8 * r + 8, :], axis=0, keepdims=True)
        for r in range(3):
            fsum[r : r + 1, :] = jnp.sum(facc[8 * r : 8 * r + 8, :], axis=0, keepdims=True)
        for g in range(parts):
            for r in range(2):
                part = macc[g, 8 * r : 8 * r + 8, :]
                msum[g, r : r + 1, :] = jnp.sum(part, axis=0, keepdims=True)


def token_stage(info, plan, sources, pieces, x, cot, dvec, mgain, mshift, fvec):
    seqs, rows, width = x.shape
    parts, units = len(pieces[0]), fvec.shape[1]
    span = width // parts
    shape = jax.ShapeDtypeStruct
    whole = lambda *dims: pl.BlockSpec(dims, lambda i: (0,) * len(dims))
    by_seq = pl.BlockSpec((None, rows, width), lambda i: (i, 0, 0))
    by_rows = lambda cols: pl.BlockSpec((rows, cols), lambda i: (i, 0))
    n = seqs * rows
    outs = pl.pallas_call(
        functools.partial(token_kernel, plan, seqs, parts),
        grid=(seqs,),
        in_specs=[pl.BlockSpec(memory_space=pltpu.SMEM)]
        + [pl.BlockSpec(memory_space=pl.ANY)] * len(sources)
        + [whole(rows, span)] * (seqs * parts)
        + [
            by_seq,
            by_seq,
            whole(*dvec.shape),
            whole(*mgain.shape),
            whole(*mshift.shape),
            whole(*fvec.shape),
        ],
        out_specs=[by_seq, by_seq]
        + [by_rows(width)] * 3
        + [pl.BlockSpec((parts, rows, span), lambda i: (0, i, 0))]
        + [by_rows(units // 2)] * 2
        + [by_rows(width)] * 4
        + [whole(rows, span)] * (seqs * parts)
        + [whole(4, width), whole(parts, 2, span), whole(3, units)],
        out_shape=[shape((seqs, rows, width), BF16), shape((seqs, rows, width), F32)]
        + [shape((n, width), BF16)] * 3
        + [shape((parts, n, span), BF16)]
        + [shape((n, units // 2), BF16)] * 2
        + [shape((n, units // 4), BF16)] * 4
        + [shape((rows, span), BF16)] * (seqs * parts)
        + [shape((4, width), F32), shape((parts, 2, span), F32), shape((3, units), F32)],
        scratch_shapes=[
            pltpu.VMEM((width, width), BF16),
            pltpu.VMEM((width, units), BF16),
            pltpu.VMEM((units, width), BF16),
            pltpu.VMEM((parts, rows, span), BF16),
            pltpu.VMEM((parts, rows, span), F32),
            pltpu.VMEM((rows, 128), F32),
            pltpu.VMEM((rows, width), F32),
            pltpu.VMEM((rows, width), F32),
            pltpu.VMEM((rows, 128), F32),
        ]
        + [pltpu.VMEM((rows, units), F32)] * 4
        + [
            pltpu.VMEM((rows, 128), F32),
            pltpu.VMEM((parts, rows, span), F32),
            pltpu.VMEM((32, width), F32),
            pltpu.VMEM((parts, 16, span), F32),
            pltpu.VMEM((24, units), F32),
            pltpu.SemaphoreType.DMA((len(plan),)),
        ],
        cost_estimate=pl.CostEstimate(
            flops=2 * n * width * (4 * units + 2 * width),
            bytes_accessed=2 * width * (2 * units + width) + 2 * n * (4 * units + 12 * width),
            transcendentals=2 * n * units,
        ),
        compiler_params=pltpu.CompilerParams(vmem_limit_bytes=60 << 20),
        name="token_stage",
    )(info, *sources, *[p for group in pieces for p in group], x, cot, dvec, mgain, mshift, fvec)
    outs = list(outs)
    mds = outs[12 : 12 + seqs * parts]
    mds = [mds[i * parts : (i + 1) * parts] for i in range(seqs)]
    return outs[:6], outs[6:8], outs[8:12], mds, outs[12 + seqs * parts :]


def swap(values, axis, mask):
    count = lax.axis_size(axis)
    return lax.ppermute(values, axis, [(i, i ^ mask) for i in range(count)])


def pick(values, index, axis):
    return lax.dynamic_index_in_dim(values, index, axis, keepdims=False)


def after(values, others):
    return lax.optimization_barrier((values, others))[0]


def spread_blocks(block, axis):
    count, me = lax.axis_size(axis), lax.axis_index(axis)
    held = {0: block}
    bit = count // 2
    while bit:
        held |= {mask | bit: swap(part, axis, bit) for mask, part in held.items()}
        bit //= 2
    whole = jnp.zeros((count,) + block.shape, block.dtype)
    for mask, part in held.items():
        whole = lax.dynamic_update_index_in_dim(whole, part, me ^ mask, 0)
    return whole


def sum_blocks(blocks, axis):
    count, me = lax.axis_size(axis), lax.axis_index(axis)
    bit = 1
    while bit < count:
        pairs = blocks.reshape((blocks.shape[0] // 2, 2) + blocks.shape[1:])
        mine = (me // bit) % 2
        sent = swap(pick(pairs, 1 - mine, 1).astype(BF16), axis, bit)
        blocks = pick(pairs, mine, 1).astype(F32) + sent.astype(F32)
        bit *= 2
    return blocks[0]


def shards(
    activations,
    cotangent,
    lengths,
    w_qkv,
    w_out,
    w_fc1,
    w_fc2,
    d_gains,
    d_biases,
    ff_gain,
    ff_biases,
):
    seqs, rows, width = activations.shape
    parts, owners = lax.axis_size("seq"), lax.axis_size("fsdp")
    s, owner = lax.axis_index("seq"), lax.axis_index("fsdp")
    core = s % 2
    span = width // parts
    n = seqs * rows
    own_rows = w_qkv.shape[0]
    own_ff = w_fc2.shape[0]
    half_ff, half_rows = own_ff // 2, own_rows // 2
    ff_half = half_ff * owners
    quarter = own_ff // own_rows

    own_w = pick(w_qkv.reshape(own_rows, 3, parts, span), s, 2).reshape(own_rows, 3 * span)
    ff_small = jnp.concatenate([ff_gain[:, None], ff_biases], axis=1).T.reshape(
        3 * quarter, own_rows
    )
    small = jnp.concatenate([d_gains.T, d_biases.T, ff_small], axis=0)
    kinds = small.shape[0]
    small_rows = 32
    small = jnp.pad(small, ((0, small_rows - kinds), (0, 3 * span - own_rows)))
    block = jnp.concatenate([own_w, small], axis=0)
    first = spread_blocks(block, "fsdp")
    my_qkv = first[:, :own_rows].reshape(width, 3 * span)
    small = first[:, own_rows : own_rows + kinds, :own_rows].astype(F32)
    d_small = small[:, :10].transpose(1, 0, 2).reshape(10, width)
    gains, biases = d_small[:3], d_small[3:]
    ff_small = small[:, 10:].reshape(owners, 3, 2, half_ff)
    ff_small = jnp.concatenate(
        [pick(ff_small, core, 2), pick(ff_small, 1 - core, 2)], axis=0
    )
    ff_small = ff_small.reshape(2, owners, 3, half_ff).transpose(2, 0, 1, 3).reshape(3, 2 * ff_half)

    w_out, w_fc1, w_fc2 = after((w_out, w_fc1, w_fc2), block)
    fc1_half = pick(w_fc1.reshape(own_rows, owners, 2, half_ff), core, 2).reshape(own_rows, ff_half)
    columns = range(0, ff_half, width)
    rest = jnp.concatenate(
        [pick(w_out.reshape(2, half_rows, width), core, 0)]
        + [fc1_half[:, c : c + width] for c in columns]
        + [pick(w_fc2.reshape(2, half_ff, width), core, 0)],
        axis=0,
    )
    rest_rows = rest.shape[0]
    rest = lax.all_gather(rest, "fsdp", axis=0, tiled=False)

    qkv_bias = pick(
        jnp.stack([biases[1], jnp.zeros_like(biases[1]), biases[2]]).reshape(3, parts, span), s, 1
    ).reshape(1, 3 * span)
    x_parts, mixed_parts, kept = [], [], []
    for i in range(seqs):
        mine = activations[i]
        across = swap(mine, "seq", 2)
        x_parts.append([mine, swap(mine, "seq", 1), across, swap(across, "seq", 1)])
    for i in range(seqs):
        normed, saved, outs, lse = attend_forward(
            s, lengths[i], x_parts[i], my_qkv, gains[0:1], biases[0:1], qkv_bias
        )
        kept.append((normed, saved, lse))
        mixed_parts.append([outs[0]] + [swap(outs[j], "seq", j) for j in range(1, parts)])
    rest = after(rest, [lse for _, _, lse in kept])
    rest_other = swap(rest, "seq", 1)

    plan, sources = [], [rest, rest_other]
    if half_rows % 16 == 0 and half_ff % 16 == 0:
        for src in range(2):
            for k in range(owners):
                plan.append((src, k, 0, half_rows, "out", k * own_rows, src, 0))
                for at, c in enumerate(columns):
                    start = half_rows + at * own_rows
                    plan.append(
                        (src, k, start, own_rows, "fc1", k * own_rows, None, src * ff_half + c)
                    )
                start = rest_rows - half_ff
                plan.append(
                    (src, k, start, half_ff, "fc2", src * ff_half + k * half_ff, None, 0)
                )
    else:
        pair = [
            jnp.where(core == 0, rest, rest_other)[:, :half_rows],
            jnp.where(core == 0, rest_other, rest)[:, :half_rows],
        ]
        tail = rest_rows - half_ff
        blocks = [
            buf[:, half_rows + at * own_rows : half_rows + (at + 1) * own_rows].reshape(width, width)
            for buf in sources
            for at in range(len(columns))
        ]
        sources = [
            jnp.concatenate(pair, axis=1).reshape(width, width),
            jnp.concatenate(blocks, axis=1),
            jnp.concatenate([buf[:, tail:].reshape(ff_half, width) for buf in sources], axis=0),
        ]
        names = ("out", "fc1", "fc2")
        plan = [(i, None, 0, sources[i].shape[0], names[i], 0, None, 0) for i in range(3)]
    info = jnp.concatenate([lengths, jnp.stack([s, core]).astype(jnp.int32)])
    dvec = jnp.stack([gains[2], biases[5], biases[4], biases[6]])
    tokens = token_stage(
        info,
        plan,
        sources,
        mixed_parts,
        activations,
        cotangent,
        dvec,
        gains[1].reshape(parts, 1, span),
        biases[3].reshape(parts, 1, span),
        ff_small,
    )
    (block_out, resid_grad, fnorm, branch, og, anorm), hid, pg, mixed_grads, sums = tokens
    dsum, msum, fsum = sums

    grad_out = jnp.einsum("gnk,nd->gkd", anorm, branch, preferred_element_type=F32)
    grad_out = grad_out.reshape(owners, 2, half_rows, width)
    grads = []
    for src in range(2):
        pieces = [pick(grad_out, core if src == 0 else 1 - core, 1)]
        pieces += [
            mm_tn(fnorm, pg[2 * src + at]).reshape(owners, own_rows, width)
            for at in range(len(columns))
        ]
        pieces.append(mm_tn(hid[src], og).reshape(owners, half_ff, width))
        grads.append(jnp.concatenate([p.astype(BF16) for p in pieces], axis=1))
    rest_sum = grads[0].astype(F32) + swap(grads[1], "seq", 1).astype(F32)
    rest_sum = rest_sum.astype(BF16).reshape(owners * rest_rows, width)
    mixed_grads = after(mixed_grads, rest_sum)
    rest_sum = lax.psum_scatter(rest_sum, "fsdp", scatter_dimension=0, tiled=True)

    grad_own, summed, head_sums, unit_sums = 0.0, [], 0.0, 0.0
    for i in range(seqs):
        pieces = [mixed_grads[i][0]]
        pieces += [swap(mixed_grads[i][j], "seq", j) for j in range(1, parts)]
        normed, saved, lse = kept[i]
        dqkv, dns, sums, cols = attend_backward(
            s, lengths[i], x_parts[i], pieces, my_qkv, saved, lse
        )
        grad_own = grad_own + mm_tn(
            normed.reshape(parts * rows, width), dqkv.reshape(parts * rows, 3 * span)
        )
        unit_sums, head_sums = unit_sums + sums, head_sums + cols
        near = [swap(dns[j], "seq", 1).astype(F32) for j in (1, 3)]
        far = (dns[2].astype(F32) + near[1]).astype(BF16)
        summed.append(dns[0].astype(F32) + near[0] + swap(far, "seq", 2).astype(F32))
    first_grad = jnp.stack(summed)
    first_unit, first_scale = centred(activations.astype(F32))
    input_grad = resid_grad + norm_back(first_grad * gains[0], first_unit, first_scale)

    def head_columns(values):
        blank = jnp.zeros((parts, span), F32)
        return lax.dynamic_update_slice(blank, values[None], (s, 0)).reshape(width)

    small_grads = jnp.stack(
        [
            unit_sums[0],
            msum[:, 0].reshape(width),
            dsum[0],
            unit_sums[1],
            head_columns(head_sums[0, :span]),
            head_columns(head_sums[0, 2 * span :]),
            msum[:, 1].reshape(width),
            dsum[2],
            dsum[1],
            dsum[3],
        ]
    )
    feed_grads = fsum.reshape(3, 2, owners, half_ff)
    feed_grads = jnp.where(core == 0, feed_grads, feed_grads[:, ::-1])
    small_blocks = jnp.concatenate(
        [
            small_grads.reshape(10, owners, own_rows).transpose(1, 0, 2),
            feed_grads.transpose(2, 0, 1, 3).reshape(owners, 3 * quarter, own_rows),
        ],
        axis=1,
    )
    small_blocks = jnp.pad(
        small_blocks, ((0, 0), (0, small_rows - kinds), (0, 3 * span - own_rows))
    )
    first_blocks = jnp.concatenate(
        [grad_own.reshape(owners, own_rows, 3 * span), small_blocks], axis=1
    )
    first_sum = sum_blocks(first_blocks, "fsdp")
    group = [first_sum] + [swap(first_sum, "seq", j) for j in range(1, parts)]
    order = s ^ jnp.arange(parts)
    stacked = jnp.stack([g[:own_rows] for g in group])
    w_qkv_grad = jnp.take(stacked, order, axis=0).reshape(parts, own_rows, 3, span)
    w_qkv_grad = w_qkv_grad.transpose(1, 2, 0, 3).reshape(own_rows, 3 * width)
    small_sum = [g[own_rows : own_rows + kinds, :own_rows] for g in group]
    small_sum = (small_sum[0] + small_sum[1]) + (small_sum[2] + small_sum[3])
    feed_sum = small_sum[10:].reshape(3, own_ff)

    rest_sum = rest_sum.astype(F32) + swap(rest_sum, "seq", 2).astype(F32)
    other_sum = swap(rest_sum, "seq", 1)
    lower = jnp.where(core == 0, rest_sum, other_sum)
    upper = jnp.where(core == 0, other_sum, rest_sum)
    both = (lower, upper)
    w_out_grad = jnp.concatenate([p[:half_rows] for p in both], axis=0)
    fc1_sums = [
        jnp.concatenate(
            [
                p[half_rows + at * own_rows : half_rows + (at + 1) * own_rows]
                for at in range(len(columns))
            ],
            axis=1,
        ).reshape(own_rows, owners, 1, half_ff)
        for p in both
    ]
    w_fc1_grad = jnp.concatenate(fc1_sums, axis=2).reshape(own_rows, 2 * ff_half)
    w_fc2_grad = jnp.concatenate([p[rest_rows - half_ff :] for p in both], axis=0)
    return (
        block_out,
        input_grad,
        w_qkv_grad,
        w_out_grad,
        w_fc1_grad,
        w_fc2_grad,
        small_sum[:3].T,
        small_sum[3:10].T,
        feed_sum[0],
        feed_sum[1:].T,
    )


def solution(mesh):
    return jax.shard_map(
        shards,
        mesh=mesh,
        in_specs=(
            P("fsdp", "seq", None),
            P("fsdp", "seq", None),
            P("fsdp"),
            P("fsdp", None),
            P("fsdp", None),
            P("fsdp", None),
            P("fsdp", None),
            P("fsdp", None),
            P("fsdp", None),
            P("fsdp"),
            P("fsdp", None),
        ),
        out_specs=(
            P("fsdp", "seq", None),
            P("fsdp", "seq", None),
            P("fsdp", None),
            P("fsdp", None),
            P("fsdp", None),
            P("fsdp", None),
            P("fsdp", None),
            P("fsdp", None),
            P("fsdp"),
            P("fsdp", None),
        ),
        check_vma=False,
    )
```

```python
import functools

import jax
import jax.numpy as jnp
from jax import lax
from jax.experimental import pallas as pl
from jax.experimental.pallas import tpu as pltpu
from jax.sharding import PartitionSpec as P

H = 12
HD = 64
eps = 1e-05
F32 = jnp.float32
BF16 = jnp.bfloat16
NT = (((1,), (1,)), ((), ()))


def mm(left, right):
    return jnp.dot(left, right, preferred_element_type=F32)


def mm_nt(left, right):
    return lax.dot_general(left, right, NT, preferred_element_type=F32)


def mm_tn(left, right):
    return lax.dot_general(left, right, (((0,), (0,)), ((), ())), preferred_element_type=F32)


def centred(values):
    center = values - jnp.mean(values, axis=-1, keepdims=True)
    spread = jnp.mean(center * center, axis=-1, keepdims=True)
    scale = lax.rsqrt(spread + eps)
    return center * scale, scale


def norm_back(grad, unit, scale):
    return scale * (
        grad
        - jnp.mean(grad, axis=-1, keepdims=True)
        - unit * jnp.mean(grad * unit, axis=-1, keepdims=True)
    )


def key_mask(block, live_rows):
    rows = lax.broadcasted_iota(jnp.int32, block.shape, 0)
    return jnp.where(rows < live_rows, block, -1e30)


def attend_kernel(parts, heads, rows, info, *refs):
    xs = refs[:parts]
    w, gain, shift, bias = refs[parts : parts + 4]
    stored = refs[parts + 4 : parts + 9]
    outs = refs[parts + 9 : 2 * parts + 9]
    lse, nrm, q, k, v, kt, vt, ot, sems = refs[2 * parts + 9 :]
    me, live = info[0], info[1]
    span = heads * HD
    for j in range(parts):
        g = me ^ j
        at = pl.ds(pl.multiple_of(g * rows, rows), rows)
        unit, _ = centred(xs[j][...].astype(F32))
        normed = (unit * gain[...] + shift[...]).astype(BF16)
        nrm[j] = normed
        qkv = mm(normed, w[...]) + bias[...]
        for h in range(heads):
            cols = slice(h * HD, (h + 1) * HD)
            kk = qkv[:, span + h * HD : span + (h + 1) * HD]
            vv = qkv[:, 2 * span + h * HD : 2 * span + (h + 1) * HD]
            q[h, at, :] = (qkv[:, cols].astype(BF16).astype(F32) * 0.125).astype(BF16)
            k[h, at, :] = kk.astype(BF16)
            v[h, at, :] = vv.astype(BF16)
            kt[h, g] = kk.T.astype(BF16)
            vt[h, g] = vv.T.astype(BF16)
    copies = [
        pltpu.make_async_copy(source, target, sems.at[index])
        for index, (source, target) in enumerate(zip((nrm, q, k, v, kt), stored))
    ]
    for copy in copies:
        copy.start()

    def variant(count):
        def step(t, carry):
            h, j = t // parts, t % parts
            g = me ^ j

            @pl.when(g < count)
            def _():
                qb = q[h, pl.ds(pl.multiple_of(g * rows, rows), rows), :]
                scores = [
                    mm_nt(k[h, c * rows : (c + 1) * rows, :], qb) for c in range(count)
                ]
                scores[-1] = key_mask(scores[-1], live - (count - 1) * rows)
                top = functools.reduce(
                    jnp.maximum, [jnp.max(s, axis=0, keepdims=True) for s in scores]
                )
                total, mixed = 0.0, 0.0
                for c in range(count):
                    e = jnp.exp(scores[c] - top)
                    total = total + jnp.sum(e, axis=0, keepdims=True)
                    mixed = mixed + mm(vt[h, c], e.astype(BF16))
                ot[t] = mixed / total
                lse[t] = jnp.broadcast_to(top + jnp.log(total), (8, rows))

            @pl.when(g >= count)
            def _():
                ot[t] = jnp.zeros((HD, rows), F32)
                lse[t] = jnp.zeros((8, rows), F32)

            return carry

        lax.fori_loop(0, heads * parts, step, 0)

    blocks = (live + rows - 1) // rows
    for count in range(1, parts + 1):
        pl.when(blocks == count)(functools.partial(variant, count))
    for j in range(parts):
        stacked = jnp.concatenate([ot[h * parts + j] for h in range(heads)], axis=0)
        outs[j][...] = stacked.T.astype(BF16)
    for copy in copies:
        copy.wait()


def attend_forward(place, live, xs, w, gain, shift, bias):
    parts, (rows, width) = len(xs), xs[0].shape
    span = w.shape[1] // 3
    heads, full = span // HD, parts * rows
    shape = jax.ShapeDtypeStruct
    vmem = pl.BlockSpec(memory_space=pltpu.VMEM)
    kept = [(parts, rows, width)] + [(heads, full, HD)] * 3 + [(heads, parts, HD, rows)]
    outs = pl.pallas_call(
        functools.partial(attend_kernel, parts, heads, rows),
        in_specs=[pl.BlockSpec(memory_space=pltpu.SMEM)] + [vmem] * (parts + 4),
        out_specs=[pl.BlockSpec(memory_space=pltpu.HBM)] * 5 + [vmem] * (parts + 1),
        out_shape=[shape(dims, BF16) for dims in kept]
        + [shape((rows, span), BF16)] * parts
        + [shape((heads * parts, 8, rows), F32)],
        scratch_shapes=[pltpu.VMEM(dims, BF16) for dims in kept]
        + [
            pltpu.VMEM((heads, parts, HD, rows), BF16),
            pltpu.VMEM((heads * parts, HD, rows), F32),
            pltpu.SemaphoreType.DMA((5,)),
        ],
        cost_estimate=pl.CostEstimate(
            flops=2 * full * width * 3 * span + 4 * full * full * span,
            bytes_accessed=2 * (2 * full * width + width * 3 * span + 6 * full * span),
            transcendentals=heads * full * full,
        ),
        compiler_params=pltpu.CompilerParams(vmem_limit_bytes=48 << 20),
        name="attend_forward",
    )(jnp.stack([place, live]), *xs, w, gain, shift, bias)
    return outs[0], outs[1:5], outs[5 : 5 + parts], outs[5 + parts]


def attend_back_kernel(parts, heads, rows, info, *refs):
    xs, grads = refs[:parts], refs[parts : 2 * parts]
    w, q, k, v, kt, lse = refs[2 * parts : 2 * parts + 6]
    dqkv = refs[2 * parts + 6]
    dns = refs[2 * parts + 7 : 3 * parts + 7]
    sums, cols = refs[3 * parts + 7 : 3 * parts + 9]
    do, dk, dv, dqt = refs[3 * parts + 9 :]
    me, live = info[0], info[1]
    for j in range(parts):
        block = grads[j][...].astype(F32)
        for h in range(heads):
            do[h * parts + j] = block[:, h * HD : (h + 1) * HD].astype(BF16)
    dk[...] = jnp.zeros_like(dk)
    dv[...] = jnp.zeros_like(dv)

    def variant(count):
        def step(t, carry):
            h, j = t // parts, t % parts
            g = me ^ j

            @pl.when(g < count)
            def _():
                qb = q[h, pl.ds(pl.multiple_of(g * rows, rows), rows), :]
                dob = do[t]
                shift = lse[t][0:1, :]
                probs, dps, inner = [], [], 0.0
                for c in range(count):
                    span = slice(c * rows, (c + 1) * rows)
                    s = mm_nt(k[h, span, :], qb)
                    if c == count - 1:
                        s = key_mask(s, live - c * rows)
                    p = jnp.exp(s - shift)
                    dp = mm_nt(v[h, span, :], dob)
                    inner = inner + jnp.sum(p * dp, axis=0, keepdims=True)
                    dv[h, c] += mm(p.astype(BF16), dob)
                    probs.append(p)
                    dps.append(dp)
                dq = 0.0
                for c in range(count):
                    ds = (probs[c] * (dps[c] - inner)).astype(BF16)
                    dk[h, c] += mm(ds, qb)
                    dq = dq + mm(kt[h, c], ds)
                dqt[t] = dq * 0.125

            @pl.when(g >= count)
            def _():
                dqt[t] = jnp.zeros((HD, rows), F32)

            return carry

        lax.fori_loop(0, heads * parts, step, 0)

    blocks = (live + rows - 1) // rows
    for count in range(1, parts + 1):
        pl.when(blocks == count)(functools.partial(variant, count))
    shift_sum, gain_sum, col_sum = 0.0, 0.0, 0.0
    for j in range(parts):
        g = me ^ j
        dq = jnp.concatenate([dqt[h * parts + j] for h in range(heads)], axis=0).T
        pieces = [dq] + [dk[h, g] for h in range(heads)] + [dv[h, g] for h in range(heads)]
        block = jnp.concatenate(pieces, axis=1).astype(BF16)
        dqkv[j] = block
        col_sum = col_sum + jnp.sum(block.astype(F32), axis=0, keepdims=True)
        dn = mm_nt(block, w[...])
        unit, _ = centred(xs[j][...].astype(F32))
        shift_sum = shift_sum + jnp.sum(dn, axis=0, keepdims=True)
        gain_sum = gain_sum + jnp.sum(dn * unit, axis=0, keepdims=True)
        dns[j][...] = dn.astype(BF16)
    sums[0:1, :] = gain_sum
    sums[1:2, :] = shift_sum
    cols[0:1, :] = col_sum


def attend_backward(place, live, xs, grads, w, saved, lse):
    parts, (rows, width) = len(xs), xs[0].shape
    span = w.shape[1] // 3
    heads, full = span // HD, parts * rows
    shape = jax.ShapeDtypeStruct
    vmem = pl.BlockSpec(memory_space=pltpu.VMEM)
    outs = pl.pallas_call(
        functools.partial(attend_back_kernel, parts, heads, rows),
        in_specs=[pl.BlockSpec(memory_space=pltpu.SMEM)] + [vmem] * (2 * parts + 6),
        out_specs=[vmem] * (parts + 3),
        out_shape=[shape((parts, rows, 3 * span), BF16)]
        + [shape((rows, width), BF16)] * parts
        + [shape((2, width), F32), shape((1, 3 * span), F32)],
        scratch_shapes=[
            pltpu.VMEM((heads * parts, rows, HD), BF16),
            pltpu.VMEM((heads, parts, rows, HD), F32),
            pltpu.VMEM((heads, parts, rows, HD), F32),
            pltpu.VMEM((heads * parts, HD, rows), F32),
        ],
        cost_estimate=pl.CostEstimate(
            flops=2 * full * width * 3 * span + 10 * full * full * span,
            bytes_accessed=2 * (3 * full * width + width * 3 * span + 9 * full * span),
            transcendentals=heads * full * full,
        ),
        compiler_params=pltpu.CompilerParams(vmem_limit_bytes=48 << 20),
        name="attend_backward",
    )(jnp.stack([place, live]), *xs, *grads, w, *saved, lse)
    return outs[0], outs[1 : 1 + parts], outs[1 + parts], outs[2 + parts]


def live_only(values, first, live):
    rows = first + lax.broadcasted_iota(jnp.int32, values.shape, 0)
    return jnp.where(rows < live, values, jnp.zeros_like(values))


def folded(values):
    return functools.reduce(
        jnp.add, [values[r : r + 8] for r in range(0, values.shape[0], 8)]
    )


def token_kernel(plan, seqs, parts, info, *refs):
    refs = list(refs)
    take = lambda count: [refs.pop(0) for _ in range(count)]
    sources = take(max(p[0] for p in plan) + 1)
    pieces = take(seqs * parts)
    x, cot, dvec, mgain, mshift, fvec = take(6)
    block_out, resid_grad, fnorm, branch, og, anorm = take(6)
    hid, pg = take(2)
    mds = take(seqs * parts)
    dsum, msum, fsum = take(3)
    wo, w1, w2, ob, munit, mscale, res, runit, rscale = take(9)
    pre, cdf, act, hg, fscale, ngs, dacc, macc, facc, sems = take(10)
    step = pl.program_id(0)
    me, core = info[seqs], info[seqs + 1]
    live = info[step] - me * x.shape[0]
    rows, width = x.shape
    span, units = width // parts, pre.shape[1]
    tile, wide = 16, 384
    quarters = units // width

    def place(quarter):
        turned = quarter + quarters // 2 * core
        return jnp.where(turned >= quarters, turned - quarters, turned)

    targets = {"out": wo, "fc1": w1, "fc2": w2}

    @pl.when(step == 0)
    def _():
        copies = []
        for index, (src, k, start, count, name, at, at_step, col, col_step) in enumerate(plan):
            source = sources[src] if k is None else sources[src].at[k]
            target = targets[name]
            turn = core if src == 0 else 1 - core
            if at_step:
                at = pl.multiple_of(at + at_step * turn, 16)
            if col_step:
                col = pl.multiple_of(col + col_step * turn, 128)
            target = target.at[pl.ds(at, count), pl.ds(col, source.shape[1])]
            copies.append(
                pltpu.make_async_copy(source.at[pl.ds(start, count)], target, sems.at[index])
            )
        for copy in copies:
            copy.start()
        dacc[...] = jnp.zeros_like(dacc)
        macc[...] = jnp.zeros_like(macc)
        facc[...] = jnp.zeros_like(facc)
        for copy in copies:
            copy.wait()

    for i in range(seqs):

        @pl.when(step == i)
        def _(i=i):
            for j in range(parts):
                ob[j] = pieces[i * parts + j][...]

    def tiles(size):
        def decorate(body):
            def run(t, carry):
                body(pl.ds(pl.multiple_of(t * size, size), size), t * size)
                return carry

            lax.fori_loop(0, rows // size, run, 0)

        return decorate

    @tiles(32)
    def _(at, first):
        blocks = [ob[j, at, :].astype(F32) for j in range(parts)]
        mean = sum(jnp.sum(b, axis=1, keepdims=True) for b in blocks) / width
        blocks = [b - mean for b in blocks]
        var = sum(jnp.sum(b * b, axis=1, keepdims=True) for b in blocks) / width
        scale = lax.rsqrt(var + eps)
        mscale[at, :] = jnp.broadcast_to(scale, (32, 128))
        for j in range(parts):
            g = me ^ j
            unit = blocks[j] * scale
            munit[j, at, :] = unit
            anorm[g, at, :] = (unit * mgain[g] + mshift[g]).astype(BF16)

    mixed = sum(mm(anorm[g], wo[g * span : (g + 1) * span, :]) for g in range(parts))
    res[...] = x[...].astype(F32) + mixed + dvec[2:3, :]

    @tiles(32)
    def _(at, first):
        unit, scale = centred(res[at, :])
        runit[at, :] = unit
        rscale[at, :] = jnp.broadcast_to(scale, (32, 128))
        fnorm[at, :] = (unit * dvec[0:1, :] + dvec[1:2, :]).astype(BF16)

    for c in range(units // width):
        cols = slice(c * width, (c + 1) * width)
        pre[:, cols] = mm(fnorm[...], w1[:, cols])
    chunks = [slice(c, c + wide) for c in range(0, units, wide)]

    @tiles(tile)
    def _(at, first):
        total, square = 0.0, 0.0
        for c in chunks:
            v = pre[at, c] + fvec[1:2, c]
            below = 0.5 * (1.0 + lax.erf(v * 0.7071067811865476))
            a = v * below
            pre[at, c] = v
            cdf[at, c] = below
            act[at, c] = a
            total = total + a
        mean = jnp.sum(total, axis=1, keepdims=True) / units
        for c in chunks:
            d = act[at, c] - mean
            act[at, c] = d
            square = square + d * d
        scale = lax.rsqrt(jnp.sum(square, axis=1, keepdims=True) / units + eps)
        fscale[at, :] = jnp.broadcast_to(scale, (tile, 128))
        for c in chunks:
            unit = act[at, c] * scale
            act[at, c] = unit
            value = (unit * fvec[0:1, c] + fvec[2:3, c]).astype(BF16)
            hid[at, c] = value

    out = res[...] + mm(hid[...], w2[...]) + dvec[3:4, :]
    block_out[...] = live_only(out, 0, live).astype(BF16)
    kept = live_only(cot[...].astype(F32), 0, live)
    og[...] = kept.astype(BF16)
    dacc[24:32, :] += folded(kept)
    for c in range(units // width):
        cols = slice(c * width, (c + 1) * width)
        hg[:, cols] = mm_nt(og[...], w2[cols, :])

    @tiles(tile)
    def _(at, first):
        one, two = 0.0, 0.0
        for c in chunks:
            unit, grad = act[at, c], hg[at, c]
            both = grad * unit
            facc[0:8, c] += folded(both)
            facc[16:24, c] += folded(grad)
            gain = fvec[0:1, c]
            hg[at, c] = grad * gain
            one = one + grad * gain
            two = two + both * gain
        one = jnp.sum(one, axis=1, keepdims=True) / units
        two = jnp.sum(two, axis=1, keepdims=True) / units
        scale = fscale[at, 0:1]
        for c in chunks:
            v = pre[at, c]
            slope = cdf[at, c] + v * (jnp.exp(-0.5 * v * v) * 0.3989422804014327)
            grad = scale * (hg[at, c] - one - act[at, c] * two) * slope
            low = grad.astype(BF16)
            pg[place(c.start // width), at, c.start % width : c.start % width + wide] = low
            facc[8:16, c] += folded(low.astype(F32))

    fg = hg.at[:, 0:width]
    fg[...] = sum(
        mm_nt(pg[place(c)], w1[:, c * width : (c + 1) * width]) for c in range(units // width)
    )

    @tiles(32)
    def _(at, first):
        grad, unit = fg[at, :], runit[at, :]
        dacc[0:8, :] += folded(grad * unit)
        dacc[8:16, :] += folded(grad)
        total = og[at, :].astype(F32) + norm_back(grad * dvec[0:1, :], unit, rscale[at, 0:1])
        resid_grad[at, :] = total
        branch[at, :] = total.astype(BF16)
        dacc[16:24, :] += folded(total)

    for g in range(parts):
        ngs[g] = mm_nt(branch[...], wo[g * span : (g + 1) * span, :])

    @tiles(32)
    def _(at, first):
        one, two, scaled = 0.0, 0.0, []
        for j in range(parts):
            g = me ^ j
            grad, unit = ngs[g, at, :], munit[j, at, :]
            macc[g, 0:8, :] += folded(grad * unit)
            macc[g, 8:16, :] += folded(grad)
            m = grad * mgain[g]
            one = one + jnp.sum(m, axis=1, keepdims=True)
            two = two + jnp.sum(m * unit, axis=1, keepdims=True)
            scaled.append(m)
        one, two, scale = one / width, two / width, mscale[at, 0:1]
        for j in range(parts):
            value = scale * (scaled[j] - one - munit[j, at, :] * two)
            ob[j, at, :] = value.astype(BF16)

    for i in range(seqs):

        @pl.when(step == i)
        def _(i=i):
            for j in range(parts):
                mds[i * parts + j][...] = ob[j]

    @pl.when(step == seqs - 1)
    def _():
        for r in range(4):
            dsum[r : r + 1, :] = jnp.sum(dacc[8 * r : 8 * r + 8, :], axis=0, keepdims=True)
        for r in range(3):
            fsum[r : r + 1, :] = jnp.sum(facc[8 * r : 8 * r + 8, :], axis=0, keepdims=True)
        for g in range(parts):
            for r in range(2):
                part = macc[g, 8 * r : 8 * r + 8, :]
                msum[g, r : r + 1, :] = jnp.sum(part, axis=0, keepdims=True)


def token_stage(info, plan, sources, pieces, x, cot, dvec, mgain, mshift, fvec):
    seqs, rows, width = x.shape
    parts, units = len(pieces[0]), fvec.shape[1]
    span = width // parts
    shape = jax.ShapeDtypeStruct
    whole = lambda *dims: pl.BlockSpec(dims, lambda i: (0,) * len(dims))
    by_seq = pl.BlockSpec((None, rows, width), lambda i: (i, 0, 0))
    by_rows = lambda cols: pl.BlockSpec((rows, cols), lambda i: (i, 0))
    n = seqs * rows
    outs = pl.pallas_call(
        functools.partial(token_kernel, plan, seqs, parts),
        grid=(seqs,),
        in_specs=[pl.BlockSpec(memory_space=pltpu.SMEM)]
        + [pl.BlockSpec(memory_space=pl.ANY)] * len(sources)
        + [whole(rows, span)] * (seqs * parts)
        + [
            by_seq,
            by_seq,
            whole(*dvec.shape),
            whole(*mgain.shape),
            whole(*mshift.shape),
            whole(*fvec.shape),
        ],
        out_specs=[by_seq, by_seq]
        + [by_rows(width)] * 3
        + [pl.BlockSpec((parts, rows, span), lambda i: (0, i, 0))]
        + [by_rows(units)]
        + [pl.BlockSpec((units // width, rows, width), lambda i: (0, i, 0))]
        + [whole(rows, span)] * (seqs * parts)
        + [whole(4, width), whole(parts, 2, span), whole(3, units)],
        out_shape=[shape((seqs, rows, width), BF16), shape((seqs, rows, width), F32)]
        + [shape((n, width), BF16)] * 3
        + [shape((parts, n, span), BF16)]
        + [shape((n, units), BF16), shape((units // width, n, width), BF16)]
        + [shape((rows, span), BF16)] * (seqs * parts)
        + [shape((4, width), F32), shape((parts, 2, span), F32), shape((3, units), F32)],
        scratch_shapes=[
            pltpu.VMEM((width, width), BF16),
            pltpu.VMEM((width, units), BF16),
            pltpu.VMEM((units, width), BF16),
            pltpu.VMEM((parts, rows, span), BF16),
            pltpu.VMEM((parts, rows, span), F32),
            pltpu.VMEM((rows, 128), F32),
            pltpu.VMEM((rows, width), F32),
            pltpu.VMEM((rows, width), F32),
            pltpu.VMEM((rows, 128), F32),
        ]
        + [pltpu.VMEM((rows, units), F32)] * 4
        + [
            pltpu.VMEM((rows, 128), F32),
            pltpu.VMEM((parts, rows, span), F32),
            pltpu.VMEM((32, width), F32),
            pltpu.VMEM((parts, 16, span), F32),
            pltpu.VMEM((24, units), F32),
            pltpu.SemaphoreType.DMA((len(plan),)),
        ],
        cost_estimate=pl.CostEstimate(
            flops=2 * n * width * (4 * units + 2 * width),
            bytes_accessed=2 * width * (2 * units + width) + 2 * n * (4 * units + 12 * width),
            transcendentals=2 * n * units,
        ),
        compiler_params=pltpu.CompilerParams(vmem_limit_bytes=60 << 20),
        name="token_stage",
    )(info, *sources, *[p for group in pieces for p in group], x, cot, dvec, mgain, mshift, fvec)
    outs = list(outs)
    mds = outs[8 : 8 + seqs * parts]
    mds = [mds[i * parts : (i + 1) * parts] for i in range(seqs)]
    return outs[:6], outs[6], outs[7], mds, outs[8 + seqs * parts :]


def swap(values, axis, mask):
    count = lax.axis_size(axis)
    return lax.ppermute(values, axis, [(i, i ^ mask) for i in range(count)])


def pick(values, index, axis):
    return lax.dynamic_index_in_dim(values, index, axis, keepdims=False)


def after(values, others):
    return lax.optimization_barrier((values, others))[0]


def spread_blocks(block, axis):
    count, me = lax.axis_size(axis), lax.axis_index(axis)
    held = {0: block}
    bit = count // 2
    while bit:
        held |= {mask | bit: swap(part, axis, bit) for mask, part in held.items()}
        bit //= 2
    whole = jnp.zeros((count,) + block.shape, block.dtype)
    for mask, part in held.items():
        whole = lax.dynamic_update_index_in_dim(whole, part, me ^ mask, 0)
    return whole


def sum_blocks(blocks, axis, kind):
    count, me = lax.axis_size(axis), lax.axis_index(axis)
    bit = 1
    while bit < count:
        pairs = blocks.reshape((blocks.shape[0] // 2, 2) + blocks.shape[1:])
        mine = (me // bit) % 2
        sent = swap(pick(pairs, 1 - mine, 1).astype(kind), axis, bit)
        blocks = pick(pairs, mine, 1).astype(F32) + sent.astype(F32)
        bit *= 2
    return blocks[0]


def shards(
    activations,
    cotangent,
    lengths,
    w_qkv,
    w_out,
    w_fc1,
    w_fc2,
    d_gains,
    d_biases,
    ff_gain,
    ff_biases,
):
    seqs, rows, width = activations.shape
    parts, owners = lax.axis_size("seq"), lax.axis_size("fsdp")
    s, owner = lax.axis_index("seq"), lax.axis_index("fsdp")
    core = s % 2
    span = width // parts
    n = seqs * rows
    own_rows = w_qkv.shape[0]
    own_ff = w_fc2.shape[0]
    half_ff, half_rows = own_ff // 2, own_rows // 2
    ff_half = half_ff * owners
    quarter = own_ff // own_rows

    own_w = pick(w_qkv.reshape(own_rows, 3, parts, span), s, 2).reshape(own_rows, 3 * span)
    ff_small = jnp.concatenate([ff_gain[:, None], ff_biases], axis=1).T.reshape(
        3 * quarter, own_rows
    )
    small = jnp.concatenate([d_gains.T, d_biases.T, ff_small], axis=0)
    kinds = small.shape[0]
    small_rows = 32
    small = jnp.pad(small, ((0, small_rows - kinds), (0, 3 * span - own_rows)))
    block = jnp.concatenate([own_w, small], axis=0)
    first = spread_blocks(block, "fsdp")
    my_qkv = first[:, :own_rows].reshape(width, 3 * span)
    small = first[:, own_rows : own_rows + kinds, :own_rows].astype(F32)
    d_small = small[:, :10].transpose(1, 0, 2).reshape(10, width)
    gains, biases = d_small[:3], d_small[3:]
    ff_small = small[:, 10:].reshape(owners, 3, own_ff).transpose(1, 0, 2).reshape(3, 2 * ff_half)

    w_out, w_fc1, w_fc2 = after((w_out, w_fc1, w_fc2), block)
    fc1_half = lax.dynamic_slice(w_fc1, (0, core * ff_half), (own_rows, ff_half))
    columns = range(0, ff_half, width)
    rest = jnp.concatenate(
        [pick(w_out.reshape(2, half_rows, width), core, 0)]
        + [fc1_half[:, c : c + width] for c in columns]
        + [pick(w_fc2.reshape(2, half_ff, width), core, 0)],
        axis=0,
    )
    rest_rows = rest.shape[0]
    rest = lax.all_gather(rest, "fsdp", axis=0, tiled=False)

    qkv_bias = pick(
        jnp.stack([biases[1], jnp.zeros_like(biases[1]), biases[2]]).reshape(3, parts, span), s, 1
    ).reshape(1, 3 * span)
    x_parts, mixed_parts, kept = [], [], []
    for i in range(seqs):
        mine = activations[i]
        across = swap(mine, "seq", 2)
        x_parts.append([mine, swap(mine, "seq", 1), across, swap(across, "seq", 1)])
    for i in range(seqs):
        if i > 0:
            x_parts[i] = after(x_parts[i], [kept[i - 1][2], mixed_parts[:-1]])
        normed, saved, outs, lse = attend_forward(
            s, lengths[i], x_parts[i], my_qkv, gains[0:1], biases[0:1], qkv_bias
        )
        kept.append((normed, saved, lse))
        mixed_parts.append([outs[0]] + [swap(outs[j], "seq", j) for j in range(1, parts)])
    rest = after(rest, [lse for _, _, lse in kept])
    rest_other = swap(rest, "seq", 1)

    plan, sources = [], [rest, rest_other]
    if half_rows % 16 == 0 and half_ff % 16 == 0:
        for src in range(2):
            for k in range(owners):
                plan.append((src, k, 0, half_rows, "out", k * own_rows, half_rows, 0, 0))
                for at, c in enumerate(columns):
                    start = half_rows + at * own_rows
                    plan.append((src, k, start, own_rows, "fc1", k * own_rows, 0, c, ff_half))
                start = rest_rows - half_ff
                plan.append((src, k, start, half_ff, "fc2", k * own_ff, half_ff, 0, 0))
    else:
        pair = [jnp.where(core == 0, rest, rest_other), jnp.where(core == 0, rest_other, rest)]
        blocks = [
            buf[:, half_rows + at * own_rows : half_rows + (at + 1) * own_rows].reshape(width, width)
            for buf in pair
            for at in range(len(columns))
        ]
        sources = [
            jnp.concatenate([buf[:, :half_rows] for buf in pair], axis=1).reshape(width, width),
            jnp.concatenate(blocks, axis=1),
            jnp.concatenate([buf[:, rest_rows - half_ff :] for buf in pair], axis=1).reshape(
                2 * ff_half, width
            ),
        ]
        names = ("out", "fc1", "fc2")
        plan = [(i, None, 0, sources[i].shape[0], names[i], 0, 0, 0, 0) for i in range(3)]
    info = jnp.concatenate([lengths, jnp.stack([s, core]).astype(jnp.int32)])
    dvec = jnp.stack([gains[2], biases[5], biases[4], biases[6]])
    tokens = token_stage(
        info,
        plan,
        sources,
        mixed_parts,
        activations,
        cotangent,
        dvec,
        gains[1].reshape(parts, 1, span),
        biases[3].reshape(parts, 1, span),
        ff_small,
    )
    (block_out, resid_grad, fnorm, branch, og, anorm), hid, pg, mixed_grads, sums = tokens
    dsum, msum, fsum = sums

    grad_out = jnp.einsum("gnk,nd->gkd", anorm, branch, preferred_element_type=F32)
    grad_out = grad_out.reshape(owners, 2, half_rows, width)
    grad_fc2 = mm_tn(hid, og).reshape(owners, 2, half_ff, width)
    grads = []
    for src in range(2):
        turn = core if src == 0 else 1 - core
        pieces = [pick(grad_out, turn, 1)]
        pieces += [
            mm_tn(fnorm, pg[len(columns) * src + at]).reshape(owners, own_rows, width)
            for at in range(len(columns))
        ]
        pieces.append(pick(grad_fc2, turn, 1))
        grads.append(jnp.concatenate([p.astype(BF16) for p in pieces], axis=1))
    rest_sum = grads[0].astype(F32) + swap(grads[1], "seq", 1).astype(F32)
    rest_sum = rest_sum.astype(BF16).reshape(owners * rest_rows, width)
    mixed_grads = [[g[0]] + [swap(g[j], "seq", j) for j in range(1, parts)] for g in mixed_grads]
    mixed_grads[0], rest_sum = lax.optimization_barrier((mixed_grads[0], rest_sum))
    rest_sum = lax.psum_scatter(rest_sum, "fsdp", scatter_dimension=0, tiled=True)

    grad_own, summed, head_sums, unit_sums, near = 0.0, [], 0.0, 0.0, []
    for i in range(seqs):
        pieces = mixed_grads[i]
        if i > 0:
            pieces = after(pieces, [sums, near[:-1]])
        normed, saved, lse = kept[i]
        dqkv, dns, sums, cols = attend_backward(
            s, lengths[i], x_parts[i], pieces, my_qkv, saved, lse
        )
        grad_own = grad_own + mm_tn(
            normed.reshape(parts * rows, width), dqkv.reshape(parts * rows, 3 * span)
        )
        unit_sums, head_sums = unit_sums + sums, head_sums + cols
        near.append([swap(dns[j], "seq", 1) for j in (1, 3)])
        far = (dns[2].astype(F32) + near[i][1].astype(F32)).astype(BF16)
        far = swap(far, "seq", 2).astype(F32)
        summed.append(dns[0].astype(F32) + near[i][0].astype(F32) + far)
    first_grad = jnp.stack(summed)
    first_unit, first_scale = centred(activations.astype(F32))
    input_grad = resid_grad + norm_back(first_grad * gains[0], first_unit, first_scale)

    def head_columns(values):
        blank = jnp.zeros((parts, span), F32)
        return lax.dynamic_update_slice(blank, values[None], (s, 0)).reshape(width)

    small_grads = jnp.stack(
        [
            unit_sums[0],
            msum[:, 0].reshape(width),
            dsum[0],
            unit_sums[1],
            head_columns(head_sums[0, :span]),
            head_columns(head_sums[0, 2 * span :]),
            msum[:, 1].reshape(width),
            dsum[2],
            dsum[1],
            dsum[3],
        ]
    )
    feed_grads = fsum.reshape(3, owners, quarter, own_rows)
    small_blocks = jnp.concatenate(
        [
            small_grads.reshape(10, owners, own_rows).transpose(1, 0, 2),
            feed_grads.transpose(1, 0, 2, 3).reshape(owners, 3 * quarter, own_rows),
        ],
        axis=1,
    )
    small_blocks = jnp.pad(small_blocks, ((0, 0), (0, small_rows - kinds), (0, 0)))
    small_sum = sum_blocks(small_blocks, "fsdp", F32)
    own_sum = sum_blocks(grad_own.reshape(owners, own_rows, 3 * span), "fsdp", BF16).astype(BF16)
    rest_sum = rest_sum.astype(F32) + swap(rest_sum, "seq", 2).astype(F32)
    own_sum = after(own_sum, rest_sum)
    small_sum = [small_sum] + [swap(small_sum, "seq", j) for j in range(1, parts)]
    small_sum = (small_sum[0] + small_sum[1]) + (small_sum[2] + small_sum[3])
    feed_sum = small_sum[10:kinds].reshape(3, own_ff)
    group = jnp.stack([own_sum] + [swap(own_sum, "seq", j) for j in range(1, parts)])
    w_qkv_grad = jnp.concatenate(
        [
            pick(group, s ^ g, 0)[:, p * span : (p + 1) * span]
            for p in range(3)
            for g in range(parts)
        ],
        axis=1,
    ).astype(F32)

    other_sum = swap(rest_sum, "seq", 1)
    pair = [
        jnp.where(core == 0, rest_sum, other_sum),
        jnp.where(core == 0, other_sum, rest_sum),
    ]
    w_out_grad = jnp.concatenate([p[:half_rows] for p in pair], axis=0)
    w_fc1_grad = jnp.concatenate(
        [
            p[half_rows + at * own_rows : half_rows + (at + 1) * own_rows]
            for p in pair
            for at in range(len(columns))
        ],
        axis=1,
    )
    w_fc2_grad = jnp.concatenate([p[rest_rows - half_ff :] for p in pair], axis=0)
    return (
        block_out,
        input_grad,
        w_qkv_grad,
        w_out_grad,
        w_fc1_grad,
        w_fc2_grad,
        small_sum[:3].T,
        small_sum[3:10].T,
        feed_sum[0],
        feed_sum[1:].T,
    )


def solution(mesh):
    return jax.shard_map(
        shards,
        mesh=mesh,
        in_specs=(
            P("fsdp", "seq", None),
            P("fsdp", "seq", None),
            P("fsdp"),
            P("fsdp", None),
            P("fsdp", None),
            P("fsdp", None),
            P("fsdp", None),
            P("fsdp", None),
            P("fsdp", None),
            P("fsdp"),
            P("fsdp", None),
        ),
        out_specs=(
            P("fsdp", "seq", None),
            P("fsdp", "seq", None),
            P("fsdp", None),
            P("fsdp", None),
            P("fsdp", None),
            P("fsdp", None),
            P("fsdp", None),
            P("fsdp", None),
            P("fsdp"),
            P("fsdp", None),
        ),
        check_vma=False,
    )
```

```python
import functools

import jax
import jax.numpy as jnp
from jax import lax
from jax.experimental import pallas as pl
from jax.experimental.pallas import tpu as pltpu
from jax.sharding import PartitionSpec as P


HD = 64
eps = 1e-05
F32 = jnp.float32
BF16 = jnp.bfloat16
NT = (((1,), (1,)), ((), ()))


def mm(left, right):
    return jnp.dot(left, right, preferred_element_type=F32)


def mm_nt(left, right):
    return lax.dot_general(left, right, NT, preferred_element_type=F32)


def mm_tn(left, right):
    return lax.dot_general(left, right, (((0,), (0,)), ((), ())), preferred_element_type=F32)


def centred(values):
    center = values - jnp.mean(values, axis=-1, keepdims=True)
    spread = jnp.mean(center * center, axis=-1, keepdims=True)
    scale = lax.rsqrt(spread + eps)
    return center * scale, scale


def norm_back(grad, unit, scale):
    return scale * (
        grad
        - jnp.mean(grad, axis=-1, keepdims=True)
        - unit * jnp.mean(grad * unit, axis=-1, keepdims=True)
    )


def key_mask(block, live_rows):
    rows = lax.broadcasted_iota(jnp.int32, block.shape, 0)
    return jnp.where(rows < live_rows, block, -1e30)


def attend_kernel(parts, heads, rows, info, *refs):
    xs = refs[:parts]
    w, gain, shift, bias = refs[parts : parts + 4]
    stored = refs[parts + 4 : parts + 9]
    outs = refs[parts + 9 : 2 * parts + 9]
    lse, nrm, q, k, v, kt, vt, ot, sems = refs[2 * parts + 9 :]
    me, live = info[0], info[1]
    span = heads * HD
    for j in range(parts):
        g = me ^ j
        at = pl.ds(pl.multiple_of(g * rows, rows), rows)
        unit, _ = centred(xs[j][...].astype(F32))
        normed = (unit * gain[...] + shift[...]).astype(BF16)
        nrm[j] = normed
        qkv = mm(normed, w[...]) + bias[...]
        for h in range(heads):
            cols = slice(h * HD, (h + 1) * HD)
            kk = qkv[:, span + h * HD : span + (h + 1) * HD]
            vv = qkv[:, 2 * span + h * HD : 2 * span + (h + 1) * HD]
            q[h, at, :] = (qkv[:, cols].astype(BF16).astype(F32) * 0.125).astype(BF16)
            k[h, at, :] = kk.astype(BF16)
            v[h, at, :] = vv.astype(BF16)
            kt[h, g] = kk.T.astype(BF16)
            vt[h, g] = vv.T.astype(BF16)
    copies = [
        pltpu.make_async_copy(source, target, sems.at[index])
        for index, (source, target) in enumerate(zip((nrm, q, k, v, kt), stored))
    ]
    for copy in copies:
        copy.start()

    def variant(count):
        def step(t, carry):
            h, j = t // parts, t % parts
            g = me ^ j

            @pl.when(g < count)
            def _():
                qb = q[h, pl.ds(pl.multiple_of(g * rows, rows), rows), :]
                scores = [
                    mm_nt(k[h, c * rows : (c + 1) * rows, :], qb) for c in range(count)
                ]
                scores[-1] = key_mask(scores[-1], live - (count - 1) * rows)
                top = functools.reduce(
                    jnp.maximum, [jnp.max(s, axis=0, keepdims=True) for s in scores]
                )
                total, mixed = 0.0, 0.0
                for c in range(count):
                    e = jnp.exp(scores[c] - top)
                    total = total + jnp.sum(e, axis=0, keepdims=True)
                    mixed = mixed + mm(vt[h, c], e.astype(BF16))
                ot[t] = mixed / total
                lse[t] = jnp.broadcast_to(top + jnp.log(total), (8, rows))

            @pl.when(g >= count)
            def _():
                ot[t] = jnp.zeros((HD, rows), F32)
                lse[t] = jnp.zeros((8, rows), F32)

            return carry

        lax.fori_loop(0, heads * parts, step, 0)

    blocks = (live + rows - 1) // rows
    for count in range(1, parts + 1):
        pl.when(blocks == count)(functools.partial(variant, count))
    for j in range(parts):
        stacked = jnp.concatenate([ot[h * parts + j] for h in range(heads)], axis=0)
        outs[j][...] = stacked.T.astype(BF16)
    for copy in copies:
        copy.wait()


def whole(*arrays):
    return [pl.BlockSpec(a.shape, lambda i, n=a.ndim: (0,) * n) for a in arrays]


def attend_forward(place, live, xs, w, gain, shift, bias):
    parts, (rows, width) = len(xs), xs[0].shape
    span = w.shape[1] // 3
    heads, full = span // HD, parts * rows
    shape = jax.ShapeDtypeStruct
    kept = [(parts, rows, width)] + [(heads, full, HD)] * 3 + [(heads, parts, HD, rows)]
    outs_like, lse_like = shape((rows, span), BF16), shape((heads * parts, 8, rows), F32)
    outs = pl.pallas_call(
        functools.partial(attend_kernel, parts, heads, rows),
        grid=(1,),
        in_specs=[pl.BlockSpec(memory_space=pltpu.SMEM)] + whole(*xs, w, gain, shift, bias),
        out_specs=[pl.BlockSpec(memory_space=pltpu.HBM)] * 5
        + whole(*[outs_like] * parts, lse_like),
        out_shape=[shape(dims, BF16) for dims in kept]
        + [outs_like] * parts
        + [lse_like],
        scratch_shapes=[pltpu.VMEM(dims, BF16) for dims in kept]
        + [
            pltpu.VMEM((heads, parts, HD, rows), BF16),
            pltpu.VMEM((heads * parts, HD, rows), F32),
            pltpu.SemaphoreType.DMA((5,)),
        ],
        cost_estimate=pl.CostEstimate(
            flops=2 * full * width * 3 * span + 4 * full * full * span,
            bytes_accessed=2 * (2 * full * width + width * 3 * span + 6 * full * span),
            transcendentals=heads * full * full,
        ),
        compiler_params=pltpu.CompilerParams(vmem_limit_bytes=60 << 20),
        name="attend_forward",
    )(jnp.stack([place, live]), *xs, w, gain, shift, bias)
    return outs[0], outs[1:5], outs[5 : 5 + parts], outs[5 + parts]


def attend_back_kernel(parts, heads, rows, info, *refs):
    xs, grads = refs[:parts], refs[parts : 2 * parts]
    w, q, k, v, kt, lse = refs[2 * parts : 2 * parts + 6]
    dqkv = refs[2 * parts + 6]
    dns = refs[2 * parts + 7 : 3 * parts + 7]
    sums, cols = refs[3 * parts + 7 : 3 * parts + 9]
    do, dk, dv, dqt = refs[3 * parts + 9 :]
    me, live = info[0], info[1]
    for j in range(parts):
        block = grads[j][...].astype(F32)
        for h in range(heads):
            do[h * parts + j] = block[:, h * HD : (h + 1) * HD].astype(BF16)
    dk[...] = jnp.zeros_like(dk)
    dv[...] = jnp.zeros_like(dv)

    def variant(count):
        def step(t, carry):
            h, j = t // parts, t % parts
            g = me ^ j

            @pl.when(g < count)
            def _():
                qb = q[h, pl.ds(pl.multiple_of(g * rows, rows), rows), :]
                dob = do[t]
                shift = lse[t][0:1, :]
                probs, dps, inner = [], [], 0.0
                for c in range(count):
                    span = slice(c * rows, (c + 1) * rows)
                    s = mm_nt(k[h, span, :], qb)
                    if c == count - 1:
                        s = key_mask(s, live - c * rows)
                    p = jnp.exp(s - shift)
                    dp = mm_nt(v[h, span, :], dob)
                    inner = inner + jnp.sum(p * dp, axis=0, keepdims=True)
                    dv[h, c] += mm(p.astype(BF16), dob)
                    probs.append(p)
                    dps.append(dp)
                dq = 0.0
                for c in range(count):
                    ds = (probs[c] * (dps[c] - inner)).astype(BF16)
                    dk[h, c] += mm(ds, qb)
                    dq = dq + mm(kt[h, c], ds)
                dqt[t] = dq * 0.125

            @pl.when(g >= count)
            def _():
                dqt[t] = jnp.zeros((HD, rows), F32)

            return carry

        lax.fori_loop(0, heads * parts, step, 0)

    blocks = (live + rows - 1) // rows
    for count in range(1, parts + 1):
        pl.when(blocks == count)(functools.partial(variant, count))
    shift_sum, gain_sum, col_sum = 0.0, 0.0, 0.0
    for j in range(parts):
        g = me ^ j
        dq = jnp.concatenate([dqt[h * parts + j] for h in range(heads)], axis=0).T
        pieces = [dq] + [dk[h, g] for h in range(heads)] + [dv[h, g] for h in range(heads)]
        block = jnp.concatenate(pieces, axis=1).astype(BF16)
        dqkv[j] = block
        col_sum = col_sum + jnp.sum(block.astype(F32), axis=0, keepdims=True)
        dn = mm_nt(block, w[...])
        unit, _ = centred(xs[j][...].astype(F32))
        shift_sum = shift_sum + jnp.sum(dn, axis=0, keepdims=True)
        gain_sum = gain_sum + jnp.sum(dn * unit, axis=0, keepdims=True)
        dns[j][...] = dn.astype(BF16)
    sums[0:1, :] = gain_sum
    sums[1:2, :] = shift_sum
    cols[0:1, :] = col_sum


def attend_backward(place, live, xs, grads, w, saved, lse):
    parts, (rows, width) = len(xs), xs[0].shape
    span = w.shape[1] // 3
    heads, full = span // HD, parts * rows
    shape = jax.ShapeDtypeStruct
    out_shape = [
        shape((parts, rows, 3 * span), BF16),
        *[shape((rows, width), BF16)] * parts,
        shape((2, width), F32),
        shape((1, 3 * span), F32),
    ]
    outs = pl.pallas_call(
        functools.partial(attend_back_kernel, parts, heads, rows),
        grid=(1,),
        in_specs=[pl.BlockSpec(memory_space=pltpu.SMEM)] + whole(*xs, *grads, w, *saved, lse),
        out_specs=whole(*out_shape),
        out_shape=out_shape,
        scratch_shapes=[
            pltpu.VMEM((heads * parts, rows, HD), BF16),
            pltpu.VMEM((heads, parts, rows, HD), F32),
            pltpu.VMEM((heads, parts, rows, HD), F32),
            pltpu.VMEM((heads * parts, HD, rows), F32),
        ],
        cost_estimate=pl.CostEstimate(
            flops=2 * full * width * 3 * span + 10 * full * full * span,
            bytes_accessed=2 * (3 * full * width + width * 3 * span + 9 * full * span),
            transcendentals=heads * full * full,
        ),
        compiler_params=pltpu.CompilerParams(vmem_limit_bytes=60 << 20),
        name="attend_backward",
    )(jnp.stack([place, live]), *xs, *grads, w, *saved, lse)
    return outs[0], outs[1 : 1 + parts], outs[1 + parts], outs[2 + parts]


def live_only(values, first, live):
    rows = first + lax.broadcasted_iota(jnp.int32, values.shape, 0)
    return jnp.where(rows < live, values, jnp.zeros_like(values))


def folded(values):
    return functools.reduce(
        jnp.add, [values[r : r + 8] for r in range(0, values.shape[0], 8)]
    )


def token_kernel(plan, seqs, parts, info, *refs):
    refs = list(refs)
    take = lambda count: [refs.pop(0) for _ in range(count)]
    sources = take(max(p[0] for p in plan) + 1)
    pieces = take(seqs * parts)
    x, cot, dvec, mgain, mshift, fvec = take(6)
    block_out, resid_grad, fnorm, branch, og, anorm = take(6)
    hid, pg = take(2)
    mds = take(seqs * parts)
    dsum, msum, fsum = take(3)
    wo, w1, w2, ob, munit, mscale, res, runit, rscale = take(9)
    pre, cdf, act, hg, fscale, ngs, dacc, macc, facc, sems = take(10)
    step = pl.program_id(0)
    me, core = info[seqs], info[seqs + 1]
    live = info[step] - me * x.shape[0]
    rows, width = x.shape
    span, units = width // parts, pre.shape[1]
    tile, wide = 16, 384
    quarters = units // width

    def place(quarter):
        turned = quarter + quarters // 2 * core
        return jnp.where(turned >= quarters, turned - quarters, turned)

    targets = {"out": wo, "fc1": w1, "fc2": w2}

    @pl.when(step == 0)
    def _():
        copies = []
        for index, (src, k, start, count, name, at, at_step, col, col_step) in enumerate(plan):
            source = sources[src] if k is None else sources[src].at[k]
            target = targets[name]
            turn = core if src == 0 else 1 - core
            if at_step:
                at = pl.multiple_of(at + at_step * turn, 16)
            if col_step:
                col = pl.multiple_of(col + col_step * turn, 128)
            target = target.at[pl.ds(at, count), pl.ds(col, source.shape[1])]
            copies.append(
                pltpu.make_async_copy(source.at[pl.ds(start, count)], target, sems.at[index])
            )
        for copy in copies:
            copy.start()
        dacc[...] = jnp.zeros_like(dacc)
        macc[...] = jnp.zeros_like(macc)
        facc[...] = jnp.zeros_like(facc)
        for copy in copies:
            copy.wait()

    for i in range(seqs):

        @pl.when(step == i)
        def _(i=i):
            for j in range(parts):
                ob[j] = pieces[i * parts + j][...]

    def tiles(size):
        def decorate(body):
            def run(t, carry):
                body(pl.ds(pl.multiple_of(t * size, size), size), t * size)
                return carry

            lax.fori_loop(0, rows // size, run, 0)

        return decorate

    @tiles(32)
    def _(at, first):
        blocks = [ob[j, at, :].astype(F32) for j in range(parts)]
        mean = sum(jnp.sum(b, axis=1, keepdims=True) for b in blocks) / width
        blocks = [b - mean for b in blocks]
        var = sum(jnp.sum(b * b, axis=1, keepdims=True) for b in blocks) / width
        scale = lax.rsqrt(var + eps)
        mscale[at, :] = jnp.broadcast_to(scale, (32, 128))
        for j in range(parts):
            g = me ^ j
            unit = blocks[j] * scale
            munit[j, at, :] = unit
            anorm[g, at, :] = (unit * mgain[g] + mshift[g]).astype(BF16)

    mixed = sum(mm(anorm[g], wo[g * span : (g + 1) * span, :]) for g in range(parts))
    res[...] = x[...].astype(F32) + mixed + dvec[2:3, :]

    @tiles(32)
    def _(at, first):
        unit, scale = centred(res[at, :])
        runit[at, :] = unit
        rscale[at, :] = jnp.broadcast_to(scale, (32, 128))
        fnorm[at, :] = (unit * dvec[0:1, :] + dvec[1:2, :]).astype(BF16)

    for c in range(units // width):
        cols = slice(c * width, (c + 1) * width)
        pre[:, cols] = mm(fnorm[...], w1[:, cols])
    chunks = [slice(c, c + wide) for c in range(0, units, wide)]

    @tiles(tile)
    def _(at, first):
        total, square = 0.0, 0.0
        for c in chunks:
            v = pre[at, c] + fvec[1:2, c]
            below = 0.5 * (1.0 + lax.erf(v * 0.7071067811865476))
            a = v * below
            pre[at, c] = v
            cdf[at, c] = below
            act[at, c] = a
            total = total + a
        mean = jnp.sum(total, axis=1, keepdims=True) / units
        for c in chunks:
            d = act[at, c] - mean
            act[at, c] = d
            square = square + d * d
        scale = lax.rsqrt(jnp.sum(square, axis=1, keepdims=True) / units + eps)
        fscale[at, :] = jnp.broadcast_to(scale, (tile, 128))
        for c in chunks:
            unit = act[at, c] * scale
            act[at, c] = unit
            value = (unit * fvec[0:1, c] + fvec[2:3, c]).astype(BF16)
            hid[at, c] = value

    out = res[...] + mm(hid[...], w2[...]) + dvec[3:4, :]
    block_out[...] = live_only(out, 0, live).astype(BF16)
    kept = live_only(cot[...].astype(F32), 0, live)
    og[...] = kept.astype(BF16)
    dacc[24:32, :] += folded(kept)
    for c in range(units // width):
        cols = slice(c * width, (c + 1) * width)
        hg[:, cols] = mm_nt(og[...], w2[cols, :])

    @tiles(tile)
    def _(at, first):
        one, two = 0.0, 0.0
        for c in chunks:
            unit, grad = act[at, c], hg[at, c]
            both = grad * unit
            facc[0:8, c] += folded(both)
            facc[16:24, c] += folded(grad)
            gain = fvec[0:1, c]
            hg[at, c] = grad * gain
            one = one + grad * gain
            two = two + both * gain
        one = jnp.sum(one, axis=1, keepdims=True) / units
        two = jnp.sum(two, axis=1, keepdims=True) / units
        scale = fscale[at, 0:1]
        for c in chunks:
            v = pre[at, c]
            slope = cdf[at, c] + v * (jnp.exp(-0.5 * v * v) * 0.3989422804014327)
            grad = scale * (hg[at, c] - one - act[at, c] * two) * slope
            low = grad.astype(BF16)
            pg[place(c.start // width), at, c.start % width : c.start % width + wide] = low
            facc[8:16, c] += folded(low.astype(F32))

    fg = hg.at[:, 0:width]
    fg[...] = sum(
        mm_nt(pg[place(c)], w1[:, c * width : (c + 1) * width]) for c in range(units // width)
    )

    @tiles(32)
    def _(at, first):
        grad, unit = fg[at, :], runit[at, :]
        dacc[0:8, :] += folded(grad * unit)
        dacc[8:16, :] += folded(grad)
        total = og[at, :].astype(F32) + norm_back(grad * dvec[0:1, :], unit, rscale[at, 0:1])
        resid_grad[at, :] = total
        branch[at, :] = total.astype(BF16)
        dacc[16:24, :] += folded(total)

    for g in range(parts):
        ngs[g] = mm_nt(branch[...], wo[g * span : (g + 1) * span, :])

    @tiles(32)
    def _(at, first):
        one, two, scaled = 0.0, 0.0, []
        for j in range(parts):
            g = me ^ j
            grad, unit = ngs[g, at, :], munit[j, at, :]
            macc[g, 0:8, :] += folded(grad * unit)
            macc[g, 8:16, :] += folded(grad)
            m = grad * mgain[g]
            one = one + jnp.sum(m, axis=1, keepdims=True)
            two = two + jnp.sum(m * unit, axis=1, keepdims=True)
            scaled.append(m)
        one, two, scale = one / width, two / width, mscale[at, 0:1]
        for j in range(parts):
            value = scale * (scaled[j] - one - munit[j, at, :] * two)
            ob[j, at, :] = value.astype(BF16)

    for i in range(seqs):

        @pl.when(step == i)
        def _(i=i):
            for j in range(parts):
                mds[i * parts + j][...] = ob[j]

    @pl.when(step == seqs - 1)
    def _():
        for r in range(4):
            dsum[r : r + 1, :] = jnp.sum(dacc[8 * r : 8 * r + 8, :], axis=0, keepdims=True)
        for r in range(3):
            fsum[r : r + 1, :] = jnp.sum(facc[8 * r : 8 * r + 8, :], axis=0, keepdims=True)
        for g in range(parts):
            for r in range(2):
                part = macc[g, 8 * r : 8 * r + 8, :]
                msum[g, r : r + 1, :] = jnp.sum(part, axis=0, keepdims=True)


def token_stage(info, plan, sources, pieces, x, cot, dvec, mgain, mshift, fvec):
    seqs, rows, width = x.shape
    parts, units = len(pieces[0]), fvec.shape[1]
    span = width // parts
    shape = jax.ShapeDtypeStruct
    full = lambda *dims: pl.BlockSpec(dims, lambda i: (0,) * len(dims))
    by_seq = pl.BlockSpec((None, rows, width), lambda i: (i, 0, 0))
    by_rows = lambda cols: pl.BlockSpec((rows, cols), lambda i: (i, 0))
    n = seqs * rows
    outs = pl.pallas_call(
        functools.partial(token_kernel, plan, seqs, parts),
        grid=(seqs,),
        in_specs=[pl.BlockSpec(memory_space=pltpu.SMEM)]
        + [pl.BlockSpec(memory_space=pl.ANY)] * len(sources)
        + [full(rows, span)] * (seqs * parts)
        + [
            by_seq,
            by_seq,
            full(*dvec.shape),
            full(*mgain.shape),
            full(*mshift.shape),
            full(*fvec.shape),
        ],
        out_specs=[by_seq, by_seq]
        + [by_rows(width)] * 3
        + [pl.BlockSpec((parts, rows, span), lambda i: (0, i, 0))]
        + [by_rows(units)]
        + [pl.BlockSpec((units // width, rows, width), lambda i: (0, i, 0))]
        + [full(rows, span)] * (seqs * parts)
        + [full(4, width), full(parts, 2, span), full(3, units)],
        out_shape=[shape((seqs, rows, width), BF16), shape((seqs, rows, width), F32)]
        + [shape((n, width), BF16)] * 3
        + [shape((parts, n, span), BF16)]
        + [shape((n, units), BF16), shape((units // width, n, width), BF16)]
        + [shape((rows, span), BF16)] * (seqs * parts)
        + [shape((4, width), F32), shape((parts, 2, span), F32), shape((3, units), F32)],
        scratch_shapes=[
            pltpu.VMEM((width, width), BF16),
            pltpu.VMEM((width, units), BF16),
            pltpu.VMEM((units, width), BF16),
            pltpu.VMEM((parts, rows, span), BF16),
            pltpu.VMEM((parts, rows, span), F32),
            pltpu.VMEM((rows, 128), F32),
            pltpu.VMEM((rows, width), F32),
            pltpu.VMEM((rows, width), F32),
            pltpu.VMEM((rows, 128), F32),
        ]
        + [pltpu.VMEM((rows, units), F32)] * 4
        + [
            pltpu.VMEM((rows, 128), F32),
            pltpu.VMEM((parts, rows, span), F32),
            pltpu.VMEM((32, width), F32),
            pltpu.VMEM((parts, 16, span), F32),
            pltpu.VMEM((24, units), F32),
            pltpu.SemaphoreType.DMA((len(plan),)),
        ],
        cost_estimate=pl.CostEstimate(
            flops=2 * n * width * (4 * units + 2 * width),
            bytes_accessed=2 * width * (2 * units + width) + 2 * n * (4 * units + 12 * width),
            transcendentals=2 * n * units,
        ),
        compiler_params=pltpu.CompilerParams(vmem_limit_bytes=60 << 20),
        name="token_stage",
    )(info, *sources, *[p for group in pieces for p in group], x, cot, dvec, mgain, mshift, fvec)
    outs = list(outs)
    mds = outs[8 : 8 + seqs * parts]
    mds = [mds[i * parts : (i + 1) * parts] for i in range(seqs)]
    return outs[:6], outs[6], outs[7], mds, outs[8 + seqs * parts :]


def swap(values, axis, mask):
    count = lax.axis_size(axis)
    return lax.ppermute(values, axis, [(i, i ^ mask) for i in range(count)])


def pick(values, index, axis):
    return lax.dynamic_index_in_dim(values, index, axis, keepdims=False)


def after(values, others):
    return lax.optimization_barrier((values, others))[0]


def spread_blocks(block, axis):
    count, me = lax.axis_size(axis), lax.axis_index(axis)
    held = {0: block}
    bit = count // 2
    while bit:
        held |= {mask | bit: swap(part, axis, bit) for mask, part in held.items()}
        bit //= 2
    whole = jnp.zeros((count,) + block.shape, block.dtype)
    for mask, part in held.items():
        whole = lax.dynamic_update_index_in_dim(whole, part, me ^ mask, 0)
    return whole


def sum_blocks(blocks, axis, kind):
    blocks = lax.all_to_all(blocks.astype(kind), axis, split_axis=0, concat_axis=0, tiled=True)
    return jnp.sum(blocks.astype(F32), axis=0)


def shards(
    activations,
    cotangent,
    lengths,
    w_qkv,
    w_out,
    w_fc1,
    w_fc2,
    d_gains,
    d_biases,
    ff_gain,
    ff_biases,
):
    seqs, rows, width = activations.shape
    parts, owners = lax.axis_size("seq"), lax.axis_size("fsdp")
    s = lax.axis_index("seq")
    core = s % 2
    span = width // parts
    own_rows = w_qkv.shape[0]
    own_ff = w_fc2.shape[0]
    half_ff, half_rows = own_ff // 2, own_rows // 2
    ff_half = half_ff * owners
    quarter = own_ff // own_rows

    own_w = pick(w_qkv.reshape(own_rows, 3, parts, span), s, 2).reshape(own_rows, 3 * span)
    ff_small = jnp.concatenate([ff_gain[:, None], ff_biases], axis=1).T.reshape(
        3 * quarter, own_rows
    )
    small = jnp.concatenate([d_gains.T, d_biases.T, ff_small], axis=0)
    kinds = small.shape[0]
    small_rows = 32
    small = jnp.pad(small, ((0, small_rows - kinds), (0, 3 * span - own_rows)))
    block = jnp.concatenate([own_w, small], axis=0)
    first = spread_blocks(block, "fsdp")
    my_qkv = first[:, :own_rows].reshape(width, 3 * span)
    small = first[:, own_rows : own_rows + kinds, :own_rows].astype(F32)
    d_small = small[:, :10].transpose(1, 0, 2).reshape(10, width)
    gains, biases = d_small[:3], d_small[3:]
    ff_small = small[:, 10:].reshape(owners, 3, own_ff).transpose(1, 0, 2).reshape(3, 2 * ff_half)

    w_out, w_fc1, w_fc2 = after((w_out, w_fc1, w_fc2), block)
    fc1_half = lax.dynamic_slice(w_fc1, (0, core * ff_half), (own_rows, ff_half))
    columns = range(0, ff_half, width)
    rest = jnp.concatenate(
        [pick(w_out.reshape(2, half_rows, width), core, 0)]
        + [fc1_half[:, c : c + width] for c in columns]
        + [pick(w_fc2.reshape(2, half_ff, width), core, 0)],
        axis=0,
    )
    rest_rows = rest.shape[0]
    rest = lax.all_gather(rest, "fsdp", axis=0, tiled=False)

    qkv_bias = pick(
        jnp.stack([biases[1], jnp.zeros_like(biases[1]), biases[2]]).reshape(3, parts, span), s, 1
    ).reshape(1, 3 * span)
    x_parts, mixed_parts, kept = [], [], []
    for i in range(seqs):
        mine = activations[i]
        across = swap(mine, "seq", 2)
        x_parts.append([mine, swap(mine, "seq", 1), across, swap(across, "seq", 1)])
    for i in range(seqs):
        if i > 0:
            x_parts[i] = after(x_parts[i], [kept[i - 1][2], mixed_parts[:-1]])
        normed, saved, outs, lse = attend_forward(
            s, lengths[i], x_parts[i], my_qkv, gains[0:1], biases[0:1], qkv_bias
        )
        kept.append((normed, saved, lse))
        mixed_parts.append([outs[0]] + [swap(outs[j], "seq", j) for j in range(1, parts)])
    rest = after(rest, [lse for _, _, lse in kept])
    rest_other = swap(rest, "seq", 1)

    plan, sources = [], [rest, rest_other]
    if half_rows % 16 == 0 and half_ff % 16 == 0:
        for src in range(2):
            for k in range(owners):
                plan.append((src, k, 0, half_rows, "out", k * own_rows, half_rows, 0, 0))
                for at, c in enumerate(columns):
                    start = half_rows + at * own_rows
                    plan.append((src, k, start, own_rows, "fc1", k * own_rows, 0, c, ff_half))
                start = rest_rows - half_ff
                plan.append((src, k, start, half_ff, "fc2", k * own_ff, half_ff, 0, 0))
    else:
        pair = [jnp.where(core == 0, rest, rest_other), jnp.where(core == 0, rest_other, rest)]
        blocks = [
            buf[:, half_rows + at * own_rows : half_rows + (at + 1) * own_rows].reshape(width, width)
            for buf in pair
            for at in range(len(columns))
        ]
        sources = [
            jnp.concatenate([buf[:, :half_rows] for buf in pair], axis=1).reshape(width, width),
            jnp.concatenate(blocks, axis=1),
            jnp.concatenate([buf[:, rest_rows - half_ff :] for buf in pair], axis=1).reshape(
                2 * ff_half, width
            ),
        ]
        names = ("out", "fc1", "fc2")
        plan = [(i, None, 0, sources[i].shape[0], names[i], 0, 0, 0, 0) for i in range(3)]
    info = jnp.concatenate([lengths, jnp.stack([s, core]).astype(jnp.int32)])
    dvec = jnp.stack([gains[2], biases[5], biases[4], biases[6]])
    tokens = token_stage(
        info,
        plan,
        sources,
        mixed_parts,
        activations,
        cotangent,
        dvec,
        gains[1].reshape(parts, 1, span),
        biases[3].reshape(parts, 1, span),
        ff_small,
    )
    (block_out, resid_grad, fnorm, branch, og, anorm), hid, pg, mixed_grads, sums = tokens
    dsum, msum, fsum = sums

    grad_out = jnp.einsum("gnk,nd->gkd", anorm, branch, preferred_element_type=F32)
    grad_out = grad_out.reshape(owners, 2, half_rows, width)
    grad_fc2 = mm_tn(hid, og).reshape(owners, 2, half_ff, width)
    mixed_grads = [[g[0]] + [swap(g[j], "seq", j) for j in range(1, parts)] for g in mixed_grads]
    grads = []
    for src in (1, 0):
        turn = core if src == 0 else 1 - core
        pieces = [pick(grad_out, turn, 1)]
        pieces += [
            mm_tn(fnorm, pg[len(columns) * src + at]).reshape(owners, own_rows, width)
            for at in range(len(columns))
        ]
        pieces.append(pick(grad_fc2, turn, 1))
        grads.append(jnp.concatenate([p.astype(BF16) for p in pieces], axis=1))
    rest_sum = grads[1].astype(F32) + swap(grads[0], "seq", 1).astype(F32)
    rest_sum = rest_sum.astype(BF16).reshape(owners * rest_rows, width)
    mixed_grads[0], rest_sum = lax.optimization_barrier((mixed_grads[0], rest_sum))
    rest_sum = lax.psum_scatter(rest_sum, "fsdp", scatter_dimension=0, tiled=True)

    grad_own, summed, head_sums, unit_sums, near = 0.0, [], 0.0, 0.0, []
    for i in range(seqs):
        pieces = mixed_grads[i]
        if i > 0:
            pieces = after(pieces, [sums, near[:-1]])
        normed, saved, lse = kept[i]
        dqkv, dns, sums, cols = attend_backward(
            s, lengths[i], x_parts[i], pieces, my_qkv, saved, lse
        )
        grad_own = grad_own + mm_tn(
            normed.reshape(parts * rows, width), dqkv.reshape(parts * rows, 3 * span)
        )
        unit_sums, head_sums = unit_sums + sums, head_sums + cols
        near.append([swap(dns[j], "seq", 1) for j in (1, 3)])
        far = (dns[2].astype(F32) + near[i][1].astype(F32)).astype(BF16)
        far = swap(far, "seq", 2).astype(F32)
        summed.append(dns[0].astype(F32) + near[i][0].astype(F32) + far)
    first_grad = jnp.stack(summed)
    first_unit, first_scale = centred(activations.astype(F32))
    input_grad = resid_grad + norm_back(first_grad * gains[0], first_unit, first_scale)

    def head_columns(values):
        blank = jnp.zeros((parts, span), F32)
        return lax.dynamic_update_slice(blank, values[None], (s, 0)).reshape(width)

    small_grads = jnp.stack(
        [
            unit_sums[0],
            msum[:, 0].reshape(width),
            dsum[0],
            unit_sums[1],
            head_columns(head_sums[0, :span]),
            head_columns(head_sums[0, 2 * span :]),
            msum[:, 1].reshape(width),
            dsum[2],
            dsum[1],
            dsum[3],
        ]
    )
    feed_grads = fsum.reshape(3, owners, quarter, own_rows)
    small_blocks = jnp.concatenate(
        [
            small_grads.reshape(10, owners, own_rows).transpose(1, 0, 2),
            feed_grads.transpose(1, 0, 2, 3).reshape(owners, 3 * quarter, own_rows),
        ],
        axis=1,
    )
    small_blocks = jnp.pad(small_blocks, ((0, 0), (0, small_rows - kinds), (0, 0)))
    small_sum = sum_blocks(small_blocks, "fsdp", F32)
    own_sum = sum_blocks(grad_own.reshape(owners, own_rows, 3 * span), "fsdp", BF16).astype(BF16)
    rest_sum = after(rest_sum, own_sum)
    rest_sum = rest_sum.astype(F32) + swap(rest_sum, "seq", 2).astype(F32)
    small_sum = [small_sum] + [swap(small_sum, "seq", j) for j in range(1, parts)]
    small_sum = (small_sum[0] + small_sum[1]) + (small_sum[2] + small_sum[3])
    feed_sum = small_sum[10:kinds].reshape(3, own_ff)
    group = jnp.stack([own_sum] + [swap(own_sum, "seq", j) for j in range(1, parts)])
    w_qkv_grad = jnp.concatenate(
        [
            pick(group, s ^ g, 0)[:, p * span : (p + 1) * span]
            for p in range(3)
            for g in range(parts)
        ],
        axis=1,
    ).astype(F32)

    other_sum = swap(rest_sum, "seq", 1)
    pair = [
        jnp.where(core == 0, rest_sum, other_sum),
        jnp.where(core == 0, other_sum, rest_sum),
    ]
    w_out_grad = jnp.concatenate([p[:half_rows] for p in pair], axis=0)
    w_fc1_grad = jnp.concatenate(
        [
            p[half_rows + at * own_rows : half_rows + (at + 1) * own_rows]
            for p in pair
            for at in range(len(columns))
        ],
        axis=1,
    )
    w_fc2_grad = jnp.concatenate([p[rest_rows - half_ff :] for p in pair], axis=0)
    return (
        block_out,
        input_grad,
        w_qkv_grad,
        w_out_grad,
        w_fc1_grad,
        w_fc2_grad,
        small_sum[:3].T,
        small_sum[3:10].T,
        feed_sum[0],
        feed_sum[1:].T,
    )


def solution(mesh):
    return jax.shard_map(
        shards,
        mesh=mesh,
        in_specs=(
            P("fsdp", "seq", None),
            P("fsdp", "seq", None),
            P("fsdp"),
            P("fsdp", None),
            P("fsdp", None),
            P("fsdp", None),
            P("fsdp", None),
            P("fsdp", None),
            P("fsdp", None),
            P("fsdp"),
            P("fsdp", None),
        ),
        out_specs=(
            P("fsdp", "seq", None),
            P("fsdp", "seq", None),
            P("fsdp", None),
            P("fsdp", None),
            P("fsdp", None),
            P("fsdp", None),
            P("fsdp", None),
            P("fsdp", None),
            P("fsdp"),
            P("fsdp", None),
        ),
        check_vma=False,
    )
```

```python
import functools

import jax
import jax.numpy as jnp
from jax import lax
from jax.experimental import pallas as pl
from jax.experimental.pallas import tpu as pltpu
from jax.sharding import PartitionSpec as P


HD = 64
eps = 1e-05
F32 = jnp.float32
BF16 = jnp.bfloat16
NT = (((1,), (1,)), ((), ()))


def mm(left, right):
    return jnp.dot(left, right, preferred_element_type=F32)


def mm_nt(left, right):
    return lax.dot_general(left, right, NT, preferred_element_type=F32)


def mm_tn(left, right):
    return lax.dot_general(left, right, (((0,), (0,)), ((), ())), preferred_element_type=F32)


def centred(values):
    center = values - jnp.mean(values, axis=-1, keepdims=True)
    spread = jnp.mean(center * center, axis=-1, keepdims=True)
    scale = lax.rsqrt(spread + eps)
    return center * scale, scale


def norm_back(grad, unit, scale):
    return scale * (
        grad
        - jnp.mean(grad, axis=-1, keepdims=True)
        - unit * jnp.mean(grad * unit, axis=-1, keepdims=True)
    )


def key_mask(block, live_rows):
    rows = lax.broadcasted_iota(jnp.int32, block.shape, 0)
    return jnp.where(rows < live_rows, block, -1e30)


def attend_kernel(parts, heads, rows, info, *refs):
    xs = refs[:parts]
    w, gain, shift, bias = refs[parts : parts + 4]
    stored = refs[parts + 4 : parts + 9]
    outs = refs[parts + 9 : 2 * parts + 9]
    lse, nrm, q, k, v, kt, vt, ot, sems = refs[2 * parts + 9 :]
    me, live = info[0], info[1]
    span = heads * HD
    for j in range(parts):
        g = me ^ j
        at = pl.ds(pl.multiple_of(g * rows, rows), rows)
        unit, _ = centred(xs[j][...].astype(F32))
        normed = (unit * gain[...] + shift[...]).astype(BF16)
        nrm[j] = normed
        qkv = mm(normed, w[...]) + bias[...]
        for h in range(heads):
            cols = slice(h * HD, (h + 1) * HD)
            kk = qkv[:, span + h * HD : span + (h + 1) * HD]
            vv = qkv[:, 2 * span + h * HD : 2 * span + (h + 1) * HD]
            q[h, at, :] = (qkv[:, cols].astype(BF16).astype(F32) * 0.125).astype(BF16)
            k[h, at, :] = kk.astype(BF16)
            v[h, at, :] = vv.astype(BF16)
            kt[h, g] = kk.T.astype(BF16)
            vt[h, g] = vv.T.astype(BF16)
    copies = [
        pltpu.make_async_copy(source, target, sems.at[index])
        for index, (source, target) in enumerate(zip((nrm, q, k, v, kt), stored))
    ]
    for copy in copies:
        copy.start()

    def variant(count):
        def step(t, carry):
            h, j = t // parts, t % parts
            g = me ^ j

            @pl.when(g < count)
            def _():
                qb = q[h, pl.ds(pl.multiple_of(g * rows, rows), rows), :]
                scores = [
                    mm_nt(k[h, c * rows : (c + 1) * rows, :], qb) for c in range(count)
                ]
                scores[-1] = key_mask(scores[-1], live - (count - 1) * rows)
                top = functools.reduce(
                    jnp.maximum, [jnp.max(s, axis=0, keepdims=True) for s in scores]
                )
                total, mixed = 0.0, 0.0
                for c in range(count):
                    e = jnp.exp(scores[c] - top)
                    total = total + jnp.sum(e, axis=0, keepdims=True)
                    mixed = mixed + mm(vt[h, c], e.astype(BF16))
                ot[t] = mixed / total
                lse[t] = jnp.broadcast_to(top + jnp.log(total), (8, rows))

            @pl.when(g >= count)
            def _():
                ot[t] = jnp.zeros((HD, rows), F32)
                lse[t] = jnp.zeros((8, rows), F32)

            return carry

        lax.fori_loop(0, heads * parts, step, 0)

    blocks = (live + rows - 1) // rows
    for count in range(1, parts + 1):
        pl.when(blocks == count)(functools.partial(variant, count))
    for j in range(parts):
        stacked = jnp.concatenate([ot[h * parts + j] for h in range(heads)], axis=0)
        outs[j][...] = stacked.T.astype(BF16)
    for copy in copies:
        copy.wait()


def whole(*arrays):
    return [pl.BlockSpec(a.shape, lambda i, n=a.ndim: (0,) * n) for a in arrays]


def attend_forward(place, live, xs, w, gain, shift, bias):
    parts, (rows, width) = len(xs), xs[0].shape
    span = w.shape[1] // 3
    heads, full = span // HD, parts * rows
    shape = jax.ShapeDtypeStruct
    kept = [(parts, rows, width)] + [(heads, full, HD)] * 3 + [(heads, parts, HD, rows)]
    outs_like, lse_like = shape((rows, span), BF16), shape((heads * parts, 8, rows), F32)
    outs = pl.pallas_call(
        functools.partial(attend_kernel, parts, heads, rows),
        grid=(1,),
        in_specs=[pl.BlockSpec(memory_space=pltpu.SMEM)] + whole(*xs, w, gain, shift, bias),
        out_specs=[pl.BlockSpec(memory_space=pltpu.HBM)] * 5
        + whole(*[outs_like] * parts, lse_like),
        out_shape=[shape(dims, BF16) for dims in kept]
        + [outs_like] * parts
        + [lse_like],
        scratch_shapes=[pltpu.VMEM(dims, BF16) for dims in kept]
        + [
            pltpu.VMEM((heads, parts, HD, rows), BF16),
            pltpu.VMEM((heads * parts, HD, rows), F32),
            pltpu.SemaphoreType.DMA((5,)),
        ],
        cost_estimate=pl.CostEstimate(
            flops=2 * full * width * 3 * span + 4 * full * full * span,
            bytes_accessed=2 * (2 * full * width + width * 3 * span + 6 * full * span),
            transcendentals=heads * full * full,
        ),
        compiler_params=pltpu.CompilerParams(vmem_limit_bytes=60 << 20),
        name="attend_forward",
    )(jnp.stack([place, live]), *xs, w, gain, shift, bias)
    return outs[0], outs[1:5], outs[5 : 5 + parts], outs[5 + parts]


def attend_back_kernel(parts, heads, rows, info, *refs):
    xs, grads = refs[:parts], refs[parts : 2 * parts]
    w, q, k, v, kt, lse = refs[2 * parts : 2 * parts + 6]
    dqkv = refs[2 * parts + 6]
    dns = refs[2 * parts + 7 : 3 * parts + 7]
    sums, cols = refs[3 * parts + 7 : 3 * parts + 9]
    do, dk, dv, dqt = refs[3 * parts + 9 :]
    me, live = info[0], info[1]
    for j in range(parts):
        block = grads[j][...].astype(F32)
        for h in range(heads):
            do[h * parts + j] = block[:, h * HD : (h + 1) * HD].astype(BF16)
    dk[...] = jnp.zeros_like(dk)
    dv[...] = jnp.zeros_like(dv)

    def variant(count):
        def step(t, carry):
            h, j = t // parts, t % parts
            g = me ^ j

            @pl.when(g < count)
            def _():
                qb = q[h, pl.ds(pl.multiple_of(g * rows, rows), rows), :]
                dob = do[t]
                shift = lse[t][0:1, :]
                probs, dps, inner = [], [], 0.0
                for c in range(count):
                    span = slice(c * rows, (c + 1) * rows)
                    s = mm_nt(k[h, span, :], qb)
                    if c == count - 1:
                        s = key_mask(s, live - c * rows)
                    p = jnp.exp(s - shift)
                    dp = mm_nt(v[h, span, :], dob)
                    inner = inner + jnp.sum(p * dp, axis=0, keepdims=True)
                    dv[h, c] += mm(p.astype(BF16), dob)
                    probs.append(p)
                    dps.append(dp)
                dq = 0.0
                for c in range(count):
                    ds = (probs[c] * (dps[c] - inner)).astype(BF16)
                    dk[h, c] += mm(ds, qb)
                    dq = dq + mm(kt[h, c], ds)
                dqt[t] = dq * 0.125

            @pl.when(g >= count)
            def _():
                dqt[t] = jnp.zeros((HD, rows), F32)

            return carry

        lax.fori_loop(0, heads * parts, step, 0)

    blocks = (live + rows - 1) // rows
    for count in range(1, parts + 1):
        pl.when(blocks == count)(functools.partial(variant, count))
    shift_sum, gain_sum, col_sum = 0.0, 0.0, 0.0
    for j in range(parts):
        g = me ^ j
        dq = jnp.concatenate([dqt[h * parts + j] for h in range(heads)], axis=0).T
        pieces = [dq] + [dk[h, g] for h in range(heads)] + [dv[h, g] for h in range(heads)]
        block = jnp.concatenate(pieces, axis=1).astype(BF16)
        dqkv[j] = block
        col_sum = col_sum + jnp.sum(block.astype(F32), axis=0, keepdims=True)
        dn = mm_nt(block, w[...])
        unit, _ = centred(xs[j][...].astype(F32))
        shift_sum = shift_sum + jnp.sum(dn, axis=0, keepdims=True)
        gain_sum = gain_sum + jnp.sum(dn * unit, axis=0, keepdims=True)
        dns[j][...] = dn.astype(BF16)
    sums[0:1, :] = gain_sum
    sums[1:2, :] = shift_sum
    cols[0:1, :] = col_sum


def attend_backward(place, live, xs, grads, w, saved, lse):
    parts, (rows, width) = len(xs), xs[0].shape
    span = w.shape[1] // 3
    heads, full = span // HD, parts * rows
    shape = jax.ShapeDtypeStruct
    out_shape = [
        shape((parts, rows, 3 * span), BF16),
        *[shape((rows, width), BF16)] * parts,
        shape((2, width), F32),
        shape((1, 3 * span), F32),
    ]
    outs = pl.pallas_call(
        functools.partial(attend_back_kernel, parts, heads, rows),
        grid=(1,),
        in_specs=[pl.BlockSpec(memory_space=pltpu.SMEM)] + whole(*xs, *grads, w, *saved, lse),
        out_specs=whole(*out_shape),
        out_shape=out_shape,
        scratch_shapes=[
            pltpu.VMEM((heads * parts, rows, HD), BF16),
            pltpu.VMEM((heads, parts, rows, HD), F32),
            pltpu.VMEM((heads, parts, rows, HD), F32),
            pltpu.VMEM((heads * parts, HD, rows), F32),
        ],
        cost_estimate=pl.CostEstimate(
            flops=2 * full * width * 3 * span + 10 * full * full * span,
            bytes_accessed=2 * (3 * full * width + width * 3 * span + 9 * full * span),
            transcendentals=heads * full * full,
        ),
        compiler_params=pltpu.CompilerParams(vmem_limit_bytes=60 << 20),
        name="attend_backward",
    )(jnp.stack([place, live]), *xs, *grads, w, *saved, lse)
    return outs[0], outs[1 : 1 + parts], outs[1 + parts], outs[2 + parts]


def live_only(values, first, live):
    rows = first + lax.broadcasted_iota(jnp.int32, values.shape, 0)
    return jnp.where(rows < live, values, jnp.zeros_like(values))


def folded(values):
    return functools.reduce(
        jnp.add, [values[r : r + 8] for r in range(0, values.shape[0], 8)]
    )


def token_kernel(plan, seqs, parts, info, *refs):
    refs = list(refs)
    take = lambda count: [refs.pop(0) for _ in range(count)]
    sources = take(max(p[0] for p in plan) + 1)
    pieces = take(seqs * parts)
    x, cot, dvec, mgain, mshift, fvec = take(6)
    block_out, resid_grad, fnorm, branch, og, anorm = take(6)
    hid, pg = take(2)
    mds = take(seqs * parts)
    dsum, msum, fsum = take(3)
    wo, w1, w2, ob, munit, mscale, res, runit, rscale = take(9)
    pre, slope, act, hg, ngs, dacc, macc, facc, sems = take(9)
    step = pl.program_id(0)
    me, core = info[seqs], info[seqs + 1]
    live = info[step] - me * x.shape[0]
    rows, width = x.shape
    span, units = width // parts, pre.shape[1]
    band, wide = 64, 256
    quarters = units // width

    def place(quarter):
        turned = quarter + quarters // 2 * core
        return jnp.where(turned >= quarters, turned - quarters, turned)

    targets = {"out": wo, "fc1": w1, "fc2": w2}

    def copies(wanted):
        for index, (src, k, start, count, name, at, at_step, col, col_step) in enumerate(plan):
            if name not in wanted:
                continue
            source = sources[src] if k is None else sources[src].at[k]
            target = targets[name]
            turn = core if src == 0 else 1 - core
            if at_step:
                at = pl.multiple_of(at + at_step * turn, 16)
            if col_step:
                col = pl.multiple_of(col + col_step * turn, 128)
            target = target.at[pl.ds(at, count), pl.ds(col, source.shape[1])]
            yield pltpu.make_async_copy(source.at[pl.ds(start, count)], target, sems.at[index])

    def arrived(name):
        @pl.when(step == 0)
        def _():
            for copy in copies((name,)):
                copy.wait()

    @pl.when(step == 0)
    def _():
        for copy in copies(("out", "fc1", "fc2")):
            copy.start()
        dacc[...] = jnp.zeros_like(dacc)
        macc[...] = jnp.zeros_like(macc)
        facc[...] = jnp.zeros_like(facc)

    for i in range(seqs):

        @pl.when(step == i)
        def _(i=i):
            for j in range(parts):
                ob[j] = pieces[i * parts + j][...]

    def tiles(size):
        def decorate(body):
            def run(t, carry):
                body(pl.ds(pl.multiple_of(t * size, size), size), t * size)
                return carry

            lax.fori_loop(0, rows // size, run, 0)

        return decorate

    @tiles(32)
    def _(at, first):
        blocks = [ob[j, at, :].astype(F32) for j in range(parts)]
        mean = sum(jnp.sum(b, axis=1, keepdims=True) for b in blocks) / width
        blocks = [b - mean for b in blocks]
        var = sum(jnp.sum(b * b, axis=1, keepdims=True) for b in blocks) / width
        scale = lax.rsqrt(var + eps)
        mscale[at, :] = jnp.broadcast_to(scale, (32, 128))
        for j in range(parts):
            g = me ^ j
            unit = blocks[j] * scale
            munit[j, at, :] = unit
            anorm[g, at, :] = (unit * mgain[g] + mshift[g]).astype(BF16)

    arrived("out")
    mixed = sum(mm(anorm[g], wo[g * span : (g + 1) * span, :]) for g in range(parts))
    res[...] = x[...].astype(F32) + mixed + dvec[2:3, :]

    @tiles(32)
    def _(at, first):
        unit, scale = centred(res[at, :])
        runit[at, :] = unit
        rscale[at, :] = jnp.broadcast_to(scale, (32, 128))
        fnorm[at, :] = (unit * dvec[0:1, :] + dvec[1:2, :]).astype(BF16)

    kept = live_only(cot[...].astype(F32), 0, live)
    og[...] = kept.astype(BF16)
    dacc[24:32, :] += folded(kept)
    chunks = [slice(c, c + wide) for c in range(0, units, wide)]
    bands = [slice(r, r + band) for r in range(0, rows, band)]

    def lanes(chunk):
        return [slice(c, c + 128) for c in range(chunk.start, chunk.stop, 128)]

    def row_mean(parts_of):
        return [jnp.sum(v, axis=1, keepdims=True) / units for v in parts_of]

    arrived("fc1")
    arrived("fc2")
    total = [jnp.zeros((band, 128), F32) for _ in bands]
    pre[:, chunks[0]] = mm(fnorm[...], w1[:, chunks[0]])
    for index, chunk in enumerate(chunks):
        if index + 1 < len(chunks):
            after_it = chunks[index + 1]
            pre[:, after_it] = mm(fnorm[...], w1[:, after_it])
        for c in lanes(chunk):
            for b, r in enumerate(bands):
                v = pre[r, c] + fvec[1:2, c]
                below = 0.5 * (1.0 + lax.erf(v * 0.7071067811865476))
                a = v * below
                slope[r, c] = below + v * (jnp.exp(-0.5 * v * v) * 0.3989422804014327)
                act[r, c] = a
                total[b] = total[b] + a
    mean = row_mean(total)
    total = [jnp.zeros((band, 128), F32) for _ in bands]
    for chunk in chunks:
        hg[:, chunk] = mm_nt(og[...], w2[chunk, :])
        for c in lanes(chunk):
            for b, r in enumerate(bands):
                d = act[r, c] - mean[b]
                total[b] = total[b] + d * d
    scale = [lax.rsqrt(v + eps) for v in row_mean(total)]
    one = [jnp.zeros((band, 128), F32) for _ in bands]
    two = [jnp.zeros((band, 128), F32) for _ in bands]
    out = res[...] + dvec[3:4, :]
    for chunk in chunks:
        for c in lanes(chunk):
            gain = fvec[0:1, c]
            gain_sum, shift_sum = 0.0, 0.0
            for b, r in enumerate(bands):
                unit = (act[r, c] - mean[b]) * scale[b]
                act[r, c] = unit
                hid[r, c] = (unit * gain + fvec[2:3, c]).astype(BF16)
                grad = hg[r, c]
                gain_sum = gain_sum + folded(grad * unit)
                shift_sum = shift_sum + folded(grad)
                grad = grad * gain
                hg[r, c] = grad
                one[b] = one[b] + grad
                two[b] = two[b] + grad * unit
            facc[0:8, c] += gain_sum
            facc[16:24, c] += shift_sum
        if chunk.stop % width == 0:
            ready = slice(chunk.stop - width, chunk.stop)
            out = out + mm(hid[:, ready], w2[ready, :])
    block_out[...] = live_only(out, 0, live).astype(BF16)
    one, two = row_mean(one), row_mean(two)
    total = 0.0
    for chunk in chunks:
        quarter, base = chunk.start // width, chunk.start // width * width
        for c in lanes(chunk):
            low_sum = 0.0
            for b, r in enumerate(bands):
                grad = scale[b] * (hg[r, c] - one[b] - act[r, c] * two[b]) * slope[r, c]
                low = grad.astype(BF16)
                pg[place(quarter), r, c.start - base : c.stop - base] = low
                low_sum = low_sum + folded(low.astype(F32))
            facc[8:16, c] += low_sum
        if chunk.stop % width == 0:
            total = total + mm_nt(pg[place(quarter)], w1[:, base : base + width])
    fg = res
    fg[...] = total

    @tiles(32)
    def _(at, first):
        grad, unit = fg[at, :], runit[at, :]
        dacc[0:8, :] += folded(grad * unit)
        dacc[8:16, :] += folded(grad)
        total = og[at, :].astype(F32) + norm_back(grad * dvec[0:1, :], unit, rscale[at, 0:1])
        resid_grad[at, :] = total
        branch[at, :] = total.astype(BF16)
        dacc[16:24, :] += folded(total)

    for g in range(parts):
        ngs[g] = mm_nt(branch[...], wo[g * span : (g + 1) * span, :])

    @tiles(32)
    def _(at, first):
        one, two, scaled = 0.0, 0.0, []
        for j in range(parts):
            g = me ^ j
            grad, unit = ngs[g, at, :], munit[j, at, :]
            macc[g, 0:8, :] += folded(grad * unit)
            macc[g, 8:16, :] += folded(grad)
            m = grad * mgain[g]
            one = one + jnp.sum(m, axis=1, keepdims=True)
            two = two + jnp.sum(m * unit, axis=1, keepdims=True)
            scaled.append(m)
        one, two, scale = one / width, two / width, mscale[at, 0:1]
        for j in range(parts):
            value = scale * (scaled[j] - one - munit[j, at, :] * two)
            ob[j, at, :] = value.astype(BF16)

    for i in range(seqs):

        @pl.when(step == i)
        def _(i=i):
            for j in range(parts):
                mds[i * parts + j][...] = ob[j]

    @pl.when(step == seqs - 1)
    def _():
        for r in range(4):
            dsum[r : r + 1, :] = jnp.sum(dacc[8 * r : 8 * r + 8, :], axis=0, keepdims=True)
        for r in range(3):
            fsum[r : r + 1, :] = jnp.sum(facc[8 * r : 8 * r + 8, :], axis=0, keepdims=True)
        for g in range(parts):
            for r in range(2):
                part = macc[g, 8 * r : 8 * r + 8, :]
                msum[g, r : r + 1, :] = jnp.sum(part, axis=0, keepdims=True)


def token_stage(info, plan, sources, pieces, x, cot, dvec, mgain, mshift, fvec):
    seqs, rows, width = x.shape
    parts, units = len(pieces[0]), fvec.shape[1]
    span = width // parts
    shape = jax.ShapeDtypeStruct
    full = lambda *dims: pl.BlockSpec(dims, lambda i: (0,) * len(dims))
    by_seq = pl.BlockSpec((None, rows, width), lambda i: (i, 0, 0))
    by_rows = lambda cols: pl.BlockSpec((rows, cols), lambda i: (i, 0))
    n = seqs * rows
    outs = pl.pallas_call(
        functools.partial(token_kernel, plan, seqs, parts),
        grid=(seqs,),
        in_specs=[pl.BlockSpec(memory_space=pltpu.SMEM)]
        + [pl.BlockSpec(memory_space=pl.ANY)] * len(sources)
        + [full(rows, span)] * (seqs * parts)
        + [
            by_seq,
            by_seq,
            full(*dvec.shape),
            full(*mgain.shape),
            full(*mshift.shape),
            full(*fvec.shape),
        ],
        out_specs=[by_seq, by_seq]
        + [by_rows(width)] * 3
        + [pl.BlockSpec((parts, rows, span), lambda i: (0, i, 0))]
        + [by_rows(units)]
        + [pl.BlockSpec((units // width, rows, width), lambda i: (0, i, 0))]
        + [full(rows, span)] * (seqs * parts)
        + [full(4, width), full(parts, 2, span), full(3, units)],
        out_shape=[shape((seqs, rows, width), BF16), shape((seqs, rows, width), F32)]
        + [shape((n, width), BF16)] * 3
        + [shape((parts, n, span), BF16)]
        + [shape((n, units), BF16), shape((units // width, n, width), BF16)]
        + [shape((rows, span), BF16)] * (seqs * parts)
        + [shape((4, width), F32), shape((parts, 2, span), F32), shape((3, units), F32)],
        scratch_shapes=[
            pltpu.VMEM((width, width), BF16),
            pltpu.VMEM((width, units), BF16),
            pltpu.VMEM((units, width), BF16),
            pltpu.VMEM((parts, rows, span), BF16),
            pltpu.VMEM((parts, rows, span), F32),
            pltpu.VMEM((rows, 128), F32),
            pltpu.VMEM((rows, width), F32),
            pltpu.VMEM((rows, width), F32),
            pltpu.VMEM((rows, 128), F32),
        ]
        + [pltpu.VMEM((rows, units), F32)] * 4
        + [
            pltpu.VMEM((parts, rows, span), F32),
            pltpu.VMEM((32, width), F32),
            pltpu.VMEM((parts, 16, span), F32),
            pltpu.VMEM((24, units), F32),
            pltpu.SemaphoreType.DMA((len(plan),)),
        ],
        cost_estimate=pl.CostEstimate(
            flops=2 * n * width * (4 * units + 2 * width),
            bytes_accessed=2 * width * (2 * units + width) + 2 * n * (4 * units + 12 * width),
            transcendentals=2 * n * units,
        ),
        compiler_params=pltpu.CompilerParams(vmem_limit_bytes=60 << 20),
        name="token_stage",
    )(info, *sources, *[p for group in pieces for p in group], x, cot, dvec, mgain, mshift, fvec)
    outs = list(outs)
    mds = outs[8 : 8 + seqs * parts]
    mds = [mds[i * parts : (i + 1) * parts] for i in range(seqs)]
    return outs[:6], outs[6], outs[7], mds, outs[8 + seqs * parts :]


def swap(values, axis, mask):
    count = lax.axis_size(axis)
    return lax.ppermute(values, axis, [(i, i ^ mask) for i in range(count)])


def pick(values, index, axis):
    return lax.dynamic_index_in_dim(values, index, axis, keepdims=False)


def after(values, others):
    return lax.optimization_barrier((values, others))[0]


def spread_blocks(block, axis):
    count, me = lax.axis_size(axis), lax.axis_index(axis)
    held = {0: block}
    bit = count // 2
    while bit:
        held |= {mask | bit: swap(part, axis, bit) for mask, part in held.items()}
        bit //= 2
    whole = jnp.zeros((count,) + block.shape, block.dtype)
    for mask, part in held.items():
        whole = lax.dynamic_update_index_in_dim(whole, part, me ^ mask, 0)
    return whole


def sum_blocks(blocks, axis, kind):
    blocks = lax.all_to_all(blocks.astype(kind), axis, split_axis=0, concat_axis=0, tiled=True)
    return jnp.sum(blocks.astype(F32), axis=0)


def shards(
    activations,
    cotangent,
    lengths,
    w_qkv,
    w_out,
    w_fc1,
    w_fc2,
    d_gains,
    d_biases,
    ff_gain,
    ff_biases,
):
    seqs, rows, width = activations.shape
    parts, owners = lax.axis_size("seq"), lax.axis_size("fsdp")
    s = lax.axis_index("seq")
    core = s % 2
    span = width // parts
    own_rows = w_qkv.shape[0]
    own_ff = w_fc2.shape[0]
    half_ff, half_rows = own_ff // 2, own_rows // 2
    ff_half = half_ff * owners
    quarter = own_ff // own_rows

    own_w = pick(w_qkv.reshape(own_rows, 3, parts, span), s, 2).reshape(own_rows, 3 * span)
    ff_small = jnp.concatenate([ff_gain[:, None], ff_biases], axis=1).T.reshape(
        3 * quarter, own_rows
    )
    small = jnp.concatenate([d_gains.T, d_biases.T, ff_small], axis=0)
    kinds = small.shape[0]
    small_rows = 32
    small = jnp.pad(small, ((0, small_rows - kinds), (0, 3 * span - own_rows)))
    block = jnp.concatenate([own_w, small], axis=0)
    first = spread_blocks(block, "fsdp")
    my_qkv = first[:, :own_rows].reshape(width, 3 * span)
    small = first[:, own_rows : own_rows + kinds, :own_rows].astype(F32)
    d_small = small[:, :10].transpose(1, 0, 2).reshape(10, width)
    gains, biases = d_small[:3], d_small[3:]
    ff_small = small[:, 10:].reshape(owners, 3, own_ff).transpose(1, 0, 2).reshape(3, 2 * ff_half)

    w_out, w_fc1, w_fc2 = after((w_out, w_fc1, w_fc2), block)
    fc1_half = lax.dynamic_slice(w_fc1, (0, core * ff_half), (own_rows, ff_half))
    columns = range(0, ff_half, width)
    rest = jnp.concatenate(
        [pick(w_out.reshape(2, half_rows, width), core, 0)]
        + [fc1_half[:, c : c + width] for c in columns]
        + [pick(w_fc2.reshape(2, half_ff, width), core, 0)],
        axis=0,
    )
    rest_rows = rest.shape[0]
    rest = lax.all_gather(rest, "fsdp", axis=0, tiled=False)

    qkv_bias = pick(
        jnp.stack([biases[1], jnp.zeros_like(biases[1]), biases[2]]).reshape(3, parts, span), s, 1
    ).reshape(1, 3 * span)
    x_parts, mixed_parts, kept = [], [], []
    for i in range(seqs):
        mine = activations[i]
        across = swap(mine, "seq", 2)
        x_parts.append([mine, swap(mine, "seq", 1), across, swap(across, "seq", 1)])
    for i in range(seqs):
        if i > 0:
            x_parts[i] = after(x_parts[i], [kept[i - 1][2], mixed_parts[:-1]])
        normed, saved, outs, lse = attend_forward(
            s, lengths[i], x_parts[i], my_qkv, gains[0:1], biases[0:1], qkv_bias
        )
        kept.append((normed, saved, lse))
        mixed_parts.append([outs[0]] + [swap(outs[j], "seq", j) for j in range(1, parts)])
    rest = after(rest, [lse for _, _, lse in kept])
    rest_other = swap(rest, "seq", 1)

    plan, sources = [], [rest, rest_other]
    if half_rows % 16 == 0 and half_ff % 16 == 0:
        for src in range(2):
            for k in range(owners):
                plan.append((src, k, 0, half_rows, "out", k * own_rows, half_rows, 0, 0))
                for at, c in enumerate(columns):
                    start = half_rows + at * own_rows
                    plan.append((src, k, start, own_rows, "fc1", k * own_rows, 0, c, ff_half))
                start = rest_rows - half_ff
                plan.append((src, k, start, half_ff, "fc2", k * own_ff, half_ff, 0, 0))
    else:
        pair = [jnp.where(core == 0, rest, rest_other), jnp.where(core == 0, rest_other, rest)]
        blocks = [
            buf[:, half_rows + at * own_rows : half_rows + (at + 1) * own_rows].reshape(width, width)
            for buf in pair
            for at in range(len(columns))
        ]
        sources = [
            jnp.concatenate([buf[:, :half_rows] for buf in pair], axis=1).reshape(width, width),
            jnp.concatenate(blocks, axis=1),
            jnp.concatenate([buf[:, rest_rows - half_ff :] for buf in pair], axis=1).reshape(
                2 * ff_half, width
            ),
        ]
        names = ("out", "fc1", "fc2")
        plan = [(i, None, 0, sources[i].shape[0], names[i], 0, 0, 0, 0) for i in range(3)]
    info = jnp.concatenate([lengths, jnp.stack([s, core]).astype(jnp.int32)])
    dvec = jnp.stack([gains[2], biases[5], biases[4], biases[6]])
    tokens = token_stage(
        info,
        plan,
        sources,
        mixed_parts,
        activations,
        cotangent,
        dvec,
        gains[1].reshape(parts, 1, span),
        biases[3].reshape(parts, 1, span),
        ff_small,
    )
    (block_out, resid_grad, fnorm, branch, og, anorm), hid, pg, mixed_grads, sums = tokens
    dsum, msum, fsum = sums

    grad_out = jnp.einsum("gnk,nd->gkd", anorm, branch, preferred_element_type=F32)
    grad_out = grad_out.reshape(owners, 2, half_rows, width)
    grad_fc2 = mm_tn(hid, og).reshape(owners, 2, half_ff, width)
    mixed_grads = [[g[0]] + [swap(g[j], "seq", j) for j in range(1, parts)] for g in mixed_grads]
    grads = []
    for src in (1, 0):
        turn = core if src == 0 else 1 - core
        pieces = [pick(grad_out, turn, 1)]
        pieces += [
            mm_tn(fnorm, pg[len(columns) * src + at]).reshape(owners, own_rows, width)
            for at in range(len(columns))
        ]
        pieces.append(pick(grad_fc2, turn, 1))
        grads.append(jnp.concatenate([p.astype(BF16) for p in pieces], axis=1))
    rest_sum = grads[1].astype(F32) + swap(grads[0], "seq", 1).astype(F32)
    rest_sum = rest_sum.astype(BF16).reshape(owners * rest_rows, width)
    mixed_grads[0], rest_sum = lax.optimization_barrier((mixed_grads[0], rest_sum))
    rest_sum = lax.psum_scatter(rest_sum, "fsdp", scatter_dimension=0, tiled=True)

    grad_own, summed, head_sums, unit_sums, near = 0.0, [], 0.0, 0.0, []
    for i in range(seqs):
        pieces = mixed_grads[i]
        if i > 0:
            pieces = after(pieces, [sums, near[:-1]])
        normed, saved, lse = kept[i]
        dqkv, dns, sums, cols = attend_backward(
            s, lengths[i], x_parts[i], pieces, my_qkv, saved, lse
        )
        grad_own = grad_own + mm_tn(
            normed.reshape(parts * rows, width), dqkv.reshape(parts * rows, 3 * span)
        )
        unit_sums, head_sums = unit_sums + sums, head_sums + cols
        near.append([swap(dns[j], "seq", 1) for j in (1, 3)])
        far = (dns[2].astype(F32) + near[i][1].astype(F32)).astype(BF16)
        far = swap(far, "seq", 2).astype(F32)
        summed.append(dns[0].astype(F32) + near[i][0].astype(F32) + far)
    first_grad = jnp.stack(summed)
    first_unit, first_scale = centred(activations.astype(F32))
    input_grad = resid_grad + norm_back(first_grad * gains[0], first_unit, first_scale)

    def head_columns(values):
        blank = jnp.zeros((parts, span), F32)
        return lax.dynamic_update_slice(blank, values[None], (s, 0)).reshape(width)

    small_grads = jnp.stack(
        [
            unit_sums[0],
            msum[:, 0].reshape(width),
            dsum[0],
            unit_sums[1],
            head_columns(head_sums[0, :span]),
            head_columns(head_sums[0, 2 * span :]),
            msum[:, 1].reshape(width),
            dsum[2],
            dsum[1],
            dsum[3],
        ]
    )
    feed_grads = fsum.reshape(3, owners, quarter, own_rows)
    small_blocks = jnp.concatenate(
        [
            small_grads.reshape(10, owners, own_rows).transpose(1, 0, 2),
            feed_grads.transpose(1, 0, 2, 3).reshape(owners, 3 * quarter, own_rows),
        ],
        axis=1,
    )
    small_blocks = jnp.pad(small_blocks, ((0, 0), (0, small_rows - kinds), (0, 0)))
    small_sum = sum_blocks(small_blocks, "fsdp", F32)
    own_sum = sum_blocks(grad_own.reshape(owners, own_rows, 3 * span), "fsdp", BF16).astype(BF16)
    rest_sum = after(rest_sum, own_sum)
    rest_sum = rest_sum.astype(F32) + swap(rest_sum, "seq", 2).astype(F32)
    small_sum = [small_sum] + [swap(small_sum, "seq", j) for j in range(1, parts)]
    small_sum = (small_sum[0] + small_sum[1]) + (small_sum[2] + small_sum[3])
    feed_sum = small_sum[10:kinds].reshape(3, own_ff)
    group = jnp.stack([own_sum] + [swap(own_sum, "seq", j) for j in range(1, parts)])
    w_qkv_grad = jnp.concatenate(
        [
            pick(group, s ^ g, 0)[:, p * span : (p + 1) * span]
            for p in range(3)
            for g in range(parts)
        ],
        axis=1,
    ).astype(F32)

    other_sum = swap(rest_sum, "seq", 1)
    pair = [
        jnp.where(core == 0, rest_sum, other_sum),
        jnp.where(core == 0, other_sum, rest_sum),
    ]
    w_out_grad = jnp.concatenate([p[:half_rows] for p in pair], axis=0)
    w_fc1_grad = jnp.concatenate(
        [
            p[half_rows + at * own_rows : half_rows + (at + 1) * own_rows]
            for p in pair
            for at in range(len(columns))
        ],
        axis=1,
    )
    w_fc2_grad = jnp.concatenate([p[rest_rows - half_ff :] for p in pair], axis=0)
    return (
        block_out,
        input_grad,
        w_qkv_grad,
        w_out_grad,
        w_fc1_grad,
        w_fc2_grad,
        small_sum[:3].T,
        small_sum[3:10].T,
        feed_sum[0],
        feed_sum[1:].T,
    )


def solution(mesh):
    return jax.shard_map(
        shards,
        mesh=mesh,
        in_specs=(
            P("fsdp", "seq", None),
            P("fsdp", "seq", None),
            P("fsdp"),
            P("fsdp", None),
            P("fsdp", None),
            P("fsdp", None),
            P("fsdp", None),
            P("fsdp", None),
            P("fsdp", None),
            P("fsdp"),
            P("fsdp", None),
        ),
        out_specs=(
            P("fsdp", "seq", None),
            P("fsdp", "seq", None),
            P("fsdp", None),
            P("fsdp", None),
            P("fsdp", None),
            P("fsdp", None),
            P("fsdp", None),
            P("fsdp", None),
            P("fsdp"),
            P("fsdp", None),
        ),
        check_vma=False,
    )
```

```python
import functools

import jax
import jax.numpy as jnp
from jax import lax
from jax.experimental import pallas as pl
from jax.experimental.pallas import tpu as pltpu
from jax.sharding import PartitionSpec as P


HD = 64
SHORTEST = 512
eps = 1e-05
F32 = jnp.float32
BF16 = jnp.bfloat16
NT = (((1,), (1,)), ((), ()))


def mm(left, right):
    return jnp.dot(left, right, preferred_element_type=F32)


def mm_nt(left, right):
    return lax.dot_general(left, right, NT, preferred_element_type=F32)


def mm_tn(left, right):
    return lax.dot_general(left, right, (((0,), (0,)), ((), ())), preferred_element_type=F32)


def centred(values):
    center = values - jnp.mean(values, axis=-1, keepdims=True)
    spread = jnp.mean(center * center, axis=-1, keepdims=True)
    scale = lax.rsqrt(spread + eps)
    return center * scale, scale


def norm_back(grad, unit, scale):
    return scale * (
        grad
        - jnp.mean(grad, axis=-1, keepdims=True)
        - unit * jnp.mean(grad * unit, axis=-1, keepdims=True)
    )


def key_mask(block, live_rows):
    rows = lax.broadcasted_iota(jnp.int32, block.shape, 0)
    return jnp.where(rows < live_rows, block, -1e30)


def attend_kernel(parts, heads, rows, info, *refs):
    xs = refs[:parts]
    w, gain, shift, bias = refs[parts : parts + 4]
    stored = refs[parts + 4 : parts + 9]
    outs = refs[parts + 9 : 2 * parts + 9]
    lse, nrm, q, k, v, kt, vt, ot, sems = refs[2 * parts + 9 :]
    me, live = info[0], info[1]
    span = heads * HD
    for j in range(parts):
        g = me ^ j
        at = pl.ds(pl.multiple_of(g * rows, rows), rows)
        unit, _ = centred(xs[j][...].astype(F32))
        normed = (unit * gain[...] + shift[...]).astype(BF16)
        nrm[j] = normed
        qkv = mm(normed, w[...]) + bias[...]
        for h in range(heads):
            cols = slice(h * HD, (h + 1) * HD)
            kk = qkv[:, span + h * HD : span + (h + 1) * HD]
            vv = qkv[:, 2 * span + h * HD : 2 * span + (h + 1) * HD]
            q[h, at, :] = (qkv[:, cols].astype(BF16).astype(F32) * 0.125).astype(BF16)
            k[h, at, :] = kk.astype(BF16)
            v[h, at, :] = vv.astype(BF16)
            kt[h, g] = kk.T.astype(BF16)
            vt[h, g] = vv.T.astype(BF16)
    copies = [
        pltpu.make_async_copy(source, target, sems.at[index])
        for index, (source, target) in enumerate(zip((nrm, q, k, v, kt), stored))
    ]
    for copy in copies:
        copy.start()

    def variant(count):
        def step(t, carry):
            h, j = t // parts, t % parts
            g = me ^ j

            @pl.when(g < count)
            def _():
                qb = q[h, pl.ds(pl.multiple_of(g * rows, rows), rows), :]
                scores = [
                    mm_nt(k[h, c * rows : (c + 1) * rows, :], qb) for c in range(count)
                ]
                scores[-1] = key_mask(scores[-1], live - (count - 1) * rows)
                top = functools.reduce(
                    jnp.maximum, [jnp.max(s, axis=0, keepdims=True) for s in scores]
                )
                total, mixed = 0.0, 0.0
                for c in range(count):
                    e = jnp.exp(scores[c] - top)
                    total = total + jnp.sum(e, axis=0, keepdims=True)
                    mixed = mixed + mm(vt[h, c], e.astype(BF16))
                ot[t] = mixed / total
                lse[t] = jnp.broadcast_to(top + jnp.log(total), (8, rows))

            @pl.when(g >= count)
            def _():
                ot[t] = jnp.zeros((HD, rows), F32)
                lse[t] = jnp.zeros((8, rows), F32)

            return carry

        lax.fori_loop(0, heads * parts, step, 0)

    blocks = (live + rows - 1) // rows
    for count in range(max(1, SHORTEST // rows), parts + 1):
        pl.when(blocks == count)(functools.partial(variant, count))
    for j in range(parts):
        stacked = jnp.concatenate([ot[h * parts + j] for h in range(heads)], axis=0)
        outs[j][...] = stacked.T.astype(BF16)
    for copy in copies:
        copy.wait()


def whole(*arrays):
    return [pl.BlockSpec(a.shape, lambda i, n=a.ndim: (0,) * n) for a in arrays]


def attend_forward(place, live, xs, w, gain, shift, bias):
    parts, (rows, width) = len(xs), xs[0].shape
    span = w.shape[1] // 3
    heads, full = span // HD, parts * rows
    shape = jax.ShapeDtypeStruct
    kept = [(parts, rows, width)] + [(heads, full, HD)] * 3 + [(heads, parts, HD, rows)]
    outs_like, lse_like = shape((rows, span), BF16), shape((heads * parts, 8, rows), F32)
    outs = pl.pallas_call(
        functools.partial(attend_kernel, parts, heads, rows),
        grid=(1,),
        in_specs=[pl.BlockSpec(memory_space=pltpu.SMEM)] + whole(*xs, w, gain, shift, bias),
        out_specs=[pl.BlockSpec(memory_space=pltpu.HBM)] * 5
        + whole(*[outs_like] * parts, lse_like),
        out_shape=[shape(dims, BF16) for dims in kept]
        + [outs_like] * parts
        + [lse_like],
        scratch_shapes=[pltpu.VMEM(dims, BF16) for dims in kept]
        + [
            pltpu.VMEM((heads, parts, HD, rows), BF16),
            pltpu.VMEM((heads * parts, HD, rows), F32),
            pltpu.SemaphoreType.DMA((5,)),
        ],
        cost_estimate=pl.CostEstimate(
            flops=2 * full * width * 3 * span + 4 * full * full * span,
            bytes_accessed=2 * (2 * full * width + width * 3 * span + 6 * full * span),
            transcendentals=heads * full * full,
        ),
        compiler_params=pltpu.CompilerParams(vmem_limit_bytes=60 << 20),
        name="attend_forward",
    )(jnp.stack([place, live]), *xs, w, gain, shift, bias)
    return outs[0], outs[1:5], outs[5 : 5 + parts], outs[5 + parts]


def attend_back_kernel(parts, heads, rows, info, *refs):
    xs, grads = refs[:parts], refs[parts : 2 * parts]
    w, q, k, v, kt, lse = refs[2 * parts : 2 * parts + 6]
    dqkv = refs[2 * parts + 6]
    dns = refs[2 * parts + 7 : 3 * parts + 7]
    sums, cols = refs[3 * parts + 7 : 3 * parts + 9]
    do, dk, dv, dqt = refs[3 * parts + 9 :]
    me, live = info[0], info[1]
    for j in range(parts):
        block = grads[j][...].astype(F32)
        for h in range(heads):
            do[h * parts + j] = block[:, h * HD : (h + 1) * HD].astype(BF16)
    dk[...] = jnp.zeros_like(dk)
    dv[...] = jnp.zeros_like(dv)

    def variant(count):
        def step(t, carry):
            h, j = t // parts, t % parts
            g = me ^ j

            @pl.when(g < count)
            def _():
                qb = q[h, pl.ds(pl.multiple_of(g * rows, rows), rows), :]
                dob = do[t]
                shift = lse[t][0:1, :]
                probs, dps, inner = [], [], 0.0
                for c in range(count):
                    span = slice(c * rows, (c + 1) * rows)
                    s = mm_nt(k[h, span, :], qb)
                    if c == count - 1:
                        s = key_mask(s, live - c * rows)
                    p = jnp.exp(s - shift)
                    dp = mm_nt(v[h, span, :], dob)
                    inner = inner + jnp.sum(p * dp, axis=0, keepdims=True)
                    dv[h, c] += mm(p.astype(BF16), dob)
                    probs.append(p)
                    dps.append(dp)
                dq = 0.0
                for c in range(count):
                    ds = (probs[c] * (dps[c] - inner)).astype(BF16)
                    dk[h, c] += mm(ds, qb)
                    dq = dq + mm(kt[h, c], ds)
                dqt[t] = dq * 0.125

            @pl.when(g >= count)
            def _():
                dqt[t] = jnp.zeros((HD, rows), F32)

            return carry

        lax.fori_loop(0, heads * parts, step, 0)

    blocks = (live + rows - 1) // rows
    for count in range(max(1, SHORTEST // rows), parts + 1):
        pl.when(blocks == count)(functools.partial(variant, count))
    shift_sum, gain_sum, col_sum = 0.0, 0.0, 0.0
    for j in range(parts):
        g = me ^ j
        dq = jnp.concatenate([dqt[h * parts + j] for h in range(heads)], axis=0).T
        pieces = [dq] + [dk[h, g] for h in range(heads)] + [dv[h, g] for h in range(heads)]
        block = jnp.concatenate(pieces, axis=1).astype(BF16)
        dqkv[j] = block
        col_sum = col_sum + jnp.sum(block.astype(F32), axis=0, keepdims=True)
        dn = mm_nt(block, w[...])
        unit, _ = centred(xs[j][...].astype(F32))
        shift_sum = shift_sum + jnp.sum(dn, axis=0, keepdims=True)
        gain_sum = gain_sum + jnp.sum(dn * unit, axis=0, keepdims=True)
        dns[j][...] = dn.astype(BF16)
    sums[0:1, :] = gain_sum
    sums[1:2, :] = shift_sum
    cols[0:1, :] = col_sum


def attend_backward(place, live, xs, grads, w, saved, lse):
    parts, (rows, width) = len(xs), xs[0].shape
    span = w.shape[1] // 3
    heads, full = span // HD, parts * rows
    shape = jax.ShapeDtypeStruct
    out_shape = [
        shape((parts, rows, 3 * span), BF16),
        *[shape((rows, width), BF16)] * parts,
        shape((2, width), F32),
        shape((1, 3 * span), F32),
    ]
    outs = pl.pallas_call(
        functools.partial(attend_back_kernel, parts, heads, rows),
        grid=(1,),
        in_specs=[pl.BlockSpec(memory_space=pltpu.SMEM)] + whole(*xs, *grads, w, *saved, lse),
        out_specs=whole(*out_shape),
        out_shape=out_shape,
        scratch_shapes=[
            pltpu.VMEM((heads * parts, rows, HD), BF16),
            pltpu.VMEM((heads, parts, rows, HD), F32),
            pltpu.VMEM((heads, parts, rows, HD), F32),
            pltpu.VMEM((heads * parts, HD, rows), F32),
        ],
        cost_estimate=pl.CostEstimate(
            flops=2 * full * width * 3 * span + 10 * full * full * span,
            bytes_accessed=2 * (3 * full * width + width * 3 * span + 9 * full * span),
            transcendentals=heads * full * full,
        ),
        compiler_params=pltpu.CompilerParams(vmem_limit_bytes=60 << 20),
        name="attend_backward",
    )(jnp.stack([place, live]), *xs, *grads, w, *saved, lse)
    return outs[0], outs[1 : 1 + parts], outs[1 + parts], outs[2 + parts]


def live_only(values, first, live):
    rows = first + lax.broadcasted_iota(jnp.int32, values.shape, 0)
    return jnp.where(rows < live, values, jnp.zeros_like(values))


def folded(values):
    return functools.reduce(
        jnp.add, [values[r : r + 8] for r in range(0, values.shape[0], 8)]
    )


def token_kernel(plan, seqs, parts, info, *refs):
    refs = list(refs)
    take = lambda count: [refs.pop(0) for _ in range(count)]
    sources = take(max(p[0] for p in plan) + 1)
    pieces = take(seqs * parts)
    x, cot, dvec, mgain, mshift, fvec = take(6)
    block_out, resid_grad, fnorm, branch, og, anorm = take(6)
    hid, pg = take(2)
    mds = take(seqs * parts)
    dsum, msum, fsum = take(3)
    wo, w1, w2, ob, munit, mscale, res, runit, rscale = take(9)
    pre, slope, act, hg, ngs, dacc, macc, facc, sems = take(9)
    step = pl.program_id(0)
    me, core = info[seqs], info[seqs + 1]
    live = info[step] - me * x.shape[0]
    rows, width = x.shape
    span, units = width // parts, pre.shape[1]
    band, wide = 64, 256
    quarters = units // width

    def place(quarter):
        turned = quarter + quarters // 2 * core
        return jnp.where(turned >= quarters, turned - quarters, turned)

    targets = {"out": wo, "fc1": w1, "fc2": w2}

    def copies(wanted):
        for index, (src, k, start, count, name, at, at_step, col, col_step) in enumerate(plan):
            if name not in wanted:
                continue
            source = sources[src] if k is None else sources[src].at[k]
            target = targets[name]
            turn = core if src == 0 else 1 - core
            if at_step:
                at = pl.multiple_of(at + at_step * turn, 16)
            if col_step:
                col = pl.multiple_of(col + col_step * turn, 128)
            target = target.at[pl.ds(at, count), pl.ds(col, source.shape[1])]
            yield pltpu.make_async_copy(source.at[pl.ds(start, count)], target, sems.at[index])

    def arrived(name):
        @pl.when(step == 0)
        def _():
            for copy in copies((name,)):
                copy.wait()

    @pl.when(step == 0)
    def _():
        for copy in copies(("out", "fc1", "fc2")):
            copy.start()
        dacc[...] = jnp.zeros_like(dacc)
        macc[...] = jnp.zeros_like(macc)
        facc[...] = jnp.zeros_like(facc)

    for i in range(seqs):

        @pl.when(step == i)
        def _(i=i):
            for j in range(parts):
                ob[j] = pieces[i * parts + j][...]

    def tiles(size):
        def decorate(body):
            def run(t, carry):
                body(pl.ds(pl.multiple_of(t * size, size), size), t * size)
                return carry

            lax.fori_loop(0, rows // size, run, 0)

        return decorate

    @tiles(32)
    def _(at, first):
        blocks = [ob[j, at, :].astype(F32) for j in range(parts)]
        mean = sum(jnp.sum(b, axis=1, keepdims=True) for b in blocks) / width
        blocks = [b - mean for b in blocks]
        var = sum(jnp.sum(b * b, axis=1, keepdims=True) for b in blocks) / width
        scale = lax.rsqrt(var + eps)
        mscale[at, :] = jnp.broadcast_to(scale, (32, 128))
        for j in range(parts):
            g = me ^ j
            unit = blocks[j] * scale
            munit[j, at, :] = unit
            anorm[g, at, :] = (unit * mgain[g] + mshift[g]).astype(BF16)

    arrived("out")
    mixed = sum(mm(anorm[g], wo[g * span : (g + 1) * span, :]) for g in range(parts))
    res[...] = x[...].astype(F32) + mixed + dvec[2:3, :]

    @tiles(32)
    def _(at, first):
        unit, scale = centred(res[at, :])
        runit[at, :] = unit
        rscale[at, :] = jnp.broadcast_to(scale, (32, 128))
        fnorm[at, :] = (unit * dvec[0:1, :] + dvec[1:2, :]).astype(BF16)

    kept = live_only(cot[...].astype(F32), 0, live)
    og[...] = kept.astype(BF16)
    dacc[24:32, :] += folded(kept)
    chunks = [slice(c, c + wide) for c in range(0, units, wide)]
    bands = [slice(r, r + band) for r in range(0, rows, band)]

    def lanes(chunk):
        return [slice(c, c + 128) for c in range(chunk.start, chunk.stop, 128)]

    def row_mean(parts_of):
        return [jnp.sum(v, axis=1, keepdims=True) / units for v in parts_of]

    arrived("fc1")
    arrived("fc2")
    total = [jnp.zeros((band, 128), F32) for _ in bands]
    pre[:, chunks[0]] = mm(fnorm[...], w1[:, chunks[0]])
    for index, chunk in enumerate(chunks):
        if index + 1 < len(chunks):
            after_it = chunks[index + 1]
            pre[:, after_it] = mm(fnorm[...], w1[:, after_it])
        for c in lanes(chunk):
            for b, r in enumerate(bands):
                v = pre[r, c] + fvec[1:2, c]
                below = 0.5 * (1.0 + lax.erf(v * 0.7071067811865476))
                a = v * below
                slope[r, c] = below + v * (jnp.exp(-0.5 * v * v) * 0.3989422804014327)
                act[r, c] = a
                total[b] = total[b] + a
    mean = row_mean(total)
    total = [jnp.zeros((band, 128), F32) for _ in bands]
    for chunk in chunks:
        hg[:, chunk] = mm_nt(og[...], w2[chunk, :])
        for c in lanes(chunk):
            for b, r in enumerate(bands):
                d = act[r, c] - mean[b]
                total[b] = total[b] + d * d
    scale = [lax.rsqrt(v + eps) for v in row_mean(total)]
    one = [jnp.zeros((band, 128), F32) for _ in bands]
    two = [jnp.zeros((band, 128), F32) for _ in bands]
    out = res[...] + dvec[3:4, :]
    for chunk in chunks:
        for c in lanes(chunk):
            gain = fvec[0:1, c]
            gain_sum, shift_sum = 0.0, 0.0
            for b, r in enumerate(bands):
                unit = (act[r, c] - mean[b]) * scale[b]
                act[r, c] = unit
                hid[r, c] = (unit * gain + fvec[2:3, c]).astype(BF16)
                grad = hg[r, c]
                gain_sum = gain_sum + folded(grad * unit)
                shift_sum = shift_sum + folded(grad)
                grad = grad * gain
                hg[r, c] = grad
                one[b] = one[b] + grad
                two[b] = two[b] + grad * unit
            facc[0:8, c] += gain_sum
            facc[16:24, c] += shift_sum
        if chunk.stop % width == 0:
            ready = slice(chunk.stop - width, chunk.stop)
            out = out + mm(hid[:, ready], w2[ready, :])
    block_out[...] = live_only(out, 0, live).astype(BF16)
    one, two = row_mean(one), row_mean(two)
    total = 0.0
    for chunk in chunks:
        quarter, base = chunk.start // width, chunk.start // width * width
        for c in lanes(chunk):
            low_sum = 0.0
            for b, r in enumerate(bands):
                grad = scale[b] * (hg[r, c] - one[b] - act[r, c] * two[b]) * slope[r, c]
                low = grad.astype(BF16)
                pg[place(quarter), r, c.start - base : c.stop - base] = low
                low_sum = low_sum + folded(low.astype(F32))
            facc[8:16, c] += low_sum
        if chunk.stop % width == 0:
            total = total + mm_nt(pg[place(quarter)], w1[:, base : base + width])
    fg = res
    fg[...] = total

    @tiles(32)
    def _(at, first):
        grad, unit = fg[at, :], runit[at, :]
        dacc[0:8, :] += folded(grad * unit)
        dacc[8:16, :] += folded(grad)
        total = og[at, :].astype(F32) + norm_back(grad * dvec[0:1, :], unit, rscale[at, 0:1])
        resid_grad[at, :] = total
        branch[at, :] = total.astype(BF16)
        dacc[16:24, :] += folded(total)

    for g in range(parts):
        ngs[g] = mm_nt(branch[...], wo[g * span : (g + 1) * span, :])

    @tiles(32)
    def _(at, first):
        one, two, scaled = 0.0, 0.0, []
        for j in range(parts):
            g = me ^ j
            grad, unit = ngs[g, at, :], munit[j, at, :]
            macc[g, 0:8, :] += folded(grad * unit)
            macc[g, 8:16, :] += folded(grad)
            m = grad * mgain[g]
            one = one + jnp.sum(m, axis=1, keepdims=True)
            two = two + jnp.sum(m * unit, axis=1, keepdims=True)
            scaled.append(m)
        one, two, scale = one / width, two / width, mscale[at, 0:1]
        for j in range(parts):
            value = scale * (scaled[j] - one - munit[j, at, :] * two)
            ob[j, at, :] = value.astype(BF16)

    for i in range(seqs):

        @pl.when(step == i)
        def _(i=i):
            for j in range(parts):
                mds[i * parts + j][...] = ob[j]

    @pl.when(step == seqs - 1)
    def _():
        for r in range(4):
            dsum[r : r + 1, :] = jnp.sum(dacc[8 * r : 8 * r + 8, :], axis=0, keepdims=True)
        for r in range(3):
            fsum[r : r + 1, :] = jnp.sum(facc[8 * r : 8 * r + 8, :], axis=0, keepdims=True)
        for g in range(parts):
            for r in range(2):
                part = macc[g, 8 * r : 8 * r + 8, :]
                msum[g, r : r + 1, :] = jnp.sum(part, axis=0, keepdims=True)


def token_stage(info, plan, sources, pieces, x, cot, dvec, mgain, mshift, fvec):
    seqs, rows, width = x.shape
    parts, units = len(pieces[0]), fvec.shape[1]
    span = width // parts
    shape = jax.ShapeDtypeStruct
    full = lambda *dims: pl.BlockSpec(dims, lambda i: (0,) * len(dims))
    by_seq = pl.BlockSpec((None, rows, width), lambda i: (i, 0, 0))
    by_rows = lambda cols: pl.BlockSpec((rows, cols), lambda i: (i, 0))
    n = seqs * rows
    outs = pl.pallas_call(
        functools.partial(token_kernel, plan, seqs, parts),
        grid=(seqs,),
        in_specs=[pl.BlockSpec(memory_space=pltpu.SMEM)]
        + [pl.BlockSpec(memory_space=pl.ANY)] * len(sources)
        + [full(rows, span)] * (seqs * parts)
        + [
            by_seq,
            by_seq,
            full(*dvec.shape),
            full(*mgain.shape),
            full(*mshift.shape),
            full(*fvec.shape),
        ],
        out_specs=[by_seq, by_seq]
        + [by_rows(width)] * 3
        + [pl.BlockSpec((parts, rows, span), lambda i: (0, i, 0))]
        + [by_rows(units)]
        + [pl.BlockSpec((units // width, rows, width), lambda i: (0, i, 0))]
        + [full(rows, span)] * (seqs * parts)
        + [full(4, width), full(parts, 2, span), full(3, units)],
        out_shape=[shape((seqs, rows, width), BF16), shape((seqs, rows, width), F32)]
        + [shape((n, width), BF16)] * 3
        + [shape((parts, n, span), BF16)]
        + [shape((n, units), BF16), shape((units // width, n, width), BF16)]
        + [shape((rows, span), BF16)] * (seqs * parts)
        + [shape((4, width), F32), shape((parts, 2, span), F32), shape((3, units), F32)],
        scratch_shapes=[
            pltpu.VMEM((width, width), BF16),
            pltpu.VMEM((width, units), BF16),
            pltpu.VMEM((units, width), BF16),
            pltpu.VMEM((parts, rows, span), BF16),
            pltpu.VMEM((parts, rows, span), F32),
            pltpu.VMEM((rows, 128), F32),
            pltpu.VMEM((rows, width), F32),
            pltpu.VMEM((rows, width), F32),
            pltpu.VMEM((rows, 128), F32),
        ]
        + [pltpu.VMEM((rows, units), F32)] * 4
        + [
            pltpu.VMEM((parts, rows, span), F32),
            pltpu.VMEM((32, width), F32),
            pltpu.VMEM((parts, 16, span), F32),
            pltpu.VMEM((24, units), F32),
            pltpu.SemaphoreType.DMA((len(plan),)),
        ],
        cost_estimate=pl.CostEstimate(
            flops=2 * n * width * (4 * units + 2 * width),
            bytes_accessed=2 * width * (2 * units + width) + 2 * n * (4 * units + 12 * width),
            transcendentals=2 * n * units,
        ),
        compiler_params=pltpu.CompilerParams(vmem_limit_bytes=60 << 20),
        name="token_stage",
    )(info, *sources, *[p for group in pieces for p in group], x, cot, dvec, mgain, mshift, fvec)
    outs = list(outs)
    mds = outs[8 : 8 + seqs * parts]
    mds = [mds[i * parts : (i + 1) * parts] for i in range(seqs)]
    return outs[:6], outs[6], outs[7], mds, outs[8 + seqs * parts :]


def swap(values, axis, mask):
    count = lax.axis_size(axis)
    return lax.ppermute(values, axis, [(i, i ^ mask) for i in range(count)])


def pick(values, index, axis):
    return lax.dynamic_index_in_dim(values, index, axis, keepdims=False)


def after(values, others):
    return lax.optimization_barrier((values, others))[0]


def spread_blocks(block, axis):
    count, me = lax.axis_size(axis), lax.axis_index(axis)
    held = {0: block}
    bit = count // 2
    while bit:
        held |= {mask | bit: swap(part, axis, bit) for mask, part in held.items()}
        bit //= 2
    whole = jnp.zeros((count,) + block.shape, block.dtype)
    for mask, part in held.items():
        whole = lax.dynamic_update_index_in_dim(whole, part, me ^ mask, 0)
    return whole


def sum_blocks(blocks, small, axis):
    count, mine = lax.axis_size(axis), lax.axis_index(axis) % 2
    sums = []
    for values, kind in ((blocks, BF16), (small, F32)):
        pairs = values.reshape((count // 2, 2) + values.shape[1:])
        sent = swap(pick(pairs, 1 - mine, 1).astype(kind), axis, 1)
        sums.append((pick(pairs, mine, 1) + sent.astype(F32)).astype(BF16))
    sums[1] = jnp.pad(sums[1], ((0, 0), (0, 0), (0, blocks.shape[2] - small.shape[2])))
    groups = [list(range(g, count, 2)) for g in range(2)]
    blocks = lax.all_to_all(
        jnp.concatenate(sums, axis=1),
        axis,
        split_axis=0,
        concat_axis=0,
        axis_index_groups=groups,
        tiled=True,
    )
    return jnp.sum(blocks.astype(F32), axis=0)


def shards(
    activations,
    cotangent,
    lengths,
    w_qkv,
    w_out,
    w_fc1,
    w_fc2,
    d_gains,
    d_biases,
    ff_gain,
    ff_biases,
):
    seqs, rows, width = activations.shape
    parts, owners = lax.axis_size("seq"), lax.axis_size("fsdp")
    s = lax.axis_index("seq")
    core = s % 2
    span = width // parts
    own_rows = w_qkv.shape[0]
    own_ff = w_fc2.shape[0]
    half_ff, half_rows = own_ff // 2, own_rows // 2
    ff_half = half_ff * owners
    quarter = own_ff // own_rows

    fc1_half = lax.dynamic_slice(w_fc1, (0, core * ff_half), (own_rows, ff_half))
    columns = range(0, ff_half, width)
    rest = jnp.concatenate(
        [pick(w_out.reshape(2, half_rows, width), core, 0)]
        + [fc1_half[:, c : c + width] for c in columns]
        + [pick(w_fc2.reshape(2, half_ff, width), core, 0)],
        axis=0,
    )
    rest_rows = rest.shape[0]
    w_qkv = after(w_qkv, rest)
    rest = lax.all_gather(rest, "fsdp", axis=0, tiled=False)

    own_w = pick(w_qkv.reshape(own_rows, 3, parts, span), s, 2).reshape(own_rows, 3 * span)
    ff_small = jnp.concatenate([ff_gain[:, None], ff_biases], axis=1).T.reshape(
        3 * quarter, own_rows
    )
    small = jnp.concatenate([d_gains.T, d_biases.T, ff_small], axis=0)
    kinds = small.shape[0]
    small_rows = 32
    small = jnp.pad(small, ((0, small_rows - kinds), (0, 3 * span - own_rows)))
    block = jnp.concatenate([own_w, small], axis=0)
    first = spread_blocks(block, "fsdp")
    my_qkv = first[:, :own_rows].reshape(width, 3 * span)
    small = first[:, own_rows : own_rows + kinds, :own_rows].astype(F32)
    d_small = small[:, :10].transpose(1, 0, 2).reshape(10, width)
    gains, biases = d_small[:3], d_small[3:]
    ff_small = small[:, 10:].reshape(owners, 3, own_ff).transpose(1, 0, 2).reshape(3, 2 * ff_half)

    qkv_bias = pick(
        jnp.stack([biases[1], jnp.zeros_like(biases[1]), biases[2]]).reshape(3, parts, span), s, 1
    ).reshape(1, 3 * span)
    x_parts, mixed_parts, kept = [], [], []
    for i in range(seqs):
        mine = activations[i]
        across = swap(mine, "seq", 2)
        x_parts.append([mine, swap(mine, "seq", 1), across, swap(across, "seq", 1)])
    for i in range(seqs):
        if i > 0:
            x_parts[i] = after(x_parts[i], [kept[i - 1][2], mixed_parts[:-1]])
        normed, saved, outs, lse = attend_forward(
            s, lengths[i], x_parts[i], my_qkv, gains[0:1], biases[0:1], qkv_bias
        )
        kept.append((normed, saved, lse))
        mixed_parts.append([outs[0]] + [swap(outs[j], "seq", j) for j in range(1, parts)])
    rest = after(rest, [lse for _, _, lse in kept])
    rest_other = swap(rest, "seq", 1)

    plan, sources = [], [rest, rest_other]
    if half_rows % 16 == 0 and half_ff % 16 == 0:
        for src in range(2):
            for k in range(owners):
                plan.append((src, k, 0, half_rows, "out", k * own_rows, half_rows, 0, 0))
                for at, c in enumerate(columns):
                    start = half_rows + at * own_rows
                    plan.append((src, k, start, own_rows, "fc1", k * own_rows, 0, c, ff_half))
                start = rest_rows - half_ff
                plan.append((src, k, start, half_ff, "fc2", k * own_ff, half_ff, 0, 0))
    else:
        pair = [jnp.where(core == 0, rest, rest_other), jnp.where(core == 0, rest_other, rest)]
        blocks = [
            buf[:, half_rows + at * own_rows : half_rows + (at + 1) * own_rows].reshape(width, width)
            for buf in pair
            for at in range(len(columns))
        ]
        sources = [
            jnp.concatenate([buf[:, :half_rows] for buf in pair], axis=1).reshape(width, width),
            jnp.concatenate(blocks, axis=1),
            jnp.concatenate([buf[:, rest_rows - half_ff :] for buf in pair], axis=1).reshape(
                2 * ff_half, width
            ),
        ]
        names = ("out", "fc1", "fc2")
        plan = [(i, None, 0, sources[i].shape[0], names[i], 0, 0, 0, 0) for i in range(3)]
    info = jnp.concatenate([lengths, jnp.stack([s, core]).astype(jnp.int32)])
    dvec = jnp.stack([gains[2], biases[5], biases[4], biases[6]])
    tokens = token_stage(
        info,
        plan,
        sources,
        mixed_parts,
        activations,
        cotangent,
        dvec,
        gains[1].reshape(parts, 1, span),
        biases[3].reshape(parts, 1, span),
        ff_small,
    )
    (block_out, resid_grad, fnorm, branch, og, anorm), hid, pg, mixed_grads, sums = tokens
    dsum, msum, fsum = sums

    grad_out = jnp.einsum("gnk,nd->gkd", anorm, branch, preferred_element_type=F32)
    grad_out = grad_out.reshape(owners, 2, half_rows, width)
    grad_fc2 = mm_tn(hid, og).reshape(owners, 2, half_ff, width)
    mixed_grads = [[g[0]] + [swap(g[j], "seq", j) for j in range(1, parts)] for g in mixed_grads]
    grads = []
    for src in (1, 0):
        turn = core if src == 0 else 1 - core
        pieces = [pick(grad_out, turn, 1)]
        pieces += [
            mm_tn(fnorm, pg[len(columns) * src + at]).reshape(owners, own_rows, width)
            for at in range(len(columns))
        ]
        pieces.append(pick(grad_fc2, turn, 1))
        grads.append(jnp.concatenate([p.astype(BF16) for p in pieces], axis=1))
    other_grads = swap(grads[0], "seq", 1)
    rest_sum = (grads[1].astype(F32) + other_grads.astype(F32)).astype(BF16)
    rest_sum = rest_sum.reshape(owners * rest_rows, width)
    mixed_grads[0], rest_sum = lax.optimization_barrier((mixed_grads[0], rest_sum))
    rest_sum = lax.psum_scatter(rest_sum, "fsdp", scatter_dimension=0, tiled=True)

    grad_own, summed, head_sums, unit_sums, near = 0.0, [], 0.0, 0.0, []
    for i in range(seqs):
        pieces = mixed_grads[i]
        if i > 0:
            pieces = after(pieces, [sums, near[:-1]])
        normed, saved, lse = kept[i]
        dqkv, dns, sums, cols = attend_backward(
            s, lengths[i], x_parts[i], pieces, my_qkv, saved, lse
        )
        grad_own = grad_own + mm_tn(
            normed.reshape(parts * rows, width), dqkv.reshape(parts * rows, 3 * span)
        )
        unit_sums, head_sums = unit_sums + sums, head_sums + cols
        near.append([swap(dns[j], "seq", 1) for j in (1, 3)])
        far = (dns[2].astype(F32) + near[i][1].astype(F32)).astype(BF16)
        far = swap(far, "seq", 2).astype(F32)
        summed.append(dns[0].astype(F32) + near[i][0].astype(F32) + far)
    first_grad = jnp.stack(summed)
    first_unit, first_scale = centred(activations.astype(F32))
    input_grad = resid_grad + norm_back(first_grad * gains[0], first_unit, first_scale)

    def head_columns(values):
        blank = jnp.zeros((parts, span), F32)
        return lax.dynamic_update_slice(blank, values[None], (s, 0)).reshape(width)

    small_grads = jnp.stack(
        [
            unit_sums[0],
            msum[:, 0].reshape(width),
            dsum[0],
            unit_sums[1],
            head_columns(head_sums[0, :span]),
            head_columns(head_sums[0, 2 * span :]),
            msum[:, 1].reshape(width),
            dsum[2],
            dsum[1],
            dsum[3],
        ]
    )
    feed_grads = fsum.reshape(3, owners, quarter, own_rows)
    small_blocks = jnp.concatenate(
        [
            small_grads.reshape(10, owners, own_rows).transpose(1, 0, 2),
            feed_grads.transpose(1, 0, 2, 3).reshape(owners, 3 * quarter, own_rows),
        ],
        axis=1,
    )
    small_blocks = jnp.pad(small_blocks, ((0, 0), (0, small_rows - kinds), (0, 0)))
    own_sum = sum_blocks(
        grad_own.reshape(owners, own_rows, 3 * span), small_blocks, "fsdp"
    )
    small_sum = own_sum[own_rows:, :own_rows]
    own_sum = own_sum[:own_rows].astype(BF16)
    across = swap(rest_sum, "seq", 2)
    small_sum = [small_sum] + [swap(small_sum, "seq", j) for j in range(1, parts)]
    small_sum = (small_sum[0] + small_sum[1]) + (small_sum[2] + small_sum[3])
    feed_sum = small_sum[10:kinds].reshape(3, own_ff)
    small_outs = (small_sum[:3].T, small_sum[3:10].T, feed_sum[0], feed_sum[1:].T)
    group = jnp.stack([own_sum] + [swap(own_sum, "seq", j) for j in range(1, parts)])
    w_qkv_grad = jnp.concatenate(
        [
            pick(group, s ^ g, 0)[:, p * span : (p + 1) * span]
            for p in range(3)
            for g in range(parts)
        ],
        axis=1,
    ).astype(F32)

    across = after(across, [w_qkv_grad, small_outs, input_grad])
    rest_sum = rest_sum.astype(F32) + across.astype(F32)
    other_sum = swap(rest_sum, "seq", 1)
    pair = [
        jnp.where(core == 0, rest_sum, other_sum),
        jnp.where(core == 0, other_sum, rest_sum),
    ]
    w_out_grad = jnp.concatenate([p[:half_rows] for p in pair], axis=0)
    w_fc1_grad = jnp.concatenate(
        [
            p[half_rows + at * own_rows : half_rows + (at + 1) * own_rows]
            for p in pair
            for at in range(len(columns))
        ],
        axis=1,
    )
    w_fc2_grad = jnp.concatenate([p[rest_rows - half_ff :] for p in pair], axis=0)
    return (
        block_out,
        input_grad,
        w_qkv_grad,
        w_out_grad,
        w_fc1_grad,
        w_fc2_grad,
        *small_outs,
    )


def solution(mesh):
    return jax.shard_map(
        shards,
        mesh=mesh,
        in_specs=(
            P("fsdp", "seq", None),
            P("fsdp", "seq", None),
            P("fsdp"),
            P("fsdp", None),
            P("fsdp", None),
            P("fsdp", None),
            P("fsdp", None),
            P("fsdp", None),
            P("fsdp", None),
            P("fsdp"),
            P("fsdp", None),
        ),
        out_specs=(
            P("fsdp", "seq", None),
            P("fsdp", "seq", None),
            P("fsdp", None),
            P("fsdp", None),
            P("fsdp", None),
            P("fsdp", None),
            P("fsdp", None),
            P("fsdp", None),
            P("fsdp"),
            P("fsdp", None),
        ),
        check_vma=False,
    )
```

```python
import functools

import jax
import jax.numpy as jnp
from jax import lax
from jax.experimental import pallas as pl
from jax.experimental.pallas import tpu as pltpu
from jax.sharding import PartitionSpec as P


HD = 64
SHORTEST = 512
eps = 1e-05
F32 = jnp.float32
BF16 = jnp.bfloat16
NT = (((1,), (1,)), ((), ()))


def mm(left, right):
    return jnp.dot(left, right, preferred_element_type=F32)


def mm_nt(left, right):
    return lax.dot_general(left, right, NT, preferred_element_type=F32)


def mm_tn(left, right):
    return lax.dot_general(left, right, (((0,), (0,)), ((), ())), preferred_element_type=F32)


def centred(values):
    center = values - jnp.mean(values, axis=-1, keepdims=True)
    spread = jnp.mean(center * center, axis=-1, keepdims=True)
    scale = lax.rsqrt(spread + eps)
    return center * scale, scale


def norm_back(grad, unit, scale):
    return scale * (
        grad
        - jnp.mean(grad, axis=-1, keepdims=True)
        - unit * jnp.mean(grad * unit, axis=-1, keepdims=True)
    )


def key_mask(block, live_rows):
    rows = lax.broadcasted_iota(jnp.int32, block.shape, 0)
    return jnp.where(rows < live_rows, block, -1e30)


def attend_kernel(parts, heads, rows, info, *refs):
    xs = refs[:parts]
    w, gain, shift, bias = refs[parts : parts + 4]
    stored = refs[parts + 4 : parts + 9]
    outs = refs[parts + 9 : 2 * parts + 9]
    lse, nrm, q, k, v, kt, vt, ot, sems = refs[2 * parts + 9 :]
    me, live = info[0], info[1]
    span = heads * HD
    for j in range(parts):
        g = me ^ j
        at = pl.ds(pl.multiple_of(g * rows, rows), rows)
        unit, _ = centred(xs[j][...].astype(F32))
        normed = (unit * gain[...] + shift[...]).astype(BF16)
        nrm[j] = normed
        qkv = mm(normed, w[...]) + bias[...]
        for h in range(heads):
            cols = slice(h * HD, (h + 1) * HD)
            kk = qkv[:, span + h * HD : span + (h + 1) * HD]
            vv = qkv[:, 2 * span + h * HD : 2 * span + (h + 1) * HD]
            q[h, at, :] = (qkv[:, cols].astype(BF16).astype(F32) * 0.125).astype(BF16)
            k[h, at, :] = kk.astype(BF16)
            v[h, at, :] = vv.astype(BF16)
            kt[h, g] = kk.T.astype(BF16)
            vt[h, g] = vv.T.astype(BF16)
    copies = [
        pltpu.make_async_copy(source, target, sems.at[index])
        for index, (source, target) in enumerate(zip((nrm, q, k, v, kt), stored))
    ]
    for copy in copies:
        copy.start()

    def variant(count):
        def step(t, carry):
            h, j = t // parts, t % parts
            g = me ^ j

            @pl.when(g < count)
            def _():
                qb = q[h, pl.ds(pl.multiple_of(g * rows, rows), rows), :]
                scores = [
                    mm_nt(k[h, c * rows : (c + 1) * rows, :], qb) for c in range(count)
                ]
                scores[-1] = key_mask(scores[-1], live - (count - 1) * rows)
                top = functools.reduce(
                    jnp.maximum, [jnp.max(s, axis=0, keepdims=True) for s in scores]
                )
                total, mixed = 0.0, 0.0
                for c in range(count):
                    e = jnp.exp(scores[c] - top)
                    total = total + jnp.sum(e, axis=0, keepdims=True)
                    mixed = mixed + mm(vt[h, c], e.astype(BF16))
                ot[t] = mixed / total
                lse[t] = jnp.broadcast_to(top + jnp.log(total), (8, rows))

            @pl.when(g >= count)
            def _():
                ot[t] = jnp.zeros((HD, rows), F32)
                lse[t] = jnp.zeros((8, rows), F32)

            return carry

        lax.fori_loop(0, heads * parts, step, 0)

    blocks = (live + rows - 1) // rows
    for count in range(max(1, SHORTEST // rows), parts + 1):
        pl.when(blocks == count)(functools.partial(variant, count))
    for j in range(parts):
        stacked = jnp.concatenate([ot[h * parts + j] for h in range(heads)], axis=0)
        outs[j][...] = stacked.T.astype(BF16)
    for copy in copies:
        copy.wait()


def whole(*arrays):
    return [pl.BlockSpec(a.shape, lambda i, n=a.ndim: (0,) * n) for a in arrays]


def attend_forward(place, live, xs, w, gain, shift, bias):
    parts, (rows, width) = len(xs), xs[0].shape
    span = w.shape[1] // 3
    heads, full = span // HD, parts * rows
    shape = jax.ShapeDtypeStruct
    kept = [(parts, rows, width)] + [(heads, full, HD)] * 3 + [(heads, parts, HD, rows)]
    outs_like, lse_like = shape((rows, span), BF16), shape((heads * parts, 8, rows), F32)
    outs = pl.pallas_call(
        functools.partial(attend_kernel, parts, heads, rows),
        grid=(1,),
        in_specs=[pl.BlockSpec(memory_space=pltpu.SMEM)] + whole(*xs, w, gain, shift, bias),
        out_specs=[pl.BlockSpec(memory_space=pltpu.HBM)] * 5
        + whole(*[outs_like] * parts, lse_like),
        out_shape=[shape(dims, BF16) for dims in kept]
        + [outs_like] * parts
        + [lse_like],
        scratch_shapes=[pltpu.VMEM(dims, BF16) for dims in kept]
        + [
            pltpu.VMEM((heads, parts, HD, rows), BF16),
            pltpu.VMEM((heads * parts, HD, rows), F32),
            pltpu.SemaphoreType.DMA((5,)),
        ],
        cost_estimate=pl.CostEstimate(
            flops=2 * full * width * 3 * span + 4 * full * full * span,
            bytes_accessed=2 * (2 * full * width + width * 3 * span + 6 * full * span),
            transcendentals=heads * full * full,
        ),
        compiler_params=pltpu.CompilerParams(vmem_limit_bytes=60 << 20),
        name="attend_forward",
    )(jnp.stack([place, live]), *xs, w, gain, shift, bias)
    return outs[0], outs[1:5], outs[5 : 5 + parts], outs[5 + parts]


def attend_back_kernel(parts, heads, rows, info, *refs):
    xs, grads = refs[:parts], refs[parts : 2 * parts]
    w, q, k, v, kt, lse = refs[2 * parts : 2 * parts + 6]
    dqkv = refs[2 * parts + 6]
    dns = refs[2 * parts + 7 : 3 * parts + 7]
    sums, cols = refs[3 * parts + 7 : 3 * parts + 9]
    do, dk, dv, dqt = refs[3 * parts + 9 :]
    me, live = info[0], info[1]
    for j in range(parts):
        block = grads[j][...].astype(F32)
        for h in range(heads):
            do[h * parts + j] = block[:, h * HD : (h + 1) * HD].astype(BF16)
    dk[...] = jnp.zeros_like(dk)
    dv[...] = jnp.zeros_like(dv)

    def variant(count):
        def step(t, carry):
            h, j = t // parts, t % parts
            g = me ^ j

            @pl.when(g < count)
            def _():
                qb = q[h, pl.ds(pl.multiple_of(g * rows, rows), rows), :]
                dob = do[t]
                shift = lse[t][0:1, :]
                probs, dps, inner = [], [], 0.0
                for c in range(count):
                    span = slice(c * rows, (c + 1) * rows)
                    s = mm_nt(k[h, span, :], qb)
                    if c == count - 1:
                        s = key_mask(s, live - c * rows)
                    p = jnp.exp(s - shift)
                    dp = mm_nt(v[h, span, :], dob)
                    inner = inner + jnp.sum(p * dp, axis=0, keepdims=True)
                    dv[h, c] += mm(p.astype(BF16), dob)
                    probs.append(p)
                    dps.append(dp)
                dq = 0.0
                for c in range(count):
                    ds = (probs[c] * (dps[c] - inner)).astype(BF16)
                    dk[h, c] += mm(ds, qb)
                    dq = dq + mm(kt[h, c], ds)
                dqt[t] = dq * 0.125

            @pl.when(g >= count)
            def _():
                dqt[t] = jnp.zeros((HD, rows), F32)

            return carry

        lax.fori_loop(0, heads * parts, step, 0)

    blocks = (live + rows - 1) // rows
    for count in range(max(1, SHORTEST // rows), parts + 1):
        pl.when(blocks == count)(functools.partial(variant, count))
    shift_sum, gain_sum, col_sum = 0.0, 0.0, 0.0
    for j in range(parts):
        g = me ^ j
        dq = jnp.concatenate([dqt[h * parts + j] for h in range(heads)], axis=0).T
        pieces = [dq] + [dk[h, g] for h in range(heads)] + [dv[h, g] for h in range(heads)]
        block = jnp.concatenate(pieces, axis=1).astype(BF16)
        dqkv[j] = block
        col_sum = col_sum + jnp.sum(block.astype(F32), axis=0, keepdims=True)
        dn = mm_nt(block, w[...])
        unit, _ = centred(xs[j][...].astype(F32))
        shift_sum = shift_sum + jnp.sum(dn, axis=0, keepdims=True)
        gain_sum = gain_sum + jnp.sum(dn * unit, axis=0, keepdims=True)
        dns[j][...] = dn.astype(BF16)
    sums[0:1, :] = gain_sum
    sums[1:2, :] = shift_sum
    cols[0:1, :] = col_sum


def attend_backward(place, live, xs, grads, w, saved, lse):
    parts, (rows, width) = len(xs), xs[0].shape
    span = w.shape[1] // 3
    heads, full = span // HD, parts * rows
    shape = jax.ShapeDtypeStruct
    out_shape = [
        shape((parts, rows, 3 * span), BF16),
        *[shape((rows, width), BF16)] * parts,
        shape((2, width), F32),
        shape((1, 3 * span), F32),
    ]
    outs = pl.pallas_call(
        functools.partial(attend_back_kernel, parts, heads, rows),
        grid=(1,),
        in_specs=[pl.BlockSpec(memory_space=pltpu.SMEM)] + whole(*xs, *grads, w, *saved, lse),
        out_specs=whole(*out_shape),
        out_shape=out_shape,
        scratch_shapes=[
            pltpu.VMEM((heads * parts, rows, HD), BF16),
            pltpu.VMEM((heads, parts, rows, HD), F32),
            pltpu.VMEM((heads, parts, rows, HD), F32),
            pltpu.VMEM((heads * parts, HD, rows), F32),
        ],
        cost_estimate=pl.CostEstimate(
            flops=2 * full * width * 3 * span + 10 * full * full * span,
            bytes_accessed=2 * (3 * full * width + width * 3 * span + 9 * full * span),
            transcendentals=heads * full * full,
        ),
        compiler_params=pltpu.CompilerParams(vmem_limit_bytes=60 << 20),
        name="attend_backward",
    )(jnp.stack([place, live]), *xs, *grads, w, *saved, lse)
    return outs[0], outs[1 : 1 + parts], outs[1 + parts], outs[2 + parts]


def live_only(values, first, live):
    rows = first + lax.broadcasted_iota(jnp.int32, values.shape, 0)
    return jnp.where(rows < live, values, jnp.zeros_like(values))


def folded(values):
    return functools.reduce(
        jnp.add, [values[r : r + 8] for r in range(0, values.shape[0], 8)]
    )


def token_kernel(plan, seqs, parts, info, *refs):
    refs = list(refs)
    take = lambda count: [refs.pop(0) for _ in range(count)]
    sources = take(max(p[0] for p in plan) + 1)
    pieces = take(seqs * parts)
    x, cot, dvec, mgain, mshift, fvec = take(6)
    block_out, resid_grad, fnorm, branch, og, anorm = take(6)
    hid, pg = take(2)
    mds = take(seqs * parts)
    dsum, msum, fsum = take(3)
    wo, w1, w2, ob, munit, mscale, res, runit, rscale = take(9)
    pre, slope, act, hg, ngs, dacc, macc, facc, sems = take(9)
    step = pl.program_id(0)
    me, core = info[seqs], info[seqs + 1]
    live = info[step] - me * x.shape[0]
    rows, width = x.shape
    span, units = width // parts, pre.shape[1]
    band, wide = 64, 256
    quarters = units // width

    def place(quarter):
        turned = quarter + quarters // 2 * core
        return jnp.where(turned >= quarters, turned - quarters, turned)

    targets = {"out": wo, "fc1": w1, "fc2": w2}

    def copies(wanted):
        for index, (src, k, start, count, name, at, at_step, col, col_step) in enumerate(plan):
            if name not in wanted:
                continue
            source = sources[src] if k is None else sources[src].at[k]
            target = targets[name]
            turn = core if src == 0 else 1 - core
            if at_step:
                at = pl.multiple_of(at + at_step * turn, 16)
            if col_step:
                col = pl.multiple_of(col + col_step * turn, 128)
            target = target.at[pl.ds(at, count), pl.ds(col, source.shape[1])]
            yield pltpu.make_async_copy(source.at[pl.ds(start, count)], target, sems.at[index])

    def arrived(name):
        @pl.when(step == 0)
        def _():
            for copy in copies((name,)):
                copy.wait()

    @pl.when(step == 0)
    def _():
        for copy in copies(("out", "fc1", "fc2")):
            copy.start()
        dacc[...] = jnp.zeros_like(dacc)
        macc[...] = jnp.zeros_like(macc)
        facc[...] = jnp.zeros_like(facc)

    for i in range(seqs):

        @pl.when(step == i)
        def _(i=i):
            for j in range(parts):
                ob[j] = pieces[i * parts + j][...]

    def tiles(size):
        def decorate(body):
            def run(t, carry):
                body(pl.ds(pl.multiple_of(t * size, size), size), t * size)
                return carry

            lax.fori_loop(0, rows // size, run, 0)

        return decorate

    @tiles(32)
    def _(at, first):
        blocks = [ob[j, at, :].astype(F32) for j in range(parts)]
        mean = sum(jnp.sum(b, axis=1, keepdims=True) for b in blocks) / width
        blocks = [b - mean for b in blocks]
        var = sum(jnp.sum(b * b, axis=1, keepdims=True) for b in blocks) / width
        scale = lax.rsqrt(var + eps)
        mscale[at, :] = jnp.broadcast_to(scale, (32, 128))
        for j in range(parts):
            g = me ^ j
            unit = blocks[j] * scale
            munit[j, at, :] = unit
            anorm[g, at, :] = (unit * mgain[g] + mshift[g]).astype(BF16)

    arrived("out")
    mixed = sum(mm(anorm[g], wo[g * span : (g + 1) * span, :]) for g in range(parts))
    res[...] = x[...].astype(F32) + mixed + dvec[2:3, :]

    @tiles(32)
    def _(at, first):
        unit, scale = centred(res[at, :])
        runit[at, :] = unit
        rscale[at, :] = jnp.broadcast_to(scale, (32, 128))
        fnorm[at, :] = (unit * dvec[0:1, :] + dvec[1:2, :]).astype(BF16)

    kept = live_only(cot[...].astype(F32), 0, live)
    og[...] = kept.astype(BF16)
    dacc[24:32, :] += folded(kept)
    chunks = [slice(c, c + wide) for c in range(0, units, wide)]
    bands = [slice(r, r + band) for r in range(0, rows, band)]

    def lanes(chunk):
        return [slice(c, c + 128) for c in range(chunk.start, chunk.stop, 128)]

    def row_mean(parts_of):
        return [jnp.sum(v, axis=1, keepdims=True) / units for v in parts_of]

    arrived("fc1")
    arrived("fc2")
    total = [jnp.zeros((band, 128), F32) for _ in bands]
    pre[:, chunks[0]] = mm(fnorm[...], w1[:, chunks[0]])
    for index, chunk in enumerate(chunks):
        if index + 1 < len(chunks):
            after_it = chunks[index + 1]
            pre[:, after_it] = mm(fnorm[...], w1[:, after_it])
        for c in lanes(chunk):
            for b, r in enumerate(bands):
                v = pre[r, c] + fvec[1:2, c]
                below = 0.5 * (1.0 + lax.erf(v * 0.7071067811865476))
                a = v * below
                slope[r, c] = below + v * (jnp.exp(-0.5 * v * v) * 0.3989422804014327)
                act[r, c] = a
                total[b] = total[b] + a
    mean = row_mean(total)
    total = [jnp.zeros((band, 128), F32) for _ in bands]
    for chunk in chunks:
        hg[:, chunk] = mm_nt(og[...], w2[chunk, :])
        for c in lanes(chunk):
            for b, r in enumerate(bands):
                d = act[r, c] - mean[b]
                total[b] = total[b] + d * d
    scale = [lax.rsqrt(v + eps) for v in row_mean(total)]
    one = [jnp.zeros((band, 128), F32) for _ in bands]
    two = [jnp.zeros((band, 128), F32) for _ in bands]
    out = res[...] + dvec[3:4, :]
    for chunk in chunks:
        for c in lanes(chunk):
            gain = fvec[0:1, c]
            gain_sum, shift_sum = 0.0, 0.0
            for b, r in enumerate(bands):
                unit = (act[r, c] - mean[b]) * scale[b]
                act[r, c] = unit
                hid[r, c] = (unit * gain + fvec[2:3, c]).astype(BF16)
                grad = hg[r, c]
                gain_sum = gain_sum + folded(grad * unit)
                shift_sum = shift_sum + folded(grad)
                grad = grad * gain
                hg[r, c] = grad
                one[b] = one[b] + grad
                two[b] = two[b] + grad * unit
            facc[0:8, c] += gain_sum
            facc[16:24, c] += shift_sum
        if chunk.stop % width == 0:
            ready = slice(chunk.stop - width, chunk.stop)
            out = out + mm(hid[:, ready], w2[ready, :])
    block_out[...] = live_only(out, 0, live).astype(BF16)
    one, two = row_mean(one), row_mean(two)
    total = 0.0
    for chunk in chunks:
        quarter, base = chunk.start // width, chunk.start // width * width
        for c in lanes(chunk):
            low_sum = 0.0
            for b, r in enumerate(bands):
                grad = scale[b] * (hg[r, c] - one[b] - act[r, c] * two[b]) * slope[r, c]
                low = grad.astype(BF16)
                pg[place(quarter), r, c.start - base : c.stop - base] = low
                low_sum = low_sum + folded(low.astype(F32))
            facc[8:16, c] += low_sum
        if chunk.stop % width == 0:
            total = total + mm_nt(pg[place(quarter)], w1[:, base : base + width])
    fg = res
    fg[...] = total

    @tiles(32)
    def _(at, first):
        grad, unit = fg[at, :], runit[at, :]
        dacc[0:8, :] += folded(grad * unit)
        dacc[8:16, :] += folded(grad)
        total = og[at, :].astype(F32) + norm_back(grad * dvec[0:1, :], unit, rscale[at, 0:1])
        resid_grad[at, :] = total
        branch[at, :] = total.astype(BF16)
        dacc[16:24, :] += folded(total)

    for g in range(parts):
        ngs[g] = mm_nt(branch[...], wo[g * span : (g + 1) * span, :])

    @tiles(32)
    def _(at, first):
        one, two, scaled = 0.0, 0.0, []
        for j in range(parts):
            g = me ^ j
            grad, unit = ngs[g, at, :], munit[j, at, :]
            macc[g, 0:8, :] += folded(grad * unit)
            macc[g, 8:16, :] += folded(grad)
            m = grad * mgain[g]
            one = one + jnp.sum(m, axis=1, keepdims=True)
            two = two + jnp.sum(m * unit, axis=1, keepdims=True)
            scaled.append(m)
        one, two, scale = one / width, two / width, mscale[at, 0:1]
        for j in range(parts):
            value = scale * (scaled[j] - one - munit[j, at, :] * two)
            ob[j, at, :] = value.astype(BF16)

    for i in range(seqs):

        @pl.when(step == i)
        def _(i=i):
            for j in range(parts):
                mds[i * parts + j][...] = ob[j]

    @pl.when(step == seqs - 1)
    def _():
        for r in range(4):
            dsum[r : r + 1, :] = jnp.sum(dacc[8 * r : 8 * r + 8, :], axis=0, keepdims=True)
        for r in range(3):
            fsum[r : r + 1, :] = jnp.sum(facc[8 * r : 8 * r + 8, :], axis=0, keepdims=True)
        for g in range(parts):
            for r in range(2):
                part = macc[g, 8 * r : 8 * r + 8, :]
                msum[g, r : r + 1, :] = jnp.sum(part, axis=0, keepdims=True)


def token_stage(info, plan, sources, pieces, x, cot, dvec, mgain, mshift, fvec):
    seqs, rows, width = x.shape
    parts, units = len(pieces[0]), fvec.shape[1]
    span = width // parts
    shape = jax.ShapeDtypeStruct
    full = lambda *dims: pl.BlockSpec(dims, lambda i: (0,) * len(dims))
    by_seq = pl.BlockSpec((None, rows, width), lambda i: (i, 0, 0))
    by_rows = lambda cols: pl.BlockSpec((rows, cols), lambda i: (i, 0))
    n = seqs * rows
    outs = pl.pallas_call(
        functools.partial(token_kernel, plan, seqs, parts),
        grid=(seqs,),
        in_specs=[pl.BlockSpec(memory_space=pltpu.SMEM)]
        + [pl.BlockSpec(memory_space=pl.ANY)] * len(sources)
        + [full(rows, span)] * (seqs * parts)
        + [
            by_seq,
            by_seq,
            full(*dvec.shape),
            full(*mgain.shape),
            full(*mshift.shape),
            full(*fvec.shape),
        ],
        out_specs=[by_seq, by_seq]
        + [by_rows(width)] * 3
        + [pl.BlockSpec((parts, rows, span), lambda i: (0, i, 0))]
        + [by_rows(units)]
        + [pl.BlockSpec((units // width, rows, width), lambda i: (0, i, 0))]
        + [full(rows, span)] * (seqs * parts)
        + [full(4, width), full(parts, 2, span), full(3, units)],
        out_shape=[shape((seqs, rows, width), BF16), shape((seqs, rows, width), F32)]
        + [shape((n, width), BF16)] * 3
        + [shape((parts, n, span), BF16)]
        + [shape((n, units), BF16), shape((units // width, n, width), BF16)]
        + [shape((rows, span), BF16)] * (seqs * parts)
        + [shape((4, width), F32), shape((parts, 2, span), F32), shape((3, units), F32)],
        scratch_shapes=[
            pltpu.VMEM((width, width), BF16),
            pltpu.VMEM((width, units), BF16),
            pltpu.VMEM((units, width), BF16),
            pltpu.VMEM((parts, rows, span), BF16),
            pltpu.VMEM((parts, rows, span), F32),
            pltpu.VMEM((rows, 128), F32),
            pltpu.VMEM((rows, width), F32),
            pltpu.VMEM((rows, width), F32),
            pltpu.VMEM((rows, 128), F32),
        ]
        + [pltpu.VMEM((rows, units), F32)] * 4
        + [
            pltpu.VMEM((parts, rows, span), F32),
            pltpu.VMEM((32, width), F32),
            pltpu.VMEM((parts, 16, span), F32),
            pltpu.VMEM((24, units), F32),
            pltpu.SemaphoreType.DMA((len(plan),)),
        ],
        cost_estimate=pl.CostEstimate(
            flops=2 * n * width * (4 * units + 2 * width),
            bytes_accessed=2 * width * (2 * units + width) + 2 * n * (4 * units + 12 * width),
            transcendentals=2 * n * units,
        ),
        compiler_params=pltpu.CompilerParams(vmem_limit_bytes=60 << 20),
        name="token_stage",
    )(info, *sources, *[p for group in pieces for p in group], x, cot, dvec, mgain, mshift, fvec)
    outs = list(outs)
    mds = outs[8 : 8 + seqs * parts]
    mds = [mds[i * parts : (i + 1) * parts] for i in range(seqs)]
    return outs[:6], outs[6], outs[7], mds, outs[8 + seqs * parts :]


def swap(values, axis, mask):
    count = lax.axis_size(axis)
    return lax.ppermute(values, axis, [(i, i ^ mask) for i in range(count)])


def pick(values, index, axis):
    return lax.dynamic_index_in_dim(values, index, axis, keepdims=False)


def after(values, others):
    return lax.optimization_barrier((values, others))[0]


def spread_blocks(block, axis):
    count, me = lax.axis_size(axis), lax.axis_index(axis)
    held = {0: block}
    bit = count // 2
    while bit:
        held |= {mask | bit: swap(part, axis, bit) for mask, part in held.items()}
        bit //= 2
    whole = jnp.zeros((count,) + block.shape, block.dtype)
    for mask, part in held.items():
        whole = lax.dynamic_update_index_in_dim(whole, part, me ^ mask, 0)
    return whole


def sum_blocks(blocks, small, axis):
    count, mine = lax.axis_size(axis), lax.axis_index(axis) % 2
    sums = []
    for values, kind in ((blocks, BF16), (small, F32)):
        pairs = values.reshape((count // 2, 2) + values.shape[1:])
        sent = swap(pick(pairs, 1 - mine, 1).astype(kind), axis, 1)
        sums.append((pick(pairs, mine, 1) + sent.astype(F32)).astype(BF16))
    sums[1] = jnp.pad(sums[1], ((0, 0), (0, 0), (0, blocks.shape[2] - small.shape[2])))
    groups = [list(range(g, count, 2)) for g in range(2)]
    blocks = lax.all_to_all(
        jnp.concatenate(sums, axis=1),
        axis,
        split_axis=0,
        concat_axis=0,
        axis_index_groups=groups,
        tiled=True,
    )
    return jnp.sum(blocks.astype(F32), axis=0)


def shards(
    activations,
    cotangent,
    lengths,
    w_qkv,
    w_out,
    w_fc1,
    w_fc2,
    d_gains,
    d_biases,
    ff_gain,
    ff_biases,
):
    seqs, rows, width = activations.shape
    parts, owners = lax.axis_size("seq"), lax.axis_size("fsdp")
    s = lax.axis_index("seq")
    core = s % 2
    span = width // parts
    own_rows = w_qkv.shape[0]
    own_ff = w_fc2.shape[0]
    half_ff, half_rows = own_ff // 2, own_rows // 2
    ff_half = half_ff * owners
    quarter = own_ff // own_rows

    fc1_half = lax.dynamic_slice(w_fc1, (0, core * ff_half), (own_rows, ff_half))
    columns = range(0, ff_half, width)
    rest = jnp.concatenate(
        [pick(w_out.reshape(2, half_rows, width), core, 0)]
        + [fc1_half[:, c : c + width] for c in columns]
        + [pick(w_fc2.reshape(2, half_ff, width), core, 0)],
        axis=0,
    )
    rest_rows = rest.shape[0]
    w_qkv = after(w_qkv, rest)
    rest = lax.all_gather(rest, "fsdp", axis=0, tiled=False)

    own_w = pick(w_qkv.reshape(own_rows, 3, parts, span), s, 2).reshape(own_rows, 3 * span)
    ff_small = jnp.concatenate([ff_gain[:, None], ff_biases], axis=1).T.reshape(
        3 * quarter, own_rows
    )
    small = jnp.concatenate([d_gains.T, d_biases.T, ff_small], axis=0)
    kinds = small.shape[0]
    small_rows = 32
    small = jnp.pad(small, ((0, small_rows - kinds), (0, 3 * span - own_rows)))
    block = jnp.concatenate([own_w, small], axis=0)
    first = spread_blocks(block, "fsdp")
    my_qkv = first[:, :own_rows].reshape(width, 3 * span)
    small = first[:, own_rows : own_rows + kinds, :own_rows].astype(F32)
    d_small = small[:, :10].transpose(1, 0, 2).reshape(10, width)
    gains, biases = d_small[:3], d_small[3:]
    ff_small = small[:, 10:].reshape(owners, 3, own_ff).transpose(1, 0, 2).reshape(3, 2 * ff_half)

    qkv_bias = pick(
        jnp.stack([biases[1], jnp.zeros_like(biases[1]), biases[2]]).reshape(3, parts, span), s, 1
    ).reshape(1, 3 * span)
    x_parts, mixed_parts, kept = [], [], []
    for i in range(seqs):
        mine = activations[i]
        across = swap(mine, "seq", 2)
        x_parts.append([mine, swap(mine, "seq", 1), across, swap(across, "seq", 1)])
    for i in range(seqs):
        if i > 0:
            x_parts[i] = after(x_parts[i], [kept[i - 1][2], mixed_parts[:-1]])
        normed, saved, outs, lse = attend_forward(
            s, lengths[i], x_parts[i], my_qkv, gains[0:1], biases[0:1], qkv_bias
        )
        kept.append((normed, saved, lse))
        mixed_parts.append([outs[0]] + [swap(outs[j], "seq", j) for j in range(1, parts)])
    rest = after(rest, [lse for _, _, lse in kept])
    rest_other = swap(rest, "seq", 1)

    plan, sources = [], [rest, rest_other]
    if half_rows % 16 == 0 and half_ff % 16 == 0:
        for src in range(2):
            for k in range(owners):
                plan.append((src, k, 0, half_rows, "out", k * own_rows, half_rows, 0, 0))
                for at, c in enumerate(columns):
                    start = half_rows + at * own_rows
                    plan.append((src, k, start, own_rows, "fc1", k * own_rows, 0, c, ff_half))
                start = rest_rows - half_ff
                plan.append((src, k, start, half_ff, "fc2", k * own_ff, half_ff, 0, 0))
    else:
        pair = [jnp.where(core == 0, rest, rest_other), jnp.where(core == 0, rest_other, rest)]
        blocks = [
            buf[:, half_rows + at * own_rows : half_rows + (at + 1) * own_rows].reshape(width, width)
            for buf in pair
            for at in range(len(columns))
        ]
        sources = [
            jnp.concatenate([buf[:, :half_rows] for buf in pair], axis=1).reshape(width, width),
            jnp.concatenate(blocks, axis=1),
            jnp.concatenate([buf[:, rest_rows - half_ff :] for buf in pair], axis=1).reshape(
                2 * ff_half, width
            ),
        ]
        names = ("out", "fc1", "fc2")
        plan = [(i, None, 0, sources[i].shape[0], names[i], 0, 0, 0, 0) for i in range(3)]
    info = jnp.concatenate([lengths, jnp.stack([s, core]).astype(jnp.int32)])
    dvec = jnp.stack([gains[2], biases[5], biases[4], biases[6]])
    tokens = token_stage(
        info,
        plan,
        sources,
        mixed_parts,
        activations,
        cotangent,
        dvec,
        gains[1].reshape(parts, 1, span),
        biases[3].reshape(parts, 1, span),
        ff_small,
    )
    (block_out, resid_grad, fnorm, branch, og, anorm), hid, pg, mixed_grads, sums = tokens
    dsum, msum, fsum = sums

    grad_out = jnp.einsum("gnk,nd->gkd", anorm, branch, preferred_element_type=F32)
    grad_out = grad_out.reshape(owners, 2, half_rows, width)
    grad_fc2 = mm_tn(hid, og).reshape(owners, 2, half_ff, width)
    mixed_grads = [[g[0]] + [swap(g[j], "seq", j) for j in range(1, parts)] for g in mixed_grads]
    grads = []
    for src in (1, 0):
        turn = core if src == 0 else 1 - core
        pieces = [pick(grad_out, turn, 1)]
        pieces += [
            mm_tn(fnorm, pg[len(columns) * src + at]).reshape(owners, own_rows, width)
            for at in range(len(columns))
        ]
        pieces.append(pick(grad_fc2, turn, 1))
        grads.append(jnp.concatenate([p.astype(BF16) for p in pieces], axis=1))
    other_grads = swap(grads[0], "seq", 1)
    rest_sum = (grads[1].astype(F32) + other_grads.astype(F32)).astype(BF16)
    rest_sum = rest_sum.reshape(owners * rest_rows, width)
    mixed_grads[0], rest_sum = lax.optimization_barrier((mixed_grads[0], rest_sum))
    rest_sum = lax.psum_scatter(rest_sum, "fsdp", scatter_dimension=0, tiled=True)

    grad_own, summed, head_sums, unit_sums, near = 0.0, [], 0.0, 0.0, []
    for i in range(seqs):
        pieces = mixed_grads[i]
        if i > 0:
            pieces = after(pieces, [sums, near[:-1]])
        normed, saved, lse = kept[i]
        dqkv, dns, sums, cols = attend_backward(
            s, lengths[i], x_parts[i], pieces, my_qkv, saved, lse
        )
        grad_own = grad_own + mm_tn(
            normed.reshape(parts * rows, width), dqkv.reshape(parts * rows, 3 * span)
        )
        unit_sums, head_sums = unit_sums + sums, head_sums + cols
        near.append([swap(dns[j], "seq", 1) for j in (1, 3)])
        far = (dns[2].astype(F32) + near[i][1].astype(F32)).astype(BF16)
        far = swap(far, "seq", 2).astype(F32)
        summed.append(dns[0].astype(F32) + near[i][0].astype(F32) + far)
    first_grad = jnp.stack(summed)
    first_unit, first_scale = centred(activations.astype(F32))
    input_grad = resid_grad + norm_back(first_grad * gains[0], first_unit, first_scale)

    def head_columns(values):
        blank = jnp.zeros((parts, span), F32)
        return lax.dynamic_update_slice(blank, values[None], (s, 0)).reshape(width)

    small_grads = jnp.stack(
        [
            unit_sums[0],
            msum[:, 0].reshape(width),
            dsum[0],
            unit_sums[1],
            head_columns(head_sums[0, :span]),
            head_columns(head_sums[0, 2 * span :]),
            msum[:, 1].reshape(width),
            dsum[2],
            dsum[1],
            dsum[3],
        ]
    )
    feed_grads = fsum.reshape(3, owners, quarter, own_rows)
    small_blocks = jnp.concatenate(
        [
            small_grads.reshape(10, owners, own_rows).transpose(1, 0, 2),
            feed_grads.transpose(1, 0, 2, 3).reshape(owners, 3 * quarter, own_rows),
        ],
        axis=1,
    )
    small_blocks = jnp.pad(small_blocks, ((0, 0), (0, small_rows - kinds), (0, 0)))
    own_sum = sum_blocks(
        grad_own.reshape(owners, own_rows, 3 * span), small_blocks, "fsdp"
    )
    small_sum = own_sum[own_rows:, :own_rows]
    own_sum = own_sum[:own_rows].astype(BF16)
    across = swap(rest_sum, "seq", 2)
    small_sum = small_sum + swap(small_sum, "seq", 1)
    small_sum = small_sum + swap(small_sum, "seq", 2)
    feed_sum = small_sum[10:kinds].reshape(3, own_ff)
    small_outs = (small_sum[:3].T, small_sum[3:10].T, feed_sum[0], feed_sum[1:].T)
    group = jnp.stack([own_sum, swap(own_sum, "seq", 2)])
    group = jnp.stack([group, swap(group, "seq", 1)], axis=1).reshape((parts,) + own_sum.shape)
    w_qkv_grad = jnp.concatenate(
        [
            pick(group, s ^ g, 0)[:, p * span : (p + 1) * span]
            for p in range(3)
            for g in range(parts)
        ],
        axis=1,
    ).astype(F32)

    across = after(across, [w_qkv_grad, small_outs, input_grad])
    rest_sum = rest_sum.astype(F32) + across.astype(F32)
    other_sum = swap(rest_sum, "seq", 1)
    pair = [
        jnp.where(core == 0, rest_sum, other_sum),
        jnp.where(core == 0, other_sum, rest_sum),
    ]
    w_out_grad = jnp.concatenate([p[:half_rows] for p in pair], axis=0)
    w_fc1_grad = jnp.concatenate(
        [
            p[half_rows + at * own_rows : half_rows + (at + 1) * own_rows]
            for p in pair
            for at in range(len(columns))
        ],
        axis=1,
    )
    w_fc2_grad = jnp.concatenate([p[rest_rows - half_ff :] for p in pair], axis=0)
    return (
        block_out,
        input_grad,
        w_qkv_grad,
        w_out_grad,
        w_fc1_grad,
        w_fc2_grad,
        *small_outs,
    )


def solution(mesh):
    return jax.shard_map(
        shards,
        mesh=mesh,
        in_specs=(
            P("fsdp", "seq", None),
            P("fsdp", "seq", None),
            P("fsdp"),
            P("fsdp", None),
            P("fsdp", None),
            P("fsdp", None),
            P("fsdp", None),
            P("fsdp", None),
            P("fsdp", None),
            P("fsdp"),
            P("fsdp", None),
        ),
        out_specs=(
            P("fsdp", "seq", None),
            P("fsdp", "seq", None),
            P("fsdp", None),
            P("fsdp", None),
            P("fsdp", None),
            P("fsdp", None),
            P("fsdp", None),
            P("fsdp", None),
            P("fsdp"),
            P("fsdp", None),
        ),
        check_vma=False,
    )
```
